32 devices in a mesh: tok: 8 (over y, x, core), mdl: 4 (over z).
Axes of the slice: x: 2, y: 2, z: 4, core: 2. Of those that a mesh axis runs over, the one named last changes fastest.
Arguments:
- hidden_states: bfloat16 [4096, 3072], P('tok', 'mdl'), may hold values from -36 to 36
- lengths: int32 [2], replicated, may hold values from 1 to 2277, 3644 in all
- positions: int32 [3, 4096], P(None, 'tok'), may hold values from 0 to 44, as said below
- modulation: float32 [6, 3072], replicated, may hold values from -3 to 3
- query_weight: bfloat16 [3072, 3072], P('tok', 'mdl'), may hold values from -1.1 to 1.1
- key_weight: bfloat16 [3072, 3072], P('tok', 'mdl'), may hold values from -1.1 to 1.1
- value_weight: bfloat16 [3072, 3072], P('tok', 'mdl'), may hold values from -0.109375 to 0.109375
- out_weight: bfloat16 [3072, 3072], P('tok', 'mdl'), may hold values from -0.109375 to 0.109375
- query_gain: float32 [64], replicated, may hold values from 0.1 to 1.9
- key_gain: float32 [64], replicated, may hold values from 0.1 to 1.9
Outputs:
- updated: bfloat16 [4096, 3072], P('tok', 'mdl')
The draws below stay inside these ranges and needn't reach their ends.
Inputs may be any that keep to these rules, and one draw needn't show every extreme that they name: lengths[0] + lengths[1] = 3644, and neither of them exceeds 2277. `positions`: frame below 13, row below 30, column below 45.
All inputs are finite; a program needn't handle non-finite values.
Results may differ from the reference program's by a relative error of at most 0.0045.
Values may be sent and summed in bfloat16 or wider, within the bound.
A program may use at most 128 MiB of HBM per device.

```python
import math
import jax
import jax.numpy as jnp
import numpy as np
from jax import lax

D = 3072
HEADS = 48
HEAD_DIM = 64
TEXT = 226
REQS = 2
TOKENS = 4096
VIDEO = 3644
MOST = 2277


def draw_hidden_states(key, part):
    base_key, row_key, col_key = jax.random.split(jax.random.fold_in(key, 101), 3)
    base = jax.random.truncated_normal(base_key, -4.0, 4.0, (TOKENS, D), jnp.float32)
    row_scale = jnp.exp(jax.random.uniform(row_key, (TOKENS, 1), jnp.float32, math.log(0.3), math.log(3.0)))
    col_scale = jnp.exp(jax.random.uniform(col_key, (1, D), jnp.float32, math.log(0.3), math.log(3.0)))
    return (base * row_scale * col_scale).astype(jnp.bfloat16)


def projection_draw(key, salt):
    base_key, col_key = jax.random.split(jax.random.fold_in(key, salt), 2)
    base = jax.random.truncated_normal(base_key, -4.0, 4.0, (D, D), jnp.float32)
    col_scale = jnp.exp(jax.random.uniform(col_key, (1, D), jnp.float32, math.log(0.3), math.log(3.0)))
    return base * col_scale * D ** (-0.5)


def draw_query_weight(key, part):
    return projection_draw(key, 211).astype(jnp.bfloat16)


def draw_key_weight(key, part):
    return projection_draw(key, 307).astype(jnp.bfloat16)


def draw_positions(key, part):
    limits = jnp.array([[13], [30], [45]], dtype=jnp.int32)
    return jax.random.randint(jax.random.fold_in(key, 7), (3, TOKENS), 0, limits, dtype=jnp.int32)


def levels(key, shape, cuts, smallest, largest):
    factor_of, own = 1.0, jax.random.fold_in(key, 6)
    for position, shards_of in cuts:
        steps = jnp.exp(jax.random.uniform(jax.random.fold_in(own, position), (shards_of,), jnp.float32, smallest / len(cuts), largest / len(cuts)))
        factor_of = factor_of * jnp.repeat(steps, shape[position] // shards_of).reshape([-1 if axis == position else 1 for axis in range(len(shape))])
    return factor_of


def profile(count, total, most, slope):
    weights = [(1 << 20) // math.isqrt(grade ** slope) + 1 for grade in range(2, count + 1)]
    rest, holding = total - most - (count - 1), [1] * (count - 1)
    while rest > 0:
        movable = [i for i in range(count - 1) if holding[i] < most]
        mass, budget = sum([weights[i] for i in movable]), rest
        for i in movable:
            more = min(most - holding[i], max(1, budget * weights[i] // mass), rest)
            holding[i] = holding[i] + more
            rest = rest - more
    return np.array([most] + holding)


def ragged_sizes(rng, amount, total, most, slope):
    if amount == 2:
        one = jax.random.randint(rng, (), max(1, total - most), min(most, total - 1) + 1)
        return jnp.stack([one, total - one])
    sizes = jnp.asarray(profile(amount, total, most, slope), jnp.int32)
    pairs = (amount - 1) // 2
    source_of, sink = sizes[1:1 + 2 * pairs:2], sizes[2:2 + 2 * pairs:2]
    room = jnp.minimum(source_of - 1, most - sink)
    moved = jax.random.randint(jax.random.fold_in(rng, 1), (pairs,), 0, 1 << 20) % (room + 1)
    sizes = sizes.at[1:1 + 2 * pairs:2].set(source_of - moved).at[2:2 + 2 * pairs:2].set(sink + moved)
    return sizes[jax.random.permutation(jax.random.fold_in(rng, 2), amount)]


def bell_draw(rng, dims, scale, limit, shards=(), held_as=jnp.bfloat16):
    drawn = scale * jax.random.normal(rng, dims, jnp.float32)
    if shards:
        drawn = drawn * levels(rng, dims, shards, -0.22, 0.18)
    return jnp.clip(drawn, -limit, limit).astype(held_as)


def setup_inputs(seed: int = 0) -> dict:
    arg_keys = jax.random.split(jax.random.key(seed), 11)
    hidden_states = draw_hidden_states(jax.random.fold_in(arg_keys[10], 71), 0)
    lengths = ragged_sizes(arg_keys[1], REQS, VIDEO, MOST, 0).astype(jnp.int32)
    positions = draw_positions(jax.random.fold_in(arg_keys[10], 71), 0)
    modulation = bell_draw(arg_keys[3], (6, D), 0.5, 3.0, (), jnp.float32)
    query_weight = draw_query_weight(jax.random.fold_in(arg_keys[10], 71), 0)
    key_weight = draw_key_weight(jax.random.fold_in(arg_keys[10], 71), 0)
    value_weight = bell_draw(arg_keys[6], (D, D), D ** -0.5, 0.109375, ((0, 8), (1, 4)))
    out_weight = bell_draw(arg_keys[7], (D, D), D ** -0.5, 0.109375, ((0, 8), (1, 4)))
    query_gain = jnp.clip(1.0 + 0.18 * jax.random.normal(arg_keys[8], (HEAD_DIM,), jnp.float32), 0.1, 1.9)
    key_gain = jnp.clip(1.0 + 0.18 * jax.random.normal(arg_keys[9], (HEAD_DIM,), jnp.float32), 0.1, 1.9)
    return {"hidden_states": hidden_states, "lengths": lengths, "positions": positions, "modulation": modulation, "query_weight": query_weight, "key_weight": key_weight, "value_weight": value_weight, "out_weight": out_weight, "query_gain": query_gain, "key_gain": key_gain}


def token_labels(row_index, lengths):
    bound = TEXT + lengths[0]
    request = (row_index >= bound).astype(jnp.int32)
    place = row_index - request * bound
    return (request, place < TEXT, bound)

def modulate(rows_bf, modulation, is_text):
    values = rows_bf.astype(jnp.float32)
    center = values - lax.optimization_barrier(jnp.mean(values, axis=1, keepdims=True))
    spread = lax.optimization_barrier(jnp.mean(center * center, axis=1, keepdims=True))
    normal = center * lax.rsqrt(spread + 1e-05)
    textual = is_text[:, None]
    shift = jnp.where(textual, modulation[3][None, :], modulation[0][None, :])
    scale = jnp.where(textual, modulation[4][None, :], modulation[1][None, :])
    return (normal * (1.0 + scale) + shift).astype(jnp.bfloat16)

def pair_angles(positions, pairs):
    index = jnp.arange(pairs, dtype=jnp.int32)
    first = pairs // 4
    second = (pairs - first) // 2
    third = pairs - first - second
    component = jnp.where(index < first, 0, jnp.where(index < first + second, 1, 2))
    local = index - jnp.where(component == 0, 0, jnp.where(component == 1, first, first + second))
    count = jnp.where(component == 0, first, jnp.where(component == 1, second, third))
    rates = jnp.power(jnp.float32(10000.0), -local.astype(jnp.float32) / count.astype(jnp.float32))
    places = positions.astype(jnp.float32)
    chosen = jnp.where(component[:, None] == 0, places[0][None, :], jnp.where(component[:, None] == 1, places[1][None, :], places[2][None, :]))
    return jnp.transpose(chosen * rates[:, None])

def head_norm(projected, gain, angles, is_text):
    width = gain.shape[0]
    shaped = projected.reshape(projected.shape[0], -1, width)
    center = shaped - lax.optimization_barrier(jnp.mean(shaped, axis=2, keepdims=True))
    spread = lax.optimization_barrier(jnp.mean(center * center, axis=2, keepdims=True))
    normal = center * lax.rsqrt(spread + 1e-06) * gain
    half = width // 2
    cosine = jnp.cos(angles)[:, None, :]
    sine = jnp.sin(angles)[:, None, :]
    lower = normal[:, :, :half]
    upper = normal[:, :, half:]
    turned = jnp.concatenate([lower * cosine - upper * sine, lower * sine + upper * cosine], axis=2)
    return jnp.where(is_text[:, None, None], normal, turned).astype(jnp.bfloat16)

def reference(hidden_states, lengths, positions, modulation, query_weight, key_weight, value_weight, out_weight, query_gain, key_gain):
    row_index = jnp.arange(TOKENS, dtype=jnp.int32)
    request, is_text, bound = token_labels(row_index, lengths)
    normed = modulate(hidden_states, modulation, is_text)
    angles = pair_angles(positions, HEAD_DIM // 2)
    query = head_norm(jnp.dot(normed, query_weight, preferred_element_type=jnp.float32), query_gain, angles, is_text)
    keys = head_norm(jnp.dot(normed, key_weight, preferred_element_type=jnp.float32), key_gain, angles, is_text)
    values = jnp.dot(normed, value_weight, preferred_element_type=jnp.float32).astype(jnp.bfloat16)
    values = values.reshape(TOKENS, HEADS, HEAD_DIM)
    same = request[:, None] == request[None, :]
    factor = HEAD_DIM ** (-0.5)

    def one_head(operands):
        head_query, head_keys, head_values = operands
        score = jnp.dot(head_query, jnp.transpose(head_keys), preferred_element_type=jnp.float32) * factor
        expo = jnp.where(same, jnp.exp(score), jnp.float32(0.0))
        total = lax.optimization_barrier(jnp.sum(expo, axis=1, keepdims=True))
        weighted = jnp.dot(expo.astype(jnp.bfloat16), head_values, preferred_element_type=jnp.float32)
        return weighted / total
    heads_out = lax.map(one_head, (jnp.transpose(query, (1, 0, 2)), jnp.transpose(keys, (1, 0, 2)), jnp.transpose(values, (1, 0, 2))))
    attended = jnp.transpose(heads_out, (1, 0, 2)).reshape(TOKENS, D).astype(jnp.bfloat16)
    projected = jnp.dot(attended, out_weight, preferred_element_type=jnp.float32)
    gate = jnp.where(is_text[:, None], modulation[5][None, :], modulation[2][None, :])
    return (hidden_states.astype(jnp.float32) + gate * projected).astype(jnp.bfloat16)
```

```python
import functools
import jax
import jax.numpy as jnp
from jax import lax
from jax.experimental import pallas as pl
from jax.experimental.pallas import tpu as pltpu
from jax.sharding import PartitionSpec as P

TEXT = 226


def token_labels(row_index, lengths):
    bound = TEXT + lengths[0]
    request = (row_index >= bound).astype(jnp.int32)
    place = row_index - request * bound
    return (request, place < TEXT, bound)


def modulate(rows_bf, modulation, is_text):
    values = rows_bf.astype(jnp.float32)
    center = values - jnp.mean(values, axis=1, keepdims=True)
    spread = jnp.mean(center * center, axis=1, keepdims=True)
    normal = center * lax.rsqrt(spread + 1e-05)
    textual = is_text[:, None]
    shift = jnp.where(textual, modulation[3][None, :], modulation[0][None, :])
    scale = jnp.where(textual, modulation[4][None, :], modulation[1][None, :])
    return (normal * (1.0 + scale) + shift).astype(jnp.bfloat16)


def pair_angles(positions, pairs):
    index = jnp.arange(pairs, dtype=jnp.int32)
    first = pairs // 4
    second = (pairs - first) // 2
    third = pairs - first - second
    component = jnp.where(index < first, 0, jnp.where(index < first + second, 1, 2))
    local = index - jnp.where(component == 0, 0, jnp.where(component == 1, first, first + second))
    count = jnp.where(component == 0, first, jnp.where(component == 1, second, third))
    rates = jnp.power(jnp.float32(10000.0), -local.astype(jnp.float32) / count.astype(jnp.float32))
    places = positions.astype(jnp.float32)
    chosen = jnp.where(
        component[:, None] == 0,
        places[0][None, :],
        jnp.where(component[:, None] == 1, places[1][None, :], places[2][None, :]),
    )
    return jnp.transpose(chosen * rates[:, None])


def gather_kernel(n_tok, n_mdl, n_row, n_col, *refs):
    count = n_row + n_col
    ins, outs = refs[:count], refs[count : 2 * count]
    exchange(
        n_tok, n_mdl, ins[:n_row], ins[n_row:], outs[:n_row], outs[n_row:], refs[2 * count :]
    )


def exchange(
    n_tok, n_mdl, rows_in, cols_in, rows_out, cols_out, semaphores, prepare=None, between=None
):
    n_row, n_col = len(rows_in), len(cols_in)
    (
        local_sem,
        send1,
        recv1,
        send2,
        recv2,
        send3,
        recv3,
        to_right,
        from_left,
        to_left,
        from_right,
    ) = semaphores
    square = n_tok == 8
    chips = n_tok // 2
    tok, mdl = lax.axis_index("tok"), lax.axis_index("mdl")
    chip, core = tok // 2, tok % 2
    sibling = chip * 2 + 1 - core

    def chip_at(step):
        if square:
            return (chip, chip + 1 - 2 * (chip % 2), (chip + 2) % 4, 3 - chip)[step]
        return (chip + step) % chips

    def source_at(step):
        return chip_at(step) if square else chip_at(chips - step)

    barrier = pltpu.get_barrier_semaphore()
    greeted = 0
    if n_row:
        for step in (1, 2) if square else range(1, chips):
            pl.semaphore_signal(
                barrier, inc=1, device_id={"tok": chip_at(step) * 2 + core, "mdl": mdl}
            )
            greeted += 1
        pl.semaphore_signal(barrier, inc=1, device_id={"tok": sibling, "mdl": mdl})
        greeted += 1
    if n_col:
        for side in (1, n_mdl - 1):
            pl.semaphore_signal(
                barrier, inc=1, device_id={"tok": tok, "mdl": (mdl + side) % n_mdl}
            )
            greeted += 1
    pl.semaphore_wait(barrier, greeted)

    def row_block(number, owner):
        size = rows_in[number].shape[0]
        return rows_out[number].at[pl.ds(pl.multiple_of(owner * size, size), size), :]

    def col_block(number, owner):
        size = cols_in[number].shape[1]
        return cols_out[number].at[:, pl.ds(pl.multiple_of(owner * size, size), size)]

    def direct(number, step):
        target = chip_at(step) * 2 + core if step else sibling
        return pltpu.make_async_remote_copy(
            src_ref=rows_in[number],
            dst_ref=row_block(number, tok),
            send_sem=send1.at[number, step],
            recv_sem=recv1.at[number, step],
            device_id={"tok": target, "mdl": mdl},
        )

    def passed(number, step):
        block = row_block(number, source_at(step) * 2 + core)
        return pltpu.make_async_remote_copy(
            src_ref=block,
            dst_ref=block,
            send_sem=send2.at[number, step],
            recv_sem=recv2.at[number, step],
            device_id={"tok": sibling, "mdl": mdl},
        )

    def relayed(number, step):
        half = rows_in[number].shape[0] // 2
        first = (source_at(step) * 2 + core) * 2 * half + (step - 1) * half
        block = rows_out[number].at[pl.ds(pl.multiple_of(first, half), half), :]
        return pltpu.make_async_remote_copy(
            src_ref=block,
            dst_ref=block,
            send_sem=send3.at[number, step],
            recv_sem=recv3.at[number, step],
            device_id={"tok": chip_at(3 - step) * 2 + core, "mdl": mdl},
        )

    directs = (1, 2) if square else range(1, chips)

    def rightward(number, step):
        block = col_block(number, mdl - step)
        return pltpu.make_async_remote_copy(
            src_ref=block if step else cols_in[number],
            dst_ref=block,
            send_sem=to_right.at[number, step],
            recv_sem=from_left.at[number, step],
            device_id={"tok": tok, "mdl": mdl + 1},
        )

    def leftward(number, step):
        block = col_block(number, mdl + step)
        return pltpu.make_async_remote_copy(
            src_ref=block if step else cols_in[number],
            dst_ref=block,
            send_sem=to_left.at[number, step],
            recv_sem=from_right.at[number, step],
            device_id={"tok": tok, "mdl": mdl - 1},
        )

    def right_if(step):
        return (mdl >= step) & (mdl < n_mdl - 1)

    def left_if(step):
        return (mdl + step < n_mdl) & (mdl > 0)

    for number in range(n_col):
        @pl.when(right_if(0))
        def _():
            rightward(number, 0).start()

        @pl.when(left_if(0))
        def _():
            leftward(number, 0).start()

    locals_ = []
    for number in range(n_col):
        locals_.append(
            pltpu.make_async_copy(
                cols_in[number], col_block(number, mdl), local_sem.at[n_row + number]
            )
        )
        locals_[-1].start()
    for number in range(n_row):
        if prepare is not None:
            prepare(number)
        for step in directs:
            direct(number, step).start()
        direct(number, 0).start()
        locals_.append(
            pltpu.make_async_copy(rows_in[number], row_block(number, tok), local_sem.at[number])
        )
        locals_[-1].start()

    def finish_diagonal(number):
        for step in (1, 2):
            relayed(number, step).wait_recv()
        passed(number, 3).start()

    for turn in range(max(n_row, n_mdl - 2 if n_col else 0)):
        hop = turn + 1
        if hop < n_mdl - 1:
            for number in range(n_col):
                @pl.when(mdl >= hop)
                def _():
                    rightward(number, hop - 1).wait_recv()

                @pl.when(right_if(hop))
                def _():
                    rightward(number, hop).start()

                @pl.when(mdl + hop < n_mdl)
                def _():
                    leftward(number, hop - 1).wait_recv()

                @pl.when(left_if(hop))
                def _():
                    leftward(number, hop).start()

        if turn < n_row:
            for step in directs:
                direct(turn, step).wait_recv()
                if square:
                    relayed(turn, step).start()
                passed(turn, step).start()
            if square and turn > 0:
                finish_diagonal(turn - 1)
        if between is not None:
            between(turn)

    if square and n_row:
        finish_diagonal(n_row - 1)
    for copy in locals_:
        copy.wait()
    for number in range(n_col):
        @pl.when(mdl >= n_mdl - 1)
        def _():
            rightward(number, n_mdl - 2).wait_recv()

        @pl.when(mdl + n_mdl - 1 < n_mdl)
        def _():
            leftward(number, n_mdl - 2).wait_recv()

    for number in range(n_row):
        direct(number, 0).wait()
        for step in directs:
            direct(number, step).wait_send()
            if square:
                relayed(number, step).wait_send()
        for step in range(1, chips):
            passed(number, step).wait()
    for number in range(n_col):
        for step in range(n_mdl - 1):
            @pl.when(right_if(step))
            def _():
                rightward(number, step).wait_send()

            @pl.when(left_if(step))
            def _():
                leftward(number, step).wait_send()


def exchange_semaphores(n_tok, n_mdl, n_row, n_col):
    row_sem = pltpu.SemaphoreType.DMA((max(n_row, 1), n_tok // 2))
    col_sem = pltpu.SemaphoreType.DMA((max(n_col, 1), n_mdl))
    return [pltpu.SemaphoreType.DMA((n_row + n_col,))] + [row_sem] * 6 + [col_sem] * 4


def project_kernel(n_tok, n_mdl, head_width, *refs):
    normed, key_w, value_w, query_w, key_gain, query_gain, cosine, sine = refs[:8]
    keys_out, values_out, query_out = refs[8:11]
    keys, values, query, key_held, value_held, query_held, load_sem = refs[11:18]
    width = keys.shape[1]
    lanes = 2 * head_width
    block = 256 if width % 256 == 0 else lanes
    loads = [
        pltpu.make_async_copy(source, held, load_sem.at[number])
        for number, (source, held) in enumerate(
            ((key_w, key_held), (value_w, value_held), (query_w, query_held))
        )
    ]
    for load in loads:
        load.start()
    lane = lax.broadcasted_iota(jnp.int32, (1, lanes), 1)
    first = lane < head_width
    early = lane % head_width < head_width // 2

    def head_mean(terms):
        one = jnp.sum(jnp.where(first, terms, 0.0), axis=1, keepdims=True)
        other = jnp.sum(jnp.where(first, 0.0, terms), axis=1, keepdims=True)
        return jnp.where(first, one, other) * (1.0 / head_width)

    def finished(summed, gain):
        center = summed - head_mean(summed)
        normal = center * lax.rsqrt(head_mean(center * center) + 1e-06) * gain[...]
        partner = jnp.where(
            early,
            pltpu.roll(normal, lanes - head_width // 2, axis=1),
            pltpu.roll(normal, head_width // 2, axis=1),
        )
        return normal * cosine[...] + partner * sine[...]

    def project(held, gain, target):
        def step(number, carry):
            columns = pl.ds(pl.multiple_of(number * block, block), block)
            summed = jnp.dot(
                normed[...], held[:, columns], preferred_element_type=jnp.float32
            )
            if gain is not None:
                summed = jnp.concatenate(
                    [
                        finished(summed[:, start : start + lanes], gain)
                        for start in range(0, block, lanes)
                    ],
                    axis=1,
                )
            target[:, columns] = summed.astype(jnp.bfloat16)
            return carry

        lax.fori_loop(0, width // block, step, 0)

    def prepare(number):
        loads[number].wait()
        if number == 0:
            project(key_held, key_gain, keys)
        else:
            project(value_held, None, values)

    query_copy = pltpu.make_async_copy(query, query_out, load_sem.at[3])

    def between(turn):
        if turn == 0:
            loads[2].wait()
            project(query_held, query_gain, query)
            query_copy.start()

    exchange(
        n_tok,
        n_mdl,
        (keys, values),
        (),
        (keys_out, values_out),
        (),
        refs[18:],
        prepare,
        between,
    )
    query_copy.wait()


def project_and_gather(mesh, normed, weights, gains, cosine, sine, head_width, collective_id):
    n_tok, n_mdl = mesh.shape["tok"], mesh.shape["mdl"]
    own_rows, depth = normed.shape
    width = weights[0].shape[1]
    full = jax.ShapeDtypeStruct((own_rows * n_tok, width), jnp.bfloat16)
    own = jax.ShapeDtypeStruct((own_rows, width), jnp.bfloat16)
    anywhere = pl.BlockSpec(memory_space=pl.ANY)
    inside = pl.BlockSpec(memory_space=pltpu.VMEM)
    return pl.pallas_call(
        functools.partial(project_kernel, n_tok, n_mdl, head_width),
        out_shape=[full, full, own],
        in_specs=[inside] + [anywhere] * 3 + [inside] * 4,
        out_specs=[anywhere] * 3,
        scratch_shapes=[pltpu.VMEM((own_rows, width), jnp.bfloat16)] * 3
        + [pltpu.VMEM((depth, width), jnp.bfloat16)] * 3
        + [pltpu.SemaphoreType.DMA((4,))]
        + exchange_semaphores(n_tok, n_mdl, 2, 0),
        compiler_params=pltpu.CompilerParams(
            collective_id=collective_id, has_side_effects=True, vmem_limit_bytes=48 * 2**20
        ),
        name="project_and_gather",
    )(normed, *weights, *gains, cosine, sine)


def gather_all(mesh, over_tok, over_mdl, collective_id):
    n_tok, n_mdl = mesh.shape["tok"], mesh.shape["mdl"]
    n_row, n_col = len(over_tok), len(over_mdl)
    shapes = [
        jax.ShapeDtypeStruct((one.shape[0] * n_tok, one.shape[1]), one.dtype) for one in over_tok
    ] + [jax.ShapeDtypeStruct((one.shape[0], one.shape[1] * n_mdl), one.dtype) for one in over_mdl]
    return pl.pallas_call(
        functools.partial(gather_kernel, n_tok, n_mdl, n_row, n_col),
        out_shape=shapes,
        in_specs=[pl.BlockSpec(memory_space=pl.ANY)] * (n_row + n_col),
        out_specs=[pl.BlockSpec(memory_space=pl.ANY)] * (n_row + n_col),
        scratch_shapes=exchange_semaphores(n_tok, n_mdl, n_row, n_col),
        compiler_params=pltpu.CompilerParams(collective_id=collective_id, has_side_effects=True),
        name=f"gather_{collective_id}",
    )(*over_tok, *over_mdl)


def attend_kernel(rows_at_once, keys_at_once, head_width, meta_ref, q_ref, k_ref, v_ref, o_ref):
    bound, first_row = meta_ref[0], meta_ref[1]
    own_rows, lanes = q_ref.shape
    count = k_ref.shape[0]
    chunks = count // keys_at_once
    per = lanes // head_width
    lane = lax.broadcasted_iota(jnp.int32, (1, lanes), 1) // head_width
    masks = [(lane == head).astype(jnp.float32) for head in range(per)]
    edge = bound // keys_at_once
    edge_start = pl.multiple_of(edge * keys_at_once, keys_at_once)
    edge_keys = edge_start + lax.broadcasted_iota(jnp.int32, (keys_at_once, 1), 0)

    for block in range(own_rows // rows_at_once):
        rows = pl.ds(block * rows_at_once, rows_at_once)
        start = first_row + block * rows_at_once
        row_ids = start + lax.broadcasted_iota(jnp.int32, (rows_at_once, 1), 0)

        def add_chunk(carry, keys, values):
            queries = q_ref[rows, :]
            result = []
            for head in range(per):
                mine = queries * (masks[head] * head_width ** (-0.5)).astype(jnp.bfloat16)
                score = lax.dot_general(
                    mine, keys, (((1,), (1,)), ((), ())), preferred_element_type=jnp.float32
                )
                expo = jnp.exp(score).astype(jnp.bfloat16)
                result.append(
                    carry[head]
                    + jnp.dot(expo, values[head], preferred_element_type=jnp.float32)
                )
            return tuple(result)

        def inner(chunk, carry):
            here = pl.ds(pl.multiple_of(chunk * keys_at_once, keys_at_once), keys_at_once)
            values = v_ref[here, :]
            with_ones = [
                values * mask.astype(jnp.bfloat16) + (1.0 - mask).astype(jnp.bfloat16)
                for mask in masks
            ]
            return add_chunk(carry, k_ref[here, :], with_ones)

        for request in range(2):
            active = start < bound if request == 0 else start + rows_at_once > bound

            @pl.when(active)
            def _():
                here = pl.ds(edge_start, keys_at_once)
                inside = edge_keys < bound if request == 0 else edge_keys >= bound
                wide = v_ref[here, :].astype(jnp.float32)
                with_ones = [
                    jnp.where(inside, wide * mask + (1.0 - mask), 0.0).astype(jnp.bfloat16)
                    for mask in masks
                ]
                zero = jnp.zeros((rows_at_once, lanes), jnp.float32)
                carry = add_chunk((zero,) * per, k_ref[here, :], with_ones)
                if request == 0:
                    low, high = 0, edge
                else:
                    low, high = edge + 1, chunks
                carry = lax.fori_loop(low, high, inner, carry)
                output = zero
                for head in range(per):
                    total = pltpu.roll(carry[head], head_width, axis=1)
                    output = jnp.where(lane == head, carry[head] / total, output)
                if request == 0:
                    o_ref[rows, :] = output.astype(o_ref.dtype)
                else:
                    old = o_ref[rows, :].astype(jnp.float32)
                    o_ref[rows, :] = jnp.where(row_ids >= bound, output, old).astype(o_ref.dtype)


def attend(query, keys, values, bound, first_row, head_width, part, parts):
    width = query.shape[1]
    own_rows = query.shape[0] // parts
    count = keys.shape[0]
    lanes = 2 * head_width
    meta = jnp.stack([bound, first_row + part * own_rows]).astype(jnp.int32)
    block = pl.BlockSpec((own_rows, lanes), lambda pair, meta: (part, pair))
    out_block = pl.BlockSpec((own_rows, lanes), lambda pair, meta: (0, pair))
    full = pl.BlockSpec((count, lanes), lambda pair, meta: (0, pair))
    return pl.pallas_call(
        functools.partial(attend_kernel, 256, 512, head_width),
        out_shape=jax.ShapeDtypeStruct((own_rows, width), jnp.bfloat16),
        grid_spec=pltpu.PrefetchScalarGridSpec(
            num_scalar_prefetch=1,
            grid=(width // lanes,),
            in_specs=[block, full, full],
            out_specs=out_block,
        ),
        compiler_params=pltpu.CompilerParams(vmem_limit_bytes=58 * 2**20),
        cost_estimate=pl.CostEstimate(
            flops=4 * own_rows * count * width,
            bytes_accessed=4 * count * width,
            transcendentals=own_rows * count * width // head_width,
        ),
        name=f"attend_{part}",
    )(meta, query, keys, values)

def fused_kernel(n_mdl, total_rows, *refs):
    (
        bound_ref, normed, key_w, value_w, query_w, key_gain, query_gain, turns, hidden, gates, out_w,
        result,
        nrm, cs, wkv, wq, qx, kv, kbias, acc, att, att_send, wout, out_acc,
        load_sem, swap_send, swap_recv,
        dx_send, dx_recv, dy_send, dy_recv, rk_send, rk_recv, rv_send, rv_recv,
        as_send, as_recv, zr_send, zr_recv, zl_send, zl_recv,
        ox_send, ox_recv, oy_send, oy_recv, ou_send, ou_recv, ow_send, ow_recv, op_send, op_recv,
    ) = refs
    rows, depth = normed.shape
    pairs = wkv.shape[0]
    lanes = 128
    head_width = lanes // 2
    half_cols = pairs * lanes
    subs = 2 * pairs
    tok, mdl = lax.axis_index("tok"), lax.axis_index("mdl")
    chip, core = tok // 2, tok % 2
    other = 1 - core
    x_chip, y_chip, far_chip = chip + 1 - 2 * (chip % 2), (chip + 2) % 4, 3 - chip
    sibling = {"tok": chip * 2 + other, "mdl": mdl}
    x_dev = {"tok": x_chip * 2 + core, "mdl": mdl}
    y_dev = {"tok": y_chip * 2 + core, "mdl": mdl}
    remote = pltpu.make_async_remote_copy

    barrier = pltpu.get_barrier_semaphore()
    for device in (sibling, x_dev, y_dev):
        pl.semaphore_signal(barrier, inc=1, device_id=device)
    for side in (1, n_mdl - 1):
        pl.semaphore_signal(barrier, inc=1, device_id={"tok": tok, "mdl": (mdl + side) % n_mdl})

    own_normed = pltpu.make_async_copy(normed, nrm.at[core], load_sem.at[0])
    own_turns = pltpu.make_async_copy(turns, cs.at[core], load_sem.at[1])
    own_normed.start()
    own_turns.start()

    def columns(p):
        return pl.ds(pl.multiple_of(core * half_cols + p * lanes, lanes), lanes)

    kv_loads = []
    for p in range(pairs):
        one = pltpu.make_async_copy(
            key_w.at[:, columns(p)], wkv.at[p, :, pl.ds(0, lanes)], load_sem.at[2 + 2 * p]
        )
        two = pltpu.make_async_copy(
            value_w.at[:, columns(p)], wkv.at[p, :, pl.ds(lanes, lanes)], load_sem.at[3 + 2 * p]
        )
        one.start()
        two.start()
        kv_loads += [one, two]
    q_load = pltpu.make_async_copy(
        query_w.at[:, pl.ds(pl.multiple_of(core * half_cols, lanes), half_cols)],
        wq,
        load_sem.at[2 + 2 * pairs],
    )
    q_load.start()
    own_out = pltpu.make_async_copy(out_w, wout.at[chip, core], load_sem.at[3 + 2 * pairs])
    own_out.start()

    pl.semaphore_wait(barrier, 5)

    swap_normed = remote(
        src_ref=normed, dst_ref=nrm.at[core],
        send_sem=swap_send.at[0], recv_sem=swap_recv.at[0], device_id=sibling,
    )
    swap_turns = remote(
        src_ref=turns, dst_ref=cs.at[core],
        send_sem=swap_send.at[1], recv_sem=swap_recv.at[1], device_id=sibling,
    )
    swap_normed.start()
    swap_turns.start()

    def copy(block, sends, recvs, index, device, target=None):
        return remote(
            src_ref=block, dst_ref=block if target is None else target,
            send_sem=sends.at[index], recv_sem=recvs.at[index], device_id=device,
        )

    def half_of(s):
        return (core + s) % 2

    def direct_x(s):
        return copy(kv.at[s // 2, chip, half_of(s)], dx_send, dx_recv, s, x_dev)

    def direct_y(s):
        return copy(kv.at[s // 2, chip, half_of(s)], dy_send, dy_recv, s, y_dev)

    def relay_k(s):
        return copy(kv.at[s // 2, x_chip, half_of(s), 0], rk_send, rk_recv, s, y_dev)

    def relay_v(s):
        return copy(kv.at[s // 2, y_chip, half_of(s), 1], rv_send, rv_recv, s, x_dev)

    def swap_att(p):
        return copy(att_send.at[p], as_send, as_recv, p, sibling, att.at[mdl, p, core])

    def z_index(p, step):
        return p * (n_mdl - 1) + step

    def z_right(p, step):
        return copy(
            att.at[mdl - step, p], zr_send, zr_recv, z_index(p, step), {"tok": tok, "mdl": mdl + 1}
        )

    def z_left(p, step):
        return copy(
            att.at[mdl + step, p], zl_send, zl_recv, z_index(p, step), {"tok": tok, "mdl": mdl - 1}
        )

    def z_start(p, step):
        @pl.when((mdl >= step) & (mdl < n_mdl - 1))
        def _():
            z_right(p, step).start()

        @pl.when((mdl + step < n_mdl) & (mdl > 0))
        def _():
            z_left(p, step).start()

    def z_arrive(p, step):
        @pl.when(mdl >= step + 1)
        def _():
            z_right(p, step).wait_recv()

        @pl.when(mdl + step + 1 < n_mdl)
        def _():
            z_left(p, step).wait_recv()

    def z_sent(p, step):
        @pl.when((mdl >= step) & (mdl < n_mdl - 1))
        def _():
            z_right(p, step).wait_send()

        @pl.when((mdl + step < n_mdl) & (mdl > 0))
        def _():
            z_left(p, step).wait_send()

    depth_own = out_w.shape[0]
    first_half, second_half = pl.ds(0, depth_own // 2), pl.ds(depth_own // 2, depth_own // 2)
    out_x = copy(out_w, ox_send, ox_recv, 0, x_dev, wout.at[chip, core])
    out_y = copy(out_w, oy_send, oy_recv, 0, y_dev, wout.at[chip, core])
    out_relay_y = copy(wout.at[x_chip, core, first_half], ou_send, ou_recv, 0, y_dev)
    out_relay_x = copy(wout.at[y_chip, core, second_half], ow_send, ow_recv, 0, x_dev)
    out_pass = [
        copy(out_w, op_send, op_recv, 0, sibling, wout.at[chip, core]),
        copy(wout.at[x_chip, core], op_send, op_recv, 1, sibling),
        copy(wout.at[y_chip, core], op_send, op_recv, 2, sibling),
        copy(wout.at[far_chip, core], op_send, op_recv, 3, sibling),
    ]

    lane = lax.broadcasted_iota(jnp.int32, (1, lanes), 1)
    first = lane < head_width
    early = lane % head_width < head_width // 2
    spot = lane % head_width
    bound = bound_ref[0]

    def request_terms(start, count, same, differs):
        ids = start + lax.broadcasted_iota(jnp.int32, (count, lanes), 0)
        later = ids >= bound
        zero_side = jnp.where(later, differs, same)
        one_side = jnp.where(later, same, differs)
        return jnp.where(spot == 0, zero_side, jnp.where(spot == 1, one_side, 0.0))

    def bias_step(index, carry):
        kbias[index] = request_terms(index * rows, rows, 0.0, -16384.0).astype(jnp.bfloat16)
        return carry

    lax.fori_loop(0, total_rows // rows, bias_step, 0)

    def clear(p, carry):
        acc[p] = jnp.zeros(acc.shape[1:], jnp.float32)
        return carry

    lax.fori_loop(0, pairs, clear, 0)

    def head_mean(terms):
        one = jnp.sum(jnp.where(first, terms, 0.0), axis=1, keepdims=True)
        two = jnp.sum(jnp.where(first, 0.0, terms), axis=1, keepdims=True)
        return jnp.where(first, one, two) * (1.0 / head_width)

    def finished(summed, gain, half):
        center = summed - head_mean(summed)
        normal = center * lax.rsqrt(head_mean(center * center) + 1e-06) * gain
        partner = jnp.where(
            early,
            pltpu.roll(normal, lanes - head_width // 2, axis=1),
            pltpu.roll(normal, head_width // 2, axis=1),
        )
        return normal * cs[half, 0] + partner * cs[half, 1]

    own_normed.wait()
    own_turns.wait()
    for p in range(pairs):
        kv_loads[2 * p].wait()
        kv_loads[2 * p + 1].wait()

    def project_pair(s, carry):
        p, half = s // 2, half_of(s)

        @pl.when(s == 1)
        def _():
            swap_normed.wait_recv()
            swap_turns.wait_recv()

        summed = jnp.dot(nrm[half], wkv[p], preferred_element_type=jnp.float32)
        kv[p, chip, half, 0] = finished(summed[:, :lanes], key_gain[...], half).astype(jnp.bfloat16)
        kv[p, chip, half, 1] = summed[:, lanes:].astype(jnp.bfloat16)

        @pl.when(s < 2)
        def _():
            direct_x(s).start()
            direct_y(s).start()

        return carry

    lax.fori_loop(0, subs, project_pair, 0)
    q_load.wait()

    def project_query(half, carry):
        where = pl.ds(pl.multiple_of(half * rows, rows), rows)
        terms = request_terms((chip * 2 + half) * rows, rows, 0.0, 1.0)
        terms = jnp.where(spot < 2, 1.0 - terms, 0.0)
        gain = query_gain[...] * (head_width ** (-0.5) * 1.4426950408889634)
        for start in range(0, half_cols, 2 * lanes):
            stop = min(start + 2 * lanes, half_cols)
            summed = jnp.dot(nrm[half], wq[:, start:stop], preferred_element_type=jnp.float32)
            for part in range((stop - start) // lanes):
                p = start // lanes + part
                query = finished(summed[:, part * lanes : (part + 1) * lanes], gain, half)
                qx[2 * p, where, :] = jnp.where(first, query, terms).astype(jnp.bfloat16)
                qx[2 * p + 1, where, :] = jnp.where(first, terms, query).astype(jnp.bfloat16)
        return carry

    lax.fori_loop(0, 2, project_query, 0)

    most = TEXT + (total_rows - 2 * TEXT) * 5 // 8
    last_first = -(-most // rows)
    first_last = (total_rows - most) // rows

    def needed(row_block, key_block):
        return (
            ((row_block < first_last) & (key_block < last_first))
            | ((row_block >= last_first) & (key_block >= first_last))
            | ((row_block >= first_last) & (row_block < last_first))
        )

    def attend_rows(where, s, source):
        p, half = s // 2, half_of(s)
        keys, values = kv[p, source, half, 0], kv[p, source, half, 1]
        bias = kbias[source * 2 + half]
        ones = jnp.ones_like(values)
        for head in range(2):
            mine = first if head == 0 else jnp.logical_not(first)
            score = lax.dot_general(
                qx[2 * p + head, where, :],
                jnp.where(mine, keys, bias),
                (((1,), (1,)), ((), ())),
                preferred_element_type=jnp.float32,
            )
            expo = jnp.exp2(score).astype(jnp.bfloat16)
            acc[p, head, where, :] += jnp.dot(
                expo, jnp.where(mine, values, ones), preferred_element_type=jnp.float32
            )

    def attend_unit(s, source, valid):
        key_block = source * 2 + half_of(s)
        low, high = needed(chip * 2, key_block), needed(chip * 2 + 1, key_block)

        @pl.when(valid & low & high)
        def _():
            attend_rows(pl.ds(0, 2 * rows), s, source)

        @pl.when(valid & low & jnp.logical_not(high))
        def _():
            attend_rows(pl.ds(0, rows), s, source)

        @pl.when(valid & high & jnp.logical_not(low))
        def _():
            attend_rows(pl.ds(rows, rows), s, source)

    def finish_pair(p):
        def rows_of(index):
            where = pl.ds(pl.multiple_of(index * rows, rows), rows)
            one, two = acc[p, 0, where, :], acc[p, 1, where, :]
            summed = jnp.where(first, one, two)
            counted = pltpu.roll(jnp.where(first, two, one), head_width, axis=1)
            return (summed / counted).astype(jnp.bfloat16)

        att_send[p] = rows_of(other)
        swap_att(p).start()
        att[mdl, p, core] = rows_of(core)

    def turn(s, carry):
        def visit(j, inner):
            source = jnp.where(
                j == 0, chip, jnp.where(j == 1, x_chip, jnp.where(j == 2, y_chip, far_chip))
            )
            unit = jnp.where(j == 3, s - 1, s)
            valid = (unit >= 0) & (unit < subs)
            unit = jnp.where(valid, unit, 0)

            @pl.when((j == 0) & (s % 2 == 1) & (s >= 3))
            def _():
                p = (s - 3) // 2
                swap_att(p).wait_recv()
                z_start(p, 0)

            @pl.when((j == 1) & (s < subs))
            def _():
                direct_x(s).wait_recv()
                direct_y(s).wait_recv()
                relay_k(s).start()
                relay_v(s).start()

                @pl.when(s + 2 < subs)
                def _():
                    direct_x(s + 2).start()
                    direct_y(s + 2).start()

                @pl.when(s + 2 == subs)
                def _():
                    out_x.start()
                    out_y.start()
                    out_pass[0].start()

            @pl.when((j == 2) & (s % 2 == 0) & (s >= 4))
            def _():
                p = (s - 4) // 2
                z_arrive(p, 1)
                z_start(p, 2)

            @pl.when((j == 3) & (s % 2 == 1) & (s >= 3))
            def _():
                p = (s - 3) // 2
                z_arrive(p, 0)
                z_start(p, 1)

            @pl.when((j == 3) & (s >= 1))
            def _():
                relay_k(s - 1).wait_recv()
                relay_v(s - 1).wait_recv()

            attend_unit(unit, source, valid)

            @pl.when((j == 3) & (s % 2 == 0) & (s >= 2))
            def _():
                finish_pair((s - 2) // 2)

            return inner

        return lax.fori_loop(0, 4, visit, carry)

    lax.fori_loop(0, subs + 1, turn, 0)

    final = pairs - 1
    swap_att(final).wait_recv()
    z_start(final, 0)
    out_x.wait_recv()
    out_y.wait_recv()
    out_relay_y.start()
    out_relay_x.start()
    out_pass[1].start()
    out_pass[2].start()
    z_arrive(final, 0)
    z_start(final, 1)
    z_arrive(final, 1)
    z_start(final, 2)
    out_relay_y.wait_recv()
    out_relay_x.wait_recv()
    out_pass[3].start()
    own_out.wait()
    for one in out_pass:
        one.wait_recv()
    for p in range(pairs - 1):
        z_arrive(p, n_mdl - 2)

    def combine(p):
        tall = [
            wout[block, side, p * lanes : (p + 1) * lanes, :]
            for block in range(n_mdl)
            for side in range(2)
        ]
        wide = [att[block, p, side] for block in range(n_mdl) for side in range(2)]
        return jnp.dot(
            jnp.concatenate(wide, axis=1),
            jnp.concatenate(tall, axis=0),
            preferred_element_type=jnp.float32,
        )

    out_acc[...] = combine(0)
    for p in range(1, pairs - 1):
        out_acc[...] += combine(p)
    z_arrive(final, n_mdl - 2)
    projected = out_acc[...] + combine(final)
    ids = tok * rows + lax.broadcasted_iota(jnp.int32, (rows, 1), 0)
    place = jnp.where(ids >= bound, ids - bound, ids)
    gate = jnp.where(place < TEXT, gates[1:2, :], gates[0:1, :])
    result[...] = (hidden[...].astype(jnp.float32) + gate * projected).astype(jnp.bfloat16)

    swap_normed.wait_send()
    swap_turns.wait_send()
    for s in range(subs):
        direct_x(s).wait_send()
        direct_y(s).wait_send()
        relay_k(s).wait_send()
        relay_v(s).wait_send()
    for p in range(pairs):
        swap_att(p).wait_send()
        for step in range(n_mdl - 1):
            z_sent(p, step)
    for one in [out_x, out_y, out_relay_y, out_relay_x] + out_pass:
        one.wait_send()


def fused(
    mesh, bound, normed, weights, gains, turns, hidden, gates, out_weight, head_width, collective_id
):
    n_tok, n_mdl = mesh.shape["tok"], mesh.shape["mdl"]
    rows, depth = normed.shape
    width = hidden.shape[1]
    lanes = 2 * head_width
    pairs = width // (2 * lanes)
    total_rows = rows * n_tok
    chips = n_tok // 2
    subs = 2 * pairs
    bf, f32 = jnp.bfloat16, jnp.float32
    anywhere = pl.BlockSpec(memory_space=pl.ANY)
    inside = pl.BlockSpec(memory_space=pltpu.VMEM)

    def sems(count):
        return [pltpu.SemaphoreType.DMA((count,))]

    return pl.pallas_call(
        functools.partial(fused_kernel, n_mdl, total_rows),
        out_shape=jax.ShapeDtypeStruct((rows, width), bf),
        in_specs=[pl.BlockSpec(memory_space=pltpu.SMEM)]
        + [anywhere] * 4
        + [inside] * 2
        + [anywhere]
        + [inside] * 2
        + [anywhere],
        out_specs=inside,
        scratch_shapes=[
            pltpu.VMEM((2, rows, depth), bf),
            pltpu.VMEM((2, 2, rows, lanes), f32),
            pltpu.VMEM((pairs, depth, 2 * lanes), bf),
            pltpu.VMEM((depth, pairs * lanes), bf),
            pltpu.VMEM((2 * pairs, 2 * rows, lanes), bf),
            pltpu.VMEM((pairs, chips, 2, 2, rows, lanes), bf),
            pltpu.VMEM((n_tok, rows, lanes), bf),
            pltpu.VMEM((pairs, 2, 2 * rows, lanes), f32),
            pltpu.VMEM((n_mdl, pairs, 2, rows, lanes), bf),
            pltpu.VMEM((pairs, rows, lanes), bf),
            pltpu.VMEM((chips, 2) + out_weight.shape, bf),
            pltpu.VMEM((rows, width), f32),
        ]
        + sems(4 + 2 * pairs)
        + sems(2) * 2
        + sems(subs) * 8
        + sems(pairs) * 2
        + sems(pairs * (n_mdl - 1)) * 4
        + sems(1) * 8
        + sems(4) * 2,
        compiler_params=pltpu.CompilerParams(
            collective_id=collective_id, has_side_effects=True, vmem_limit_bytes=58 * 2**20
        ),
        name="fused",
    )(bound, normed, *weights, *gains, turns, hidden, gates, out_weight)


def shards(
    mesh,
    hidden_states,
    lengths,
    positions,
    modulation,
    query_weight,
    key_weight,
    value_weight,
    out_weight,
    query_gain,
    key_gain,
):
    own_rows = hidden_states.shape[0]
    head_width = query_gain.shape[0]
    full_rows = lax.all_gather(hidden_states, "mdl", axis=1, tiled=True)
    key_full, value_full, query_full = gather_all(
        mesh, [key_weight, value_weight, query_weight], [], 0
    )
    row_index = lax.axis_index("tok") * own_rows + jnp.arange(own_rows, dtype=jnp.int32)
    request, is_text, bound = token_labels(row_index, lengths)
    normed = modulate(full_rows, modulation, is_text)
    angles = pair_angles(positions, head_width // 2)
    textual = is_text[:, None]
    cosine = jnp.tile(jnp.where(textual, 1.0, jnp.cos(angles)), (1, 4))
    sine = jnp.where(textual, 0.0, jnp.sin(angles))
    sine = jnp.tile(jnp.concatenate([-sine, sine], axis=1), (1, 2))
    if mesh.shape["tok"] == 8 and mesh.shape["mdl"] == 4:
        out_width = out_weight.shape[1]
        gates = lax.dynamic_slice_in_dim(
            modulation, lax.axis_index("mdl") * out_width, out_width, 1
        )
        return fused(
            mesh,
            bound[None].astype(jnp.int32),
            normed,
            (key_full, value_full, query_full),
            [jnp.tile(gain, 2)[None, :] for gain in (key_gain, query_gain)],
            jnp.stack([cosine, sine]),
            hidden_states,
            jnp.stack([gates[2], gates[5]]),
            out_weight,
            head_width,
            1,
        )
    keys, values, query_flat = project_and_gather(
        mesh,
        normed,
        (key_full, value_full, query_full),
        [jnp.tile(gain, 2)[None, :] for gain in (key_gain, query_gain)],
        cosine,
        sine,
        head_width,
        1,
    )
    first_row = lax.axis_index("tok") * own_rows
    first, second = (
        attend(query_flat, keys, values, bound, first_row, head_width, part, 2)
        for part in range(2)
    )
    first_heads = lax.all_gather(first, "mdl", axis=1, tiled=True)
    out_full, second_heads = gather_all(mesh, [out_weight], [second], 2)
    out_width = out_weight.shape[1]
    projected = jnp.concatenate(
        [
            jnp.dot(heads, out_full, preferred_element_type=jnp.float32)
            for heads in (first_heads, second_heads)
        ],
        axis=0,
    )
    gate_rows = lax.dynamic_slice_in_dim(
        modulation, lax.axis_index("mdl") * out_width, out_width, 1
    )
    gate = jnp.where(is_text[:, None], gate_rows[5][None, :], gate_rows[2][None, :])
    return (hidden_states.astype(jnp.float32) + gate * projected).astype(jnp.bfloat16)


def solution(mesh):
    return jax.shard_map(
        functools.partial(shards, mesh),
        mesh=mesh,
        in_specs=(
            P("tok", "mdl"),
            P(),
            P(None, "tok"),
            P(),
            P("tok", "mdl"),
            P("tok", "mdl"),
            P("tok", "mdl"),
            P("tok", "mdl"),
            P(),
            P(),
        ),
        out_specs=P("tok", "mdl"),
        check_vma=False,
    )
```

```python
import functools
import jax
import jax.numpy as jnp
from jax import lax
from jax.experimental import pallas as pl
from jax.experimental.pallas import tpu as pltpu
from jax.sharding import PartitionSpec as P

TEXT = 226


def token_labels(row_index, lengths):
    bound = TEXT + lengths[0]
    request = (row_index >= bound).astype(jnp.int32)
    place = row_index - request * bound
    return (request, place < TEXT, bound)


def modulate(rows_bf, modulation, is_text):
    values = rows_bf.astype(jnp.float32)
    center = values - jnp.mean(values, axis=1, keepdims=True)
    spread = jnp.mean(center * center, axis=1, keepdims=True)
    normal = center * lax.rsqrt(spread + 1e-05)
    textual = is_text[:, None]
    shift = jnp.where(textual, modulation[3][None, :], modulation[0][None, :])
    scale = jnp.where(textual, modulation[4][None, :], modulation[1][None, :])
    return (normal * (1.0 + scale) + shift).astype(jnp.bfloat16)


def pair_angles(positions, pairs):
    index = jnp.arange(pairs, dtype=jnp.int32)
    first = pairs // 4
    second = (pairs - first) // 2
    third = pairs - first - second
    component = jnp.where(index < first, 0, jnp.where(index < first + second, 1, 2))
    local = index - jnp.where(component == 0, 0, jnp.where(component == 1, first, first + second))
    count = jnp.where(component == 0, first, jnp.where(component == 1, second, third))
    rates = jnp.power(jnp.float32(10000.0), -local.astype(jnp.float32) / count.astype(jnp.float32))
    places = positions.astype(jnp.float32)
    chosen = jnp.where(
        component[:, None] == 0,
        places[0][None, :],
        jnp.where(component[:, None] == 1, places[1][None, :], places[2][None, :]),
    )
    return jnp.transpose(chosen * rates[:, None])


def gather_kernel(n_tok, n_mdl, n_row, n_col, *refs):
    count = n_row + n_col
    ins, outs = refs[:count], refs[count : 2 * count]
    exchange(
        n_tok, n_mdl, ins[:n_row], ins[n_row:], outs[:n_row], outs[n_row:], refs[2 * count :]
    )


def exchange(
    n_tok, n_mdl, rows_in, cols_in, rows_out, cols_out, semaphores, prepare=None, between=None
):
    n_row, n_col = len(rows_in), len(cols_in)
    (
        local_sem,
        send1,
        recv1,
        send2,
        recv2,
        send3,
        recv3,
        to_right,
        from_left,
        to_left,
        from_right,
    ) = semaphores
    square = n_tok == 8
    chips = n_tok // 2
    tok, mdl = lax.axis_index("tok"), lax.axis_index("mdl")
    chip, core = tok // 2, tok % 2
    sibling = chip * 2 + 1 - core

    def chip_at(step):
        if square:
            return (chip, chip + 1 - 2 * (chip % 2), (chip + 2) % 4, 3 - chip)[step]
        return (chip + step) % chips

    def source_at(step):
        return chip_at(step) if square else chip_at(chips - step)

    barrier = pltpu.get_barrier_semaphore()
    greeted = 0
    if n_row:
        for step in (1, 2) if square else range(1, chips):
            pl.semaphore_signal(
                barrier, inc=1, device_id={"tok": chip_at(step) * 2 + core, "mdl": mdl}
            )
            greeted += 1
        pl.semaphore_signal(barrier, inc=1, device_id={"tok": sibling, "mdl": mdl})
        greeted += 1
    if n_col:
        for side in (1, n_mdl - 1):
            pl.semaphore_signal(
                barrier, inc=1, device_id={"tok": tok, "mdl": (mdl + side) % n_mdl}
            )
            greeted += 1
    pl.semaphore_wait(barrier, greeted)

    def row_block(number, owner):
        size = rows_in[number].shape[0]
        return rows_out[number].at[pl.ds(pl.multiple_of(owner * size, size), size), :]

    def col_block(number, owner):
        size = cols_in[number].shape[1]
        return cols_out[number].at[:, pl.ds(pl.multiple_of(owner * size, size), size)]

    def direct(number, step):
        target = chip_at(step) * 2 + core if step else sibling
        return pltpu.make_async_remote_copy(
            src_ref=rows_in[number],
            dst_ref=row_block(number, tok),
            send_sem=send1.at[number, step],
            recv_sem=recv1.at[number, step],
            device_id={"tok": target, "mdl": mdl},
        )

    def passed(number, step):
        block = row_block(number, source_at(step) * 2 + core)
        return pltpu.make_async_remote_copy(
            src_ref=block,
            dst_ref=block,
            send_sem=send2.at[number, step],
            recv_sem=recv2.at[number, step],
            device_id={"tok": sibling, "mdl": mdl},
        )

    def relayed(number, step):
        half = rows_in[number].shape[0] // 2
        first = (source_at(step) * 2 + core) * 2 * half + (step - 1) * half
        block = rows_out[number].at[pl.ds(pl.multiple_of(first, half), half), :]
        return pltpu.make_async_remote_copy(
            src_ref=block,
            dst_ref=block,
            send_sem=send3.at[number, step],
            recv_sem=recv3.at[number, step],
            device_id={"tok": chip_at(3 - step) * 2 + core, "mdl": mdl},
        )

    directs = (1, 2) if square else range(1, chips)

    def rightward(number, step):
        block = col_block(number, mdl - step)
        return pltpu.make_async_remote_copy(
            src_ref=block if step else cols_in[number],
            dst_ref=block,
            send_sem=to_right.at[number, step],
            recv_sem=from_left.at[number, step],
            device_id={"tok": tok, "mdl": mdl + 1},
        )

    def leftward(number, step):
        block = col_block(number, mdl + step)
        return pltpu.make_async_remote_copy(
            src_ref=block if step else cols_in[number],
            dst_ref=block,
            send_sem=to_left.at[number, step],
            recv_sem=from_right.at[number, step],
            device_id={"tok": tok, "mdl": mdl - 1},
        )

    def right_if(step):
        return (mdl >= step) & (mdl < n_mdl - 1)

    def left_if(step):
        return (mdl + step < n_mdl) & (mdl > 0)

    for number in range(n_col):
        @pl.when(right_if(0))
        def _():
            rightward(number, 0).start()

        @pl.when(left_if(0))
        def _():
            leftward(number, 0).start()

    locals_ = []
    for number in range(n_col):
        locals_.append(
            pltpu.make_async_copy(
                cols_in[number], col_block(number, mdl), local_sem.at[n_row + number]
            )
        )
        locals_[-1].start()
    for number in range(n_row):
        if prepare is not None:
            prepare(number)
        for step in directs:
            direct(number, step).start()
        direct(number, 0).start()
        locals_.append(
            pltpu.make_async_copy(rows_in[number], row_block(number, tok), local_sem.at[number])
        )
        locals_[-1].start()

    def finish_diagonal(number):
        for step in (1, 2):
            relayed(number, step).wait_recv()
        passed(number, 3).start()

    for turn in range(max(n_row, n_mdl - 2 if n_col else 0)):
        hop = turn + 1
        if hop < n_mdl - 1:
            for number in range(n_col):
                @pl.when(mdl >= hop)
                def _():
                    rightward(number, hop - 1).wait_recv()

                @pl.when(right_if(hop))
                def _():
                    rightward(number, hop).start()

                @pl.when(mdl + hop < n_mdl)
                def _():
                    leftward(number, hop - 1).wait_recv()

                @pl.when(left_if(hop))
                def _():
                    leftward(number, hop).start()

        if turn < n_row:
            for step in directs:
                direct(turn, step).wait_recv()
                if square:
                    relayed(turn, step).start()
                passed(turn, step).start()
            if square and turn > 0:
                finish_diagonal(turn - 1)
        if between is not None:
            between(turn)

    if square and n_row:
        finish_diagonal(n_row - 1)
    for copy in locals_:
        copy.wait()
    for number in range(n_col):
        @pl.when(mdl >= n_mdl - 1)
        def _():
            rightward(number, n_mdl - 2).wait_recv()

        @pl.when(mdl + n_mdl - 1 < n_mdl)
        def _():
            leftward(number, n_mdl - 2).wait_recv()

    for number in range(n_row):
        direct(number, 0).wait()
        for step in directs:
            direct(number, step).wait_send()
            if square:
                relayed(number, step).wait_send()
        for step in range(1, chips):
            passed(number, step).wait()
    for number in range(n_col):
        for step in range(n_mdl - 1):
            @pl.when(right_if(step))
            def _():
                rightward(number, step).wait_send()

            @pl.when(left_if(step))
            def _():
                leftward(number, step).wait_send()


def exchange_semaphores(n_tok, n_mdl, n_row, n_col):
    row_sem = pltpu.SemaphoreType.DMA((max(n_row, 1), n_tok // 2))
    col_sem = pltpu.SemaphoreType.DMA((max(n_col, 1), n_mdl))
    return [pltpu.SemaphoreType.DMA((n_row + n_col,))] + [row_sem] * 6 + [col_sem] * 4


def project_kernel(n_tok, n_mdl, head_width, *refs):
    normed, key_w, value_w, query_w, key_gain, query_gain, cosine, sine = refs[:8]
    keys_out, values_out, query_out = refs[8:11]
    keys, values, query, key_held, value_held, query_held, load_sem = refs[11:18]
    width = keys.shape[1]
    lanes = 2 * head_width
    block = 256 if width % 256 == 0 else lanes
    loads = [
        pltpu.make_async_copy(source, held, load_sem.at[number])
        for number, (source, held) in enumerate(
            ((key_w, key_held), (value_w, value_held), (query_w, query_held))
        )
    ]
    for load in loads:
        load.start()
    lane = lax.broadcasted_iota(jnp.int32, (1, lanes), 1)
    first = lane < head_width
    early = lane % head_width < head_width // 2

    def head_mean(terms):
        one = jnp.sum(jnp.where(first, terms, 0.0), axis=1, keepdims=True)
        other = jnp.sum(jnp.where(first, 0.0, terms), axis=1, keepdims=True)
        return jnp.where(first, one, other) * (1.0 / head_width)

    def finished(summed, gain):
        center = summed - head_mean(summed)
        normal = center * lax.rsqrt(head_mean(center * center) + 1e-06) * gain[...]
        partner = jnp.where(
            early,
            pltpu.roll(normal, lanes - head_width // 2, axis=1),
            pltpu.roll(normal, head_width // 2, axis=1),
        )
        return normal * cosine[...] + partner * sine[...]

    def project(held, gain, target):
        def step(number, carry):
            columns = pl.ds(pl.multiple_of(number * block, block), block)
            summed = jnp.dot(
                normed[...], held[:, columns], preferred_element_type=jnp.float32
            )
            if gain is not None:
                summed = jnp.concatenate(
                    [
                        finished(summed[:, start : start + lanes], gain)
                        for start in range(0, block, lanes)
                    ],
                    axis=1,
                )
            target[:, columns] = summed.astype(jnp.bfloat16)
            return carry

        lax.fori_loop(0, width // block, step, 0)

    def prepare(number):
        loads[number].wait()
        if number == 0:
            project(key_held, key_gain, keys)
        else:
            project(value_held, None, values)

    query_copy = pltpu.make_async_copy(query, query_out, load_sem.at[3])

    def between(turn):
        if turn == 0:
            loads[2].wait()
            project(query_held, query_gain, query)
            query_copy.start()

    exchange(
        n_tok,
        n_mdl,
        (keys, values),
        (),
        (keys_out, values_out),
        (),
        refs[18:],
        prepare,
        between,
    )
    query_copy.wait()


def project_and_gather(mesh, normed, weights, gains, cosine, sine, head_width, collective_id):
    n_tok, n_mdl = mesh.shape["tok"], mesh.shape["mdl"]
    own_rows, depth = normed.shape
    width = weights[0].shape[1]
    full = jax.ShapeDtypeStruct((own_rows * n_tok, width), jnp.bfloat16)
    own = jax.ShapeDtypeStruct((own_rows, width), jnp.bfloat16)
    anywhere = pl.BlockSpec(memory_space=pl.ANY)
    inside = pl.BlockSpec(memory_space=pltpu.VMEM)
    return pl.pallas_call(
        functools.partial(project_kernel, n_tok, n_mdl, head_width),
        out_shape=[full, full, own],
        in_specs=[inside] + [anywhere] * 3 + [inside] * 4,
        out_specs=[anywhere] * 3,
        scratch_shapes=[pltpu.VMEM((own_rows, width), jnp.bfloat16)] * 3
        + [pltpu.VMEM((depth, width), jnp.bfloat16)] * 3
        + [pltpu.SemaphoreType.DMA((4,))]
        + exchange_semaphores(n_tok, n_mdl, 2, 0),
        compiler_params=pltpu.CompilerParams(
            collective_id=collective_id, has_side_effects=True, vmem_limit_bytes=48 * 2**20
        ),
        name="project_and_gather",
    )(normed, *weights, *gains, cosine, sine)


def gather_all(mesh, over_tok, over_mdl, collective_id):
    n_tok, n_mdl = mesh.shape["tok"], mesh.shape["mdl"]
    n_row, n_col = len(over_tok), len(over_mdl)
    shapes = [
        jax.ShapeDtypeStruct((one.shape[0] * n_tok, one.shape[1]), one.dtype) for one in over_tok
    ] + [jax.ShapeDtypeStruct((one.shape[0], one.shape[1] * n_mdl), one.dtype) for one in over_mdl]
    return pl.pallas_call(
        functools.partial(gather_kernel, n_tok, n_mdl, n_row, n_col),
        out_shape=shapes,
        in_specs=[pl.BlockSpec(memory_space=pl.ANY)] * (n_row + n_col),
        out_specs=[pl.BlockSpec(memory_space=pl.ANY)] * (n_row + n_col),
        scratch_shapes=exchange_semaphores(n_tok, n_mdl, n_row, n_col),
        compiler_params=pltpu.CompilerParams(collective_id=collective_id, has_side_effects=True),
        name=f"gather_{collective_id}",
    )(*over_tok, *over_mdl)


def attend_kernel(rows_at_once, keys_at_once, head_width, meta_ref, q_ref, k_ref, v_ref, o_ref):
    bound, first_row = meta_ref[0], meta_ref[1]
    own_rows, lanes = q_ref.shape
    count = k_ref.shape[0]
    chunks = count // keys_at_once
    per = lanes // head_width
    lane = lax.broadcasted_iota(jnp.int32, (1, lanes), 1) // head_width
    masks = [(lane == head).astype(jnp.float32) for head in range(per)]
    edge = bound // keys_at_once
    edge_start = pl.multiple_of(edge * keys_at_once, keys_at_once)
    edge_keys = edge_start + lax.broadcasted_iota(jnp.int32, (keys_at_once, 1), 0)

    for block in range(own_rows // rows_at_once):
        rows = pl.ds(block * rows_at_once, rows_at_once)
        start = first_row + block * rows_at_once
        row_ids = start + lax.broadcasted_iota(jnp.int32, (rows_at_once, 1), 0)

        def add_chunk(carry, keys, values):
            queries = q_ref[rows, :]
            result = []
            for head in range(per):
                mine = queries * (masks[head] * head_width ** (-0.5)).astype(jnp.bfloat16)
                score = lax.dot_general(
                    mine, keys, (((1,), (1,)), ((), ())), preferred_element_type=jnp.float32
                )
                expo = jnp.exp(score).astype(jnp.bfloat16)
                result.append(
                    carry[head]
                    + jnp.dot(expo, values[head], preferred_element_type=jnp.float32)
                )
            return tuple(result)

        def inner(chunk, carry):
            here = pl.ds(pl.multiple_of(chunk * keys_at_once, keys_at_once), keys_at_once)
            values = v_ref[here, :]
            with_ones = [
                values * mask.astype(jnp.bfloat16) + (1.0 - mask).astype(jnp.bfloat16)
                for mask in masks
            ]
            return add_chunk(carry, k_ref[here, :], with_ones)

        for request in range(2):
            active = start < bound if request == 0 else start + rows_at_once > bound

            @pl.when(active)
            def _():
                here = pl.ds(edge_start, keys_at_once)
                inside = edge_keys < bound if request == 0 else edge_keys >= bound
                wide = v_ref[here, :].astype(jnp.float32)
                with_ones = [
                    jnp.where(inside, wide * mask + (1.0 - mask), 0.0).astype(jnp.bfloat16)
                    for mask in masks
                ]
                zero = jnp.zeros((rows_at_once, lanes), jnp.float32)
                carry = add_chunk((zero,) * per, k_ref[here, :], with_ones)
                if request == 0:
                    low, high = 0, edge
                else:
                    low, high = edge + 1, chunks
                carry = lax.fori_loop(low, high, inner, carry)
                output = zero
                for head in range(per):
                    total = pltpu.roll(carry[head], head_width, axis=1)
                    output = jnp.where(lane == head, carry[head] / total, output)
                if request == 0:
                    o_ref[rows, :] = output.astype(o_ref.dtype)
                else:
                    old = o_ref[rows, :].astype(jnp.float32)
                    o_ref[rows, :] = jnp.where(row_ids >= bound, output, old).astype(o_ref.dtype)


def attend(query, keys, values, bound, first_row, head_width, part, parts):
    width = query.shape[1]
    own_rows = query.shape[0] // parts
    count = keys.shape[0]
    lanes = 2 * head_width
    meta = jnp.stack([bound, first_row + part * own_rows]).astype(jnp.int32)
    block = pl.BlockSpec((own_rows, lanes), lambda pair, meta: (part, pair))
    out_block = pl.BlockSpec((own_rows, lanes), lambda pair, meta: (0, pair))
    full = pl.BlockSpec((count, lanes), lambda pair, meta: (0, pair))
    return pl.pallas_call(
        functools.partial(attend_kernel, 256, 512, head_width),
        out_shape=jax.ShapeDtypeStruct((own_rows, width), jnp.bfloat16),
        grid_spec=pltpu.PrefetchScalarGridSpec(
            num_scalar_prefetch=1,
            grid=(width // lanes,),
            in_specs=[block, full, full],
            out_specs=out_block,
        ),
        compiler_params=pltpu.CompilerParams(vmem_limit_bytes=58 * 2**20),
        cost_estimate=pl.CostEstimate(
            flops=4 * own_rows * count * width,
            bytes_accessed=4 * count * width,
            transcendentals=own_rows * count * width // head_width,
        ),
        name=f"attend_{part}",
    )(meta, query, keys, values)

def fused_kernel(n_mdl, total_rows, *refs):
    (
        lengths, hidden, positions, modulation, key_w, value_w, query_w, out_w, key_gain, query_gain,
        result,
        hid, nrm, cs, weights, qx, kv, kbias, acc, att, att_send, wout, out_acc,
        load_sem, tile_sem, swap_send, swap_recv,
        hr_send, hr_recv, hl_send, hl_recv, ns_send, ns_recv, ws_send, ws_recv,
        wx_send, wx_recv, wy_send, wy_recv, wr_send, wr_recv, wl_send, wl_recv,
        dx_send, dx_recv, dy_send, dy_recv, rk_send, rk_recv, rv_send, rv_recv,
        as_send, as_recv, zr_send, zr_recv, zl_send, zl_recv,
        ox_send, ox_recv, oy_send, oy_recv, ou_send, ou_recv, ow_send, ow_recv, op_send, op_recv,
    ) = refs
    rows, width = hidden.shape
    pairs = weights.shape[0]
    depth = nrm.shape[2]
    lanes = weights.shape[-1]
    tile_rows = key_w.shape[0]
    blocks = 4
    block_rows = rows // blocks
    head_width = lanes // 2
    half_cols = pairs * lanes
    subs = 2 * pairs
    tok, mdl = lax.axis_index("tok"), lax.axis_index("mdl")
    chip, core = tok // 2, tok % 2
    other = 1 - core
    x_chip, y_chip, far_chip = chip + 1 - 2 * (chip % 2), (chip + 2) % 4, 3 - chip
    sibling = {"tok": chip * 2 + other, "mdl": mdl}
    x_dev = {"tok": x_chip * 2 + core, "mdl": mdl}
    y_dev = {"tok": y_chip * 2 + core, "mdl": mdl}
    remote = pltpu.make_async_remote_copy

    barrier = pltpu.get_barrier_semaphore()
    for device in (sibling, x_dev, y_dev):
        pl.semaphore_signal(barrier, inc=1, device_id=device)
    for side in (1, n_mdl - 1):
        pl.semaphore_signal(barrier, inc=1, device_id={"tok": tok, "mdl": (mdl + side) % n_mdl})

    own_hidden = pltpu.make_async_copy(hidden, hid.at[mdl], load_sem.at[0])
    own_hidden.start()
    own_out = pltpu.make_async_copy(out_w, wout.at[chip, core], load_sem.at[1])

    def columns(side, p):
        return pl.ds(pl.multiple_of(side * half_cols + p * lanes, lanes), lanes)

    projections = (key_w, value_w, query_w)
    own_tiles, swap_tiles = [], []
    for p in range(pairs):
        for m in range(3):
            number = 3 * p + m
            own_tiles.append(
                pltpu.make_async_copy(
                    projections[m].at[:, columns(core, p)],
                    weights.at[p, m, chip, core],
                    tile_sem.at[number],
                )
            )
            own_tiles[-1].start()
            swap_tiles.append(
                remote(
                    src_ref=projections[m].at[:, columns(other, p)],
                    dst_ref=weights.at[p, m, chip, core],
                    send_sem=ws_send.at[number], recv_sem=ws_recv.at[number], device_id=sibling,
                )
            )

    pl.semaphore_wait(barrier, 5)

    def copy(block, sends, recvs, index, device, target=None):
        return remote(
            src_ref=block, dst_ref=block if target is None else target,
            send_sem=sends.at[index], recv_sem=recvs.at[index], device_id=device,
        )

    def half_of(s):
        return (core + s) % 2

    def block_of(r):
        return pl.ds(r * block_rows, block_rows)

    def hidden_right(r, step):
        target = hid.at[mdl - step, block_of(r)]
        return copy(
            target if step else hidden.at[block_of(r)],
            hr_send, hr_recv, r * (n_mdl - 1) + step, {"tok": tok, "mdl": mdl + 1}, target,
        )

    def hidden_left(r, step):
        target = hid.at[mdl + step, block_of(r)]
        return copy(
            target if step else hidden.at[block_of(r)],
            hl_send, hl_recv, r * (n_mdl - 1) + step, {"tok": tok, "mdl": mdl - 1}, target,
        )

    def swap_normed(r):
        return copy(nrm.at[core, block_of(r)], ns_send, ns_recv, r, sibling)

    swap_turns = copy(cs.at[core], swap_send, swap_recv, 0, sibling)

    def weight_x(s):
        return copy(weights.at[s // 2, :, chip, half_of(s)], wx_send, wx_recv, s, x_dev)

    def weight_y(s):
        return copy(weights.at[s // 2, :, chip, half_of(s)], wy_send, wy_recv, s, y_dev)

    upper, lower = pl.ds(0, tile_rows // 2), pl.ds(tile_rows // 2, tile_rows // 2)

    def weight_relay_y(s):
        return copy(
            weights.at[s // 2, :, x_chip, half_of(s), upper], wr_send, wr_recv, s, y_dev
        )

    def weight_relay_x(s):
        return copy(
            weights.at[s // 2, :, y_chip, half_of(s), lower], wl_send, wl_recv, s, x_dev
        )

    def direct_x(s):
        return copy(kv.at[s // 2, chip, half_of(s)], dx_send, dx_recv, s, x_dev)

    def direct_y(s):
        return copy(kv.at[s // 2, chip, half_of(s)], dy_send, dy_recv, s, y_dev)

    def relay_k(s):
        return copy(kv.at[s // 2, x_chip, half_of(s), 0], rk_send, rk_recv, s, y_dev)

    def relay_v(s):
        return copy(kv.at[s // 2, y_chip, half_of(s), 1], rv_send, rv_recv, s, x_dev)

    def swap_att(p):
        return copy(att_send.at[p], as_send, as_recv, p, sibling, att.at[mdl, p, core])

    def z_index(p, step):
        return p * (n_mdl - 1) + step

    def z_right(p, step):
        return copy(
            att.at[mdl - step, p], zr_send, zr_recv, z_index(p, step), {"tok": tok, "mdl": mdl + 1}
        )

    def z_left(p, step):
        return copy(
            att.at[mdl + step, p], zl_send, zl_recv, z_index(p, step), {"tok": tok, "mdl": mdl - 1}
        )

    def line_start(right, left, index, step):
        @pl.when((mdl >= step) & (mdl < n_mdl - 1))
        def _():
            right(index, step).start()

        @pl.when((mdl + step < n_mdl) & (mdl > 0))
        def _():
            left(index, step).start()

    def line_arrive(right, left, index, step):
        @pl.when(mdl >= step + 1)
        def _():
            right(index, step).wait_recv()

        @pl.when(mdl + step + 1 < n_mdl)
        def _():
            left(index, step).wait_recv()

    def line_sent(right, left, index, step):
        @pl.when((mdl >= step) & (mdl < n_mdl - 1))
        def _():
            right(index, step).wait_send()

        @pl.when((mdl + step < n_mdl) & (mdl > 0))
        def _():
            left(index, step).wait_send()

    z_start = functools.partial(line_start, z_right, z_left)
    z_arrive = functools.partial(line_arrive, z_right, z_left)
    z_sent = functools.partial(line_sent, z_right, z_left)
    hidden_start = functools.partial(line_start, hidden_right, hidden_left)
    hidden_arrive = functools.partial(line_arrive, hidden_right, hidden_left)
    hidden_sent = functools.partial(line_sent, hidden_right, hidden_left)

    out_x = copy(out_w, ox_send, ox_recv, 0, x_dev, wout.at[chip, core])
    out_y = copy(out_w, oy_send, oy_recv, 0, y_dev, wout.at[chip, core])
    out_relay_y = copy(wout.at[x_chip, core, upper], ou_send, ou_recv, 0, y_dev)
    out_relay_x = copy(wout.at[y_chip, core, lower], ow_send, ow_recv, 0, x_dev)
    out_pass = [
        copy(out_w, op_send, op_recv, 0, sibling, wout.at[chip, core]),
        copy(wout.at[x_chip, core], op_send, op_recv, 1, sibling),
        copy(wout.at[y_chip, core], op_send, op_recv, 2, sibling),
        copy(wout.at[far_chip, core], op_send, op_recv, 3, sibling),
    ]

    for r in range(blocks):
        hidden_start(r, 0)

    def send_weights(s):
        if s % 2 == 0:
            for one in own_tiles[3 * (s // 2) : 3 * (s // 2) + 3]:
                one.wait()
        else:
            for one in swap_tiles[3 * (s // 2) : 3 * (s // 2) + 3]:
                one.wait_recv()
        weight_x(s).start()
        weight_y(s).start()

    for one in swap_tiles[:3]:
        one.start()
    send_weights(0)
    for one in swap_tiles[3:]:
        one.start()
    own_out.start()
    send_weights(1)

    def weight_event(s):
        weight_x(s).wait_recv()
        weight_y(s).wait_recv()
        weight_relay_y(s).start()
        weight_relay_x(s).start()
        if s + 2 < subs:
            send_weights(s + 2)

    lane = lax.broadcasted_iota(jnp.int32, (1, lanes), 1)
    first = lane < head_width
    early = lane % head_width < head_width // 2
    spot = lane % head_width
    bound = TEXT + lengths[0]

    def request_terms(start, count, same, differs):
        ids = start + lax.broadcasted_iota(jnp.int32, (count, lanes), 0)
        later = ids >= bound
        zero_side = jnp.where(later, differs, same)
        one_side = jnp.where(later, same, differs)
        return jnp.where(spot == 0, zero_side, jnp.where(spot == 1, one_side, 0.0))

    def bias_step(index, carry):
        kbias[index] = request_terms(index * rows, rows, 0.0, -16384.0).astype(jnp.bfloat16)
        return carry

    lax.fori_loop(0, total_rows // rows, bias_step, 0)

    def clear(p, carry):
        acc[p] = jnp.zeros(acc.shape[1:], jnp.float32)
        return carry

    lax.fori_loop(0, pairs, clear, 0)

    def wide_gain(gain):
        return jnp.concatenate([gain[...], gain[...]], axis=1)

    def head_mean(terms):
        one = jnp.sum(jnp.where(first, terms, 0.0), axis=1, keepdims=True)
        two = jnp.sum(jnp.where(first, 0.0, terms), axis=1, keepdims=True)
        return jnp.where(first, one, two) * (1.0 / head_width)

    def finished(summed, gain, half):
        center = summed - head_mean(summed)
        normal = center * lax.rsqrt(head_mean(center * center) + 1e-06) * gain
        partner = jnp.where(
            early,
            pltpu.roll(normal, lanes - head_width // 2, axis=1),
            pltpu.roll(normal, head_width // 2, axis=1),
        )
        return normal * cs[half, 0] + partner * cs[half, 1]

    quarter = head_width // 2
    pair = lane % quarter
    one_count = quarter // 4
    two_count = (quarter - one_count) // 2
    three_count = quarter - one_count - two_count
    is_one, is_two = pair < one_count, pair < one_count + two_count
    local = pair - jnp.where(is_one, 0, jnp.where(is_two, one_count, one_count + two_count))
    count = jnp.where(is_one, one_count, jnp.where(is_two, two_count, three_count))
    power = local.astype(jnp.float32) / count.astype(jnp.float32)
    rates = jnp.exp(power * -9.210340371976184)
    places = jnp.transpose(
        jnp.concatenate(
            [positions[...].astype(jnp.float32), jnp.zeros((5, rows), jnp.float32)], axis=0
        )
    )
    angles = rates * jnp.where(
        is_one, places[:, 0:1], jnp.where(is_two, places[:, 1:2], places[:, 2:3])
    )

    def textual(start, count):
        ids = tok * rows + start + lax.broadcasted_iota(jnp.int32, (count, 1), 0)
        place = jnp.where(ids >= bound, ids - bound, ids)
        return place < TEXT

    is_text = textual(0, rows)
    cs[core, 0] = jnp.where(is_text, 1.0, jnp.cos(angles))
    sine = jnp.sin(angles)
    cs[core, 1] = jnp.where(is_text, 0.0, jnp.where(early, -sine, sine))
    swap_turns.start()

    def normalize(r):
        wide = jnp.concatenate([hid[z, block_of(r), :] for z in range(n_mdl)], axis=1)
        values_in = wide.astype(jnp.float32)
        center = values_in - jnp.mean(values_in, axis=1, keepdims=True)
        spread = jnp.mean(center * center, axis=1, keepdims=True)
        normal = center * lax.rsqrt(spread + 1e-05)
        text_rows = textual(r * block_rows, block_rows)
        shift = jnp.where(text_rows, modulation[3:4, :], modulation[0:1, :])
        scale = jnp.where(text_rows, modulation[4:5, :], modulation[1:2, :])
        nrm[core, block_of(r), :] = (normal * (1.0 + scale) + shift).astype(jnp.bfloat16)
        swap_normed(r).start()

    def hidden_hop(r, step):
        hidden_arrive(r, step - 1)
        if step < n_mdl - 1:
            hidden_start(r, step)
        else:
            if r == 0:
                own_hidden.wait()
            normalize(r)

    hidden_hop(0, 1)
    weight_event(0)
    hidden_hop(1, 1)
    hidden_hop(2, 1)
    weight_event(1)
    hidden_hop(3, 1)
    hidden_hop(0, 2)
    weight_event(2)
    hidden_hop(1, 2)
    hidden_hop(2, 2)
    hidden_hop(3, 2)
    weight_event(3)
    hidden_hop(0, 3)
    hidden_hop(1, 3)
    weight_event(4)
    hidden_hop(2, 3)
    hidden_hop(3, 3)
    for s in range(4):
        weight_relay_y(s).wait_recv()
        weight_relay_x(s).wait_recv()

    def weight_of(p, m):
        return weights[p, m].reshape(depth, lanes)

    def project_pair(s, carry):
        p, half = s // 2, half_of(s)

        @pl.when(s == 1)
        def _():
            weight_event(subs - 1)
            for r in range(blocks):
                swap_normed(r).wait_recv()
            swap_turns.wait_recv()

        @pl.when(s == subs - 2)
        def _():
            for late in (subs - 2, subs - 1):
                weight_relay_y(late).wait_recv()
                weight_relay_x(late).wait_recv()

        summed = jnp.dot(
            nrm[half],
            jnp.concatenate([weight_of(p, 0), weight_of(p, 1)], axis=1),
            preferred_element_type=jnp.float32,
        )
        kv[p, chip, half, 0] = finished(summed[:, :lanes], wide_gain(key_gain), half).astype(jnp.bfloat16)
        kv[p, chip, half, 1] = summed[:, lanes:].astype(jnp.bfloat16)

        @pl.when(s < 2)
        def _():
            direct_x(s).start()
            direct_y(s).start()

        return carry

    lax.fori_loop(0, subs, project_pair, 0)

    def project_query(half, carry):
        where = pl.ds(pl.multiple_of(half * rows, rows), rows)
        terms = request_terms((chip * 2 + half) * rows, rows, 0.0, 1.0)
        terms = jnp.where(spot < 2, 1.0 - terms, 0.0)
        gain = wide_gain(query_gain) * (head_width ** (-0.5) * 1.4426950408889634)
        for start in range(0, pairs, 2):
            group = range(start, min(start + 2, pairs))
            summed = jnp.dot(
                nrm[half],
                jnp.concatenate([weight_of(p, 2) for p in group], axis=1),
                preferred_element_type=jnp.float32,
            )
            for part, p in enumerate(group):
                query = finished(summed[:, part * lanes : (part + 1) * lanes], gain, half)
                qx[2 * p, where, :] = jnp.where(first, query, terms).astype(jnp.bfloat16)
                qx[2 * p + 1, where, :] = jnp.where(first, terms, query).astype(jnp.bfloat16)
        return carry

    lax.fori_loop(0, 2, project_query, 0)

    most = TEXT + (total_rows - 2 * TEXT) * 5 // 8
    last_first = -(-most // rows)
    first_last = (total_rows - most) // rows

    def needed(row_block, key_block):
        return (
            ((row_block < first_last) & (key_block < last_first))
            | ((row_block >= last_first) & (key_block >= first_last))
            | ((row_block >= first_last) & (row_block < last_first))
        )

    def attend_rows(where, s, source):
        p, half = s // 2, half_of(s)
        keys, values = kv[p, source, half, 0], kv[p, source, half, 1]
        bias = kbias[source * 2 + half]
        ones = jnp.ones_like(values)
        for head in range(2):
            mine = first if head == 0 else jnp.logical_not(first)
            score = lax.dot_general(
                qx[2 * p + head, where, :],
                jnp.where(mine, keys, bias),
                (((1,), (1,)), ((), ())),
                preferred_element_type=jnp.float32,
            )
            expo = jnp.exp2(score).astype(jnp.bfloat16)
            acc[p, head, where, :] += jnp.dot(
                expo, jnp.where(mine, values, ones), preferred_element_type=jnp.float32
            )

    def attend_unit(s, source, valid):
        key_block = source * 2 + half_of(s)
        low, high = needed(chip * 2, key_block), needed(chip * 2 + 1, key_block)

        @pl.when(valid & low & high)
        def _():
            attend_rows(pl.ds(0, 2 * rows), s, source)

        @pl.when(valid & low & jnp.logical_not(high))
        def _():
            attend_rows(pl.ds(0, rows), s, source)

        @pl.when(valid & high & jnp.logical_not(low))
        def _():
            attend_rows(pl.ds(rows, rows), s, source)

    def finish_pair(p):
        def rows_of(index):
            where = pl.ds(pl.multiple_of(index * rows, rows), rows)
            one, two = acc[p, 0, where, :], acc[p, 1, where, :]
            summed = jnp.where(first, one, two)
            counted = pltpu.roll(jnp.where(first, two, one), head_width, axis=1)
            return (summed / counted).astype(jnp.bfloat16)

        att_send[p] = rows_of(other)
        swap_att(p).start()
        att[mdl, p, core] = rows_of(core)

    def turn(s, carry):
        def visit(j, inner):
            source = jnp.where(
                j == 0, chip, jnp.where(j == 1, x_chip, jnp.where(j == 2, y_chip, far_chip))
            )
            unit = jnp.where(j == 3, s - 1, s)
            valid = (unit >= 0) & (unit < subs)
            unit = jnp.where(valid, unit, 0)

            @pl.when((j == 0) & (s % 2 == 1) & (s >= 3))
            def _():
                p = (s - 3) // 2
                swap_att(p).wait_recv()
                z_start(p, 0)

            @pl.when((j == 1) & (s < subs))
            def _():
                direct_x(s).wait_recv()
                direct_y(s).wait_recv()
                relay_k(s).start()
                relay_v(s).start()

                @pl.when(s + 2 < subs)
                def _():
                    direct_x(s + 2).start()
                    direct_y(s + 2).start()

                @pl.when(s + 2 == subs)
                def _():
                    out_x.start()
                    out_y.start()
                    out_pass[0].start()

            @pl.when((j == 2) & (s % 2 == 0) & (s >= 4))
            def _():
                p = (s - 4) // 2
                z_arrive(p, 1)
                z_start(p, 2)

            @pl.when((j == 3) & (s % 2 == 1) & (s >= 3))
            def _():
                p = (s - 3) // 2
                z_arrive(p, 0)
                z_start(p, 1)

            @pl.when((j == 3) & (s >= 1))
            def _():
                relay_k(s - 1).wait_recv()
                relay_v(s - 1).wait_recv()

            attend_unit(unit, source, valid)

            @pl.when((j == 3) & (s % 2 == 0) & (s >= 2))
            def _():
                finish_pair((s - 2) // 2)

            return inner

        return lax.fori_loop(0, 4, visit, carry)

    lax.fori_loop(0, subs + 1, turn, 0)

    final = pairs - 1
    swap_att(final).wait_recv()
    z_start(final, 0)
    out_x.wait_recv()
    out_y.wait_recv()
    out_relay_y.start()
    out_relay_x.start()
    out_pass[1].start()
    out_pass[2].start()
    z_arrive(final, 0)
    z_start(final, 1)
    z_arrive(final, 1)
    z_start(final, 2)
    out_relay_y.wait_recv()
    out_relay_x.wait_recv()
    out_pass[3].start()
    own_out.wait()
    for one in out_pass:
        one.wait_recv()
    for p in range(pairs - 1):
        z_arrive(p, n_mdl - 2)

    def combine(p):
        tall = [
            wout[block, side, p * lanes : (p + 1) * lanes, :]
            for block in range(n_mdl)
            for side in range(2)
        ]
        wide = [att[block, p, side] for block in range(n_mdl) for side in range(2)]
        return jnp.dot(
            jnp.concatenate(wide, axis=1),
            jnp.concatenate(tall, axis=0),
            preferred_element_type=jnp.float32,
        )

    out_acc[...] = combine(0)
    for p in range(1, pairs - 1):
        out_acc[...] += combine(p)
    z_arrive(final, n_mdl - 2)
    projected = out_acc[...] + combine(final)
    own_columns = pl.ds(pl.multiple_of(mdl * width, lanes), width)
    gate = jnp.where(is_text, modulation[5:6, own_columns], modulation[2:3, own_columns])
    result[...] = (hid[mdl].astype(jnp.float32) + gate * projected).astype(jnp.bfloat16)

    swap_turns.wait_send()
    for r in range(blocks):
        swap_normed(r).wait_send()
        for step in range(n_mdl - 1):
            hidden_sent(r, step)
    for one in swap_tiles:
        one.wait_send()
    for s in range(subs):
        weight_x(s).wait_send()
        weight_y(s).wait_send()
        weight_relay_y(s).wait_send()
        weight_relay_x(s).wait_send()
        direct_x(s).wait_send()
        direct_y(s).wait_send()
        relay_k(s).wait_send()
        relay_v(s).wait_send()
    for p in range(pairs):
        swap_att(p).wait_send()
        for step in range(n_mdl - 1):
            z_sent(p, step)
    for one in [out_x, out_y, out_relay_y, out_relay_x] + out_pass:
        one.wait_send()


def fused(
    mesh, lengths, hidden, positions, modulation, weights, out_weight, gains, collective_id
):
    n_tok, n_mdl = mesh.shape["tok"], mesh.shape["mdl"]
    rows, width = hidden.shape
    depth = width * n_mdl
    lanes = 2 * gains[0].shape[1]
    pairs = width // (2 * lanes)
    total_rows = rows * n_tok
    chips = n_tok // 2
    subs = 2 * pairs
    blocks = 4
    bf, f32 = jnp.bfloat16, jnp.float32
    anywhere = pl.BlockSpec(memory_space=pl.ANY)
    inside = pl.BlockSpec(memory_space=pltpu.VMEM)

    def sems(count):
        return [pltpu.SemaphoreType.DMA((count,))]

    return pl.pallas_call(
        functools.partial(fused_kernel, n_mdl, total_rows),
        out_shape=jax.ShapeDtypeStruct((rows, width), bf),
        in_specs=[pl.BlockSpec(memory_space=pltpu.SMEM), anywhere]
        + [inside] * 2
        + [anywhere] * 4
        + [inside] * 2,
        out_specs=inside,
        scratch_shapes=[
            pltpu.VMEM((n_mdl, rows, width), bf),
            pltpu.VMEM((2, rows, depth), bf),
            pltpu.VMEM((2, 2, rows, lanes), f32),
            pltpu.VMEM((pairs, 3, chips, 2, out_weight.shape[0], lanes), bf),
            pltpu.VMEM((2 * pairs, 2 * rows, lanes), bf),
            pltpu.VMEM((pairs, chips, 2, 2, rows, lanes), bf),
            pltpu.VMEM((n_tok, rows, lanes), bf),
            pltpu.VMEM((pairs, 2, 2 * rows, lanes), f32),
            pltpu.VMEM((n_mdl, pairs, 2, rows, lanes), bf),
            pltpu.VMEM((pairs, rows, lanes), bf),
            pltpu.VMEM((chips, 2) + out_weight.shape, bf),
            pltpu.VMEM((rows, width), f32),
        ]
        + sems(2)
        + sems(3 * pairs)
        + sems(1) * 2
        + sems(blocks * (n_mdl - 1)) * 4
        + sems(blocks) * 2
        + sems(3 * pairs) * 2
        + sems(subs) * 8
        + sems(subs) * 8
        + sems(pairs) * 2
        + sems(pairs * (n_mdl - 1)) * 4
        + sems(1) * 8
        + sems(4) * 2,
        compiler_params=pltpu.CompilerParams(
            collective_id=collective_id, has_side_effects=True, vmem_limit_bytes=60 * 2**20
        ),
        name="fused",
    )(lengths, hidden, positions, modulation, *weights, out_weight, *gains)


def shards(
    mesh,
    hidden_states,
    lengths,
    positions,
    modulation,
    query_weight,
    key_weight,
    value_weight,
    out_weight,
    query_gain,
    key_gain,
):
    own_rows = hidden_states.shape[0]
    head_width = query_gain.shape[0]
    if mesh.shape["tok"] == 8 and mesh.shape["mdl"] == 4:
        return fused(
            mesh,
            lengths,
            hidden_states,
            positions,
            modulation,
            (key_weight, value_weight, query_weight),
            out_weight,
            [gain[None, :] for gain in (key_gain, query_gain)],
            0,
        )
    full_rows = lax.all_gather(hidden_states, "mdl", axis=1, tiled=True)
    key_full, value_full, query_full = gather_all(
        mesh, [key_weight, value_weight, query_weight], [], 0
    )
    row_index = lax.axis_index("tok") * own_rows + jnp.arange(own_rows, dtype=jnp.int32)
    request, is_text, bound = token_labels(row_index, lengths)
    normed = modulate(full_rows, modulation, is_text)
    angles = pair_angles(positions, head_width // 2)
    textual = is_text[:, None]
    cosine = jnp.tile(jnp.where(textual, 1.0, jnp.cos(angles)), (1, 4))
    sine = jnp.where(textual, 0.0, jnp.sin(angles))
    sine = jnp.tile(jnp.concatenate([-sine, sine], axis=1), (1, 2))
    keys, values, query_flat = project_and_gather(
        mesh,
        normed,
        (key_full, value_full, query_full),
        [jnp.tile(gain, 2)[None, :] for gain in (key_gain, query_gain)],
        cosine,
        sine,
        head_width,
        1,
    )
    first_row = lax.axis_index("tok") * own_rows
    first, second = (
        attend(query_flat, keys, values, bound, first_row, head_width, part, 2)
        for part in range(2)
    )
    first_heads = lax.all_gather(first, "mdl", axis=1, tiled=True)
    out_full, second_heads = gather_all(mesh, [out_weight], [second], 2)
    out_width = out_weight.shape[1]
    projected = jnp.concatenate(
        [
            jnp.dot(heads, out_full, preferred_element_type=jnp.float32)
            for heads in (first_heads, second_heads)
        ],
        axis=0,
    )
    gate_rows = lax.dynamic_slice_in_dim(
        modulation, lax.axis_index("mdl") * out_width, out_width, 1
    )
    gate = jnp.where(is_text[:, None], gate_rows[5][None, :], gate_rows[2][None, :])
    return (hidden_states.astype(jnp.float32) + gate * projected).astype(jnp.bfloat16)


def solution(mesh):
    return jax.shard_map(
        functools.partial(shards, mesh),
        mesh=mesh,
        in_specs=(
            P("tok", "mdl"),
            P(),
            P(None, "tok"),
            P(),
            P("tok", "mdl"),
            P("tok", "mdl"),
            P("tok", "mdl"),
            P("tok", "mdl"),
            P(),
            P(),
        ),
        out_specs=P("tok", "mdl"),
        check_vma=False,
    )
```

```python
import functools
import jax
import jax.numpy as jnp
from jax import lax
from jax.experimental import pallas as pl
from jax.experimental.pallas import tpu as pltpu
from jax.sharding import PartitionSpec as P

TEXT = 226


def token_labels(row_index, lengths):
    bound = TEXT + lengths[0]
    request = (row_index >= bound).astype(jnp.int32)
    place = row_index - request * bound
    return (request, place < TEXT, bound)


def modulate(rows_bf, modulation, is_text):
    values = rows_bf.astype(jnp.float32)
    center = values - jnp.mean(values, axis=1, keepdims=True)
    spread = jnp.mean(center * center, axis=1, keepdims=True)
    normal = center * lax.rsqrt(spread + 1e-05)
    textual = is_text[:, None]
    shift = jnp.where(textual, modulation[3][None, :], modulation[0][None, :])
    scale = jnp.where(textual, modulation[4][None, :], modulation[1][None, :])
    return (normal * (1.0 + scale) + shift).astype(jnp.bfloat16)


def pair_angles(positions, pairs):
    index = jnp.arange(pairs, dtype=jnp.int32)
    first = pairs // 4
    second = (pairs - first) // 2
    third = pairs - first - second
    component = jnp.where(index < first, 0, jnp.where(index < first + second, 1, 2))
    local = index - jnp.where(component == 0, 0, jnp.where(component == 1, first, first + second))
    count = jnp.where(component == 0, first, jnp.where(component == 1, second, third))
    rates = jnp.power(jnp.float32(10000.0), -local.astype(jnp.float32) / count.astype(jnp.float32))
    places = positions.astype(jnp.float32)
    chosen = jnp.where(
        component[:, None] == 0,
        places[0][None, :],
        jnp.where(component[:, None] == 1, places[1][None, :], places[2][None, :]),
    )
    return jnp.transpose(chosen * rates[:, None])


def gather_kernel(n_tok, n_mdl, n_row, n_col, *refs):
    count = n_row + n_col
    ins, outs = refs[:count], refs[count : 2 * count]
    exchange(
        n_tok, n_mdl, ins[:n_row], ins[n_row:], outs[:n_row], outs[n_row:], refs[2 * count :]
    )


def exchange(
    n_tok, n_mdl, rows_in, cols_in, rows_out, cols_out, semaphores, prepare=None, between=None
):
    n_row, n_col = len(rows_in), len(cols_in)
    (
        local_sem,
        send1,
        recv1,
        send2,
        recv2,
        send3,
        recv3,
        to_right,
        from_left,
        to_left,
        from_right,
    ) = semaphores
    square = n_tok == 8
    chips = n_tok // 2
    tok, mdl = lax.axis_index("tok"), lax.axis_index("mdl")
    chip, core = tok // 2, tok % 2
    sibling = chip * 2 + 1 - core

    def chip_at(step):
        if square:
            return (chip, chip + 1 - 2 * (chip % 2), (chip + 2) % 4, 3 - chip)[step]
        return (chip + step) % chips

    def source_at(step):
        return chip_at(step) if square else chip_at(chips - step)

    barrier = pltpu.get_barrier_semaphore()
    greeted = 0
    if n_row:
        for step in (1, 2) if square else range(1, chips):
            pl.semaphore_signal(
                barrier, inc=1, device_id={"tok": chip_at(step) * 2 + core, "mdl": mdl}
            )
            greeted += 1
        pl.semaphore_signal(barrier, inc=1, device_id={"tok": sibling, "mdl": mdl})
        greeted += 1
    if n_col:
        for side in (1, n_mdl - 1):
            pl.semaphore_signal(
                barrier, inc=1, device_id={"tok": tok, "mdl": (mdl + side) % n_mdl}
            )
            greeted += 1
    pl.semaphore_wait(barrier, greeted)

    def row_block(number, owner):
        size = rows_in[number].shape[0]
        return rows_out[number].at[pl.ds(pl.multiple_of(owner * size, size), size), :]

    def col_block(number, owner):
        size = cols_in[number].shape[1]
        return cols_out[number].at[:, pl.ds(pl.multiple_of(owner * size, size), size)]

    def direct(number, step):
        target = chip_at(step) * 2 + core if step else sibling
        return pltpu.make_async_remote_copy(
            src_ref=rows_in[number],
            dst_ref=row_block(number, tok),
            send_sem=send1.at[number, step],
            recv_sem=recv1.at[number, step],
            device_id={"tok": target, "mdl": mdl},
        )

    def passed(number, step):
        block = row_block(number, source_at(step) * 2 + core)
        return pltpu.make_async_remote_copy(
            src_ref=block,
            dst_ref=block,
            send_sem=send2.at[number, step],
            recv_sem=recv2.at[number, step],
            device_id={"tok": sibling, "mdl": mdl},
        )

    def relayed(number, step):
        half = rows_in[number].shape[0] // 2
        first = (source_at(step) * 2 + core) * 2 * half + (step - 1) * half
        block = rows_out[number].at[pl.ds(pl.multiple_of(first, half), half), :]
        return pltpu.make_async_remote_copy(
            src_ref=block,
            dst_ref=block,
            send_sem=send3.at[number, step],
            recv_sem=recv3.at[number, step],
            device_id={"tok": chip_at(3 - step) * 2 + core, "mdl": mdl},
        )

    directs = (1, 2) if square else range(1, chips)

    def rightward(number, step):
        block = col_block(number, mdl - step)
        return pltpu.make_async_remote_copy(
            src_ref=block if step else cols_in[number],
            dst_ref=block,
            send_sem=to_right.at[number, step],
            recv_sem=from_left.at[number, step],
            device_id={"tok": tok, "mdl": mdl + 1},
        )

    def leftward(number, step):
        block = col_block(number, mdl + step)
        return pltpu.make_async_remote_copy(
            src_ref=block if step else cols_in[number],
            dst_ref=block,
            send_sem=to_left.at[number, step],
            recv_sem=from_right.at[number, step],
            device_id={"tok": tok, "mdl": mdl - 1},
        )

    def right_if(step):
        return (mdl >= step) & (mdl < n_mdl - 1)

    def left_if(step):
        return (mdl + step < n_mdl) & (mdl > 0)

    for number in range(n_col):
        @pl.when(right_if(0))
        def _():
            rightward(number, 0).start()

        @pl.when(left_if(0))
        def _():
            leftward(number, 0).start()

    locals_ = []
    for number in range(n_col):
        locals_.append(
            pltpu.make_async_copy(
                cols_in[number], col_block(number, mdl), local_sem.at[n_row + number]
            )
        )
        locals_[-1].start()
    for number in range(n_row):
        if prepare is not None:
            prepare(number)
        for step in directs:
            direct(number, step).start()
        direct(number, 0).start()
        locals_.append(
            pltpu.make_async_copy(rows_in[number], row_block(number, tok), local_sem.at[number])
        )
        locals_[-1].start()

    def finish_diagonal(number):
        for step in (1, 2):
            relayed(number, step).wait_recv()
        passed(number, 3).start()

    for turn in range(max(n_row, n_mdl - 2 if n_col else 0)):
        hop = turn + 1
        if hop < n_mdl - 1:
            for number in range(n_col):
                @pl.when(mdl >= hop)
                def _():
                    rightward(number, hop - 1).wait_recv()

                @pl.when(right_if(hop))
                def _():
                    rightward(number, hop).start()

                @pl.when(mdl + hop < n_mdl)
                def _():
                    leftward(number, hop - 1).wait_recv()

                @pl.when(left_if(hop))
                def _():
                    leftward(number, hop).start()

        if turn < n_row:
            for step in directs:
                direct(turn, step).wait_recv()
                if square:
                    relayed(turn, step).start()
                passed(turn, step).start()
            if square and turn > 0:
                finish_diagonal(turn - 1)
        if between is not None:
            between(turn)

    if square and n_row:
        finish_diagonal(n_row - 1)
    for copy in locals_:
        copy.wait()
    for number in range(n_col):
        @pl.when(mdl >= n_mdl - 1)
        def _():
            rightward(number, n_mdl - 2).wait_recv()

        @pl.when(mdl + n_mdl - 1 < n_mdl)
        def _():
            leftward(number, n_mdl - 2).wait_recv()

    for number in range(n_row):
        direct(number, 0).wait()
        for step in directs:
            direct(number, step).wait_send()
            if square:
                relayed(number, step).wait_send()
        for step in range(1, chips):
            passed(number, step).wait()
    for number in range(n_col):
        for step in range(n_mdl - 1):
            @pl.when(right_if(step))
            def _():
                rightward(number, step).wait_send()

            @pl.when(left_if(step))
            def _():
                leftward(number, step).wait_send()


def exchange_semaphores(n_tok, n_mdl, n_row, n_col):
    row_sem = pltpu.SemaphoreType.DMA((max(n_row, 1), n_tok // 2))
    col_sem = pltpu.SemaphoreType.DMA((max(n_col, 1), n_mdl))
    return [pltpu.SemaphoreType.DMA((n_row + n_col,))] + [row_sem] * 6 + [col_sem] * 4


def project_kernel(n_tok, n_mdl, head_width, *refs):
    normed, key_w, value_w, query_w, key_gain, query_gain, cosine, sine = refs[:8]
    keys_out, values_out, query_out = refs[8:11]
    keys, values, query, key_held, value_held, query_held, load_sem = refs[11:18]
    width = keys.shape[1]
    lanes = 2 * head_width
    block = 256 if width % 256 == 0 else lanes
    loads = [
        pltpu.make_async_copy(source, held, load_sem.at[number])
        for number, (source, held) in enumerate(
            ((key_w, key_held), (value_w, value_held), (query_w, query_held))
        )
    ]
    for load in loads:
        load.start()
    lane = lax.broadcasted_iota(jnp.int32, (1, lanes), 1)
    first = lane < head_width
    early = lane % head_width < head_width // 2

    def head_mean(terms):
        one = jnp.sum(jnp.where(first, terms, 0.0), axis=1, keepdims=True)
        other = jnp.sum(jnp.where(first, 0.0, terms), axis=1, keepdims=True)
        return jnp.where(first, one, other) * (1.0 / head_width)

    def finished(summed, gain):
        center = summed - head_mean(summed)
        normal = center * lax.rsqrt(head_mean(center * center) + 1e-06) * gain[...]
        partner = jnp.where(
            early,
            pltpu.roll(normal, lanes - head_width // 2, axis=1),
            pltpu.roll(normal, head_width // 2, axis=1),
        )
        return normal * cosine[...] + partner * sine[...]

    def project(held, gain, target):
        def step(number, carry):
            columns = pl.ds(pl.multiple_of(number * block, block), block)
            summed = jnp.dot(
                normed[...], held[:, columns], preferred_element_type=jnp.float32
            )
            if gain is not None:
                summed = jnp.concatenate(
                    [
                        finished(summed[:, start : start + lanes], gain)
                        for start in range(0, block, lanes)
                    ],
                    axis=1,
                )
            target[:, columns] = summed.astype(jnp.bfloat16)
            return carry

        lax.fori_loop(0, width // block, step, 0)

    def prepare(number):
        loads[number].wait()
        if number == 0:
            project(key_held, key_gain, keys)
        else:
            project(value_held, None, values)

    query_copy = pltpu.make_async_copy(query, query_out, load_sem.at[3])

    def between(turn):
        if turn == 0:
            loads[2].wait()
            project(query_held, query_gain, query)
            query_copy.start()

    exchange(
        n_tok,
        n_mdl,
        (keys, values),
        (),
        (keys_out, values_out),
        (),
        refs[18:],
        prepare,
        between,
    )
    query_copy.wait()


def project_and_gather(mesh, normed, weights, gains, cosine, sine, head_width, collective_id):
    n_tok, n_mdl = mesh.shape["tok"], mesh.shape["mdl"]
    own_rows, depth = normed.shape
    width = weights[0].shape[1]
    full = jax.ShapeDtypeStruct((own_rows * n_tok, width), jnp.bfloat16)
    own = jax.ShapeDtypeStruct((own_rows, width), jnp.bfloat16)
    anywhere = pl.BlockSpec(memory_space=pl.ANY)
    inside = pl.BlockSpec(memory_space=pltpu.VMEM)
    return pl.pallas_call(
        functools.partial(project_kernel, n_tok, n_mdl, head_width),
        out_shape=[full, full, own],
        in_specs=[inside] + [anywhere] * 3 + [inside] * 4,
        out_specs=[anywhere] * 3,
        scratch_shapes=[pltpu.VMEM((own_rows, width), jnp.bfloat16)] * 3
        + [pltpu.VMEM((depth, width), jnp.bfloat16)] * 3
        + [pltpu.SemaphoreType.DMA((4,))]
        + exchange_semaphores(n_tok, n_mdl, 2, 0),
        compiler_params=pltpu.CompilerParams(
            collective_id=collective_id, has_side_effects=True, vmem_limit_bytes=48 * 2**20
        ),
        name="project_and_gather",
    )(normed, *weights, *gains, cosine, sine)


def gather_all(mesh, over_tok, over_mdl, collective_id):
    n_tok, n_mdl = mesh.shape["tok"], mesh.shape["mdl"]
    n_row, n_col = len(over_tok), len(over_mdl)
    shapes = [
        jax.ShapeDtypeStruct((one.shape[0] * n_tok, one.shape[1]), one.dtype) for one in over_tok
    ] + [jax.ShapeDtypeStruct((one.shape[0], one.shape[1] * n_mdl), one.dtype) for one in over_mdl]
    return pl.pallas_call(
        functools.partial(gather_kernel, n_tok, n_mdl, n_row, n_col),
        out_shape=shapes,
        in_specs=[pl.BlockSpec(memory_space=pl.ANY)] * (n_row + n_col),
        out_specs=[pl.BlockSpec(memory_space=pl.ANY)] * (n_row + n_col),
        scratch_shapes=exchange_semaphores(n_tok, n_mdl, n_row, n_col),
        compiler_params=pltpu.CompilerParams(collective_id=collective_id, has_side_effects=True),
        name=f"gather_{collective_id}",
    )(*over_tok, *over_mdl)


def attend_kernel(rows_at_once, keys_at_once, head_width, meta_ref, q_ref, k_ref, v_ref, o_ref):
    bound, first_row = meta_ref[0], meta_ref[1]
    own_rows, lanes = q_ref.shape
    count = k_ref.shape[0]
    chunks = count // keys_at_once
    per = lanes // head_width
    lane = lax.broadcasted_iota(jnp.int32, (1, lanes), 1) // head_width
    masks = [(lane == head).astype(jnp.float32) for head in range(per)]
    edge = bound // keys_at_once
    edge_start = pl.multiple_of(edge * keys_at_once, keys_at_once)
    edge_keys = edge_start + lax.broadcasted_iota(jnp.int32, (keys_at_once, 1), 0)

    for block in range(own_rows // rows_at_once):
        rows = pl.ds(block * rows_at_once, rows_at_once)
        start = first_row + block * rows_at_once
        row_ids = start + lax.broadcasted_iota(jnp.int32, (rows_at_once, 1), 0)

        def add_chunk(carry, keys, values):
            queries = q_ref[rows, :]
            result = []
            for head in range(per):
                mine = queries * (masks[head] * head_width ** (-0.5)).astype(jnp.bfloat16)
                score = lax.dot_general(
                    mine, keys, (((1,), (1,)), ((), ())), preferred_element_type=jnp.float32
                )
                expo = jnp.exp(score).astype(jnp.bfloat16)
                result.append(
                    carry[head]
                    + jnp.dot(expo, values[head], preferred_element_type=jnp.float32)
                )
            return tuple(result)

        def inner(chunk, carry):
            here = pl.ds(pl.multiple_of(chunk * keys_at_once, keys_at_once), keys_at_once)
            values = v_ref[here, :]
            with_ones = [
                values * mask.astype(jnp.bfloat16) + (1.0 - mask).astype(jnp.bfloat16)
                for mask in masks
            ]
            return add_chunk(carry, k_ref[here, :], with_ones)

        for request in range(2):
            active = start < bound if request == 0 else start + rows_at_once > bound

            @pl.when(active)
            def _():
                here = pl.ds(edge_start, keys_at_once)
                inside = edge_keys < bound if request == 0 else edge_keys >= bound
                wide = v_ref[here, :].astype(jnp.float32)
                with_ones = [
                    jnp.where(inside, wide * mask + (1.0 - mask), 0.0).astype(jnp.bfloat16)
                    for mask in masks
                ]
                zero = jnp.zeros((rows_at_once, lanes), jnp.float32)
                carry = add_chunk((zero,) * per, k_ref[here, :], with_ones)
                if request == 0:
                    low, high = 0, edge
                else:
                    low, high = edge + 1, chunks
                carry = lax.fori_loop(low, high, inner, carry)
                output = zero
                for head in range(per):
                    total = pltpu.roll(carry[head], head_width, axis=1)
                    output = jnp.where(lane == head, carry[head] / total, output)
                if request == 0:
                    o_ref[rows, :] = output.astype(o_ref.dtype)
                else:
                    old = o_ref[rows, :].astype(jnp.float32)
                    o_ref[rows, :] = jnp.where(row_ids >= bound, output, old).astype(o_ref.dtype)


def attend(query, keys, values, bound, first_row, head_width, part, parts):
    width = query.shape[1]
    own_rows = query.shape[0] // parts
    count = keys.shape[0]
    lanes = 2 * head_width
    meta = jnp.stack([bound, first_row + part * own_rows]).astype(jnp.int32)
    block = pl.BlockSpec((own_rows, lanes), lambda pair, meta: (part, pair))
    out_block = pl.BlockSpec((own_rows, lanes), lambda pair, meta: (0, pair))
    full = pl.BlockSpec((count, lanes), lambda pair, meta: (0, pair))
    return pl.pallas_call(
        functools.partial(attend_kernel, 256, 512, head_width),
        out_shape=jax.ShapeDtypeStruct((own_rows, width), jnp.bfloat16),
        grid_spec=pltpu.PrefetchScalarGridSpec(
            num_scalar_prefetch=1,
            grid=(width // lanes,),
            in_specs=[block, full, full],
            out_specs=out_block,
        ),
        compiler_params=pltpu.CompilerParams(vmem_limit_bytes=58 * 2**20),
        cost_estimate=pl.CostEstimate(
            flops=4 * own_rows * count * width,
            bytes_accessed=4 * count * width,
            transcendentals=own_rows * count * width // head_width,
        ),
        name=f"attend_{part}",
    )(meta, query, keys, values)

def fused_kernel(n_mdl, total_rows, *refs):
    (
        lengths, hidden, positions, modulation, key_w, value_w, query_w, out_w, key_gain, query_gain,
        result,
        hid, nrm, cs, weights, qx, kv, kbias, acc, att, att_send, att_in, wout, out_acc,
        load_sem, tile_sem, swap_send, swap_recv,
        hr_send, hr_recv, hl_send, hl_recv, ns_send, ns_recv, ws_send, ws_recv,
        wx_send, wx_recv, wy_send, wy_recv, wr_send, wr_recv, wl_send, wl_recv,
        dx_send, dx_recv, dy_send, dy_recv, rk_send, rk_recv, rv_send, rv_recv,
        as_send, as_recv, zr_send, zr_recv, zl_send, zl_recv,
        ox_send, ox_recv, oy_send, oy_recv, ou_send, ou_recv, op_send, op_recv,
    ) = refs
    rows, width = hidden.shape
    pairs = weights.shape[0]
    depth = nrm.shape[2]
    lanes = weights.shape[-1]
    tile_rows = key_w.shape[0]
    blocks = 4
    block_rows = rows // blocks
    head_width = lanes // 2
    half_cols = pairs * lanes
    subs = 2 * pairs
    tok, mdl = lax.axis_index("tok"), lax.axis_index("mdl")
    chip, core = tok // 2, tok % 2
    other = 1 - core
    x_chip, y_chip, far_chip = chip + 1 - 2 * (chip % 2), (chip + 2) % 4, 3 - chip
    sibling = {"tok": chip * 2 + other, "mdl": mdl}
    x_dev = {"tok": x_chip * 2 + core, "mdl": mdl}
    y_dev = {"tok": y_chip * 2 + core, "mdl": mdl}
    remote = pltpu.make_async_remote_copy

    barrier = pltpu.get_barrier_semaphore()
    for device in (sibling, x_dev, y_dev):
        pl.semaphore_signal(barrier, inc=1, device_id=device)
    for side in (1, n_mdl - 1):
        pl.semaphore_signal(barrier, inc=1, device_id={"tok": tok, "mdl": (mdl + side) % n_mdl})

    own_hidden = pltpu.make_async_copy(hidden, hid.at[mdl], load_sem.at[0])
    own_hidden.start()
    own_out = pltpu.make_async_copy(out_w, wout.at[chip, core], load_sem.at[1])

    def columns(side, p):
        return pl.ds(pl.multiple_of(side * half_cols + p * lanes, lanes), lanes)

    projections = (key_w, value_w, query_w)
    own_tiles, swap_tiles = [], []
    for p in range(pairs):
        for m in range(3):
            number = 3 * p + m
            own_tiles.append(
                pltpu.make_async_copy(
                    projections[m].at[:, columns(core, p)],
                    weights.at[p, m, chip, core],
                    tile_sem.at[number],
                )
            )
            own_tiles[-1].start()
            swap_tiles.append(
                remote(
                    src_ref=projections[m].at[:, columns(other, p)],
                    dst_ref=weights.at[p, m, chip, core],
                    send_sem=ws_send.at[number], recv_sem=ws_recv.at[number], device_id=sibling,
                )
            )

    pl.semaphore_wait(barrier, 5)

    def copy(block, sends, recvs, index, device, target=None):
        return remote(
            src_ref=block, dst_ref=block if target is None else target,
            send_sem=sends.at[index], recv_sem=recvs.at[index], device_id=device,
        )

    def half_of(s):
        return (core + s) % 2

    def block_of(r):
        return pl.ds(r * block_rows, block_rows)

    def hidden_right(r, step):
        target = hid.at[mdl - step, block_of(r)]
        return copy(
            target if step else hidden.at[block_of(r)],
            hr_send, hr_recv, r * (n_mdl - 1) + step, {"tok": tok, "mdl": mdl + 1}, target,
        )

    def hidden_left(r, step):
        target = hid.at[mdl + step, block_of(r)]
        return copy(
            target if step else hidden.at[block_of(r)],
            hl_send, hl_recv, r * (n_mdl - 1) + step, {"tok": tok, "mdl": mdl - 1}, target,
        )

    def swap_normed(r):
        return copy(nrm.at[core, block_of(r)], ns_send, ns_recv, r, sibling)

    swap_turns = copy(cs.at[core], swap_send, swap_recv, 0, sibling)

    def weight_x(s):
        return copy(weights.at[s // 2, :, chip, half_of(s)], wx_send, wx_recv, s, x_dev)

    def weight_y(s):
        return copy(weights.at[s // 2, :, chip, half_of(s)], wy_send, wy_recv, s, y_dev)

    upper, lower = pl.ds(0, tile_rows // 2), pl.ds(tile_rows // 2, tile_rows // 2)

    def weight_relay_y(s):
        return copy(
            weights.at[s // 2, :, x_chip, half_of(s), upper], wr_send, wr_recv, s, y_dev
        )

    def weight_relay_x(s):
        return copy(
            weights.at[s // 2, :, y_chip, half_of(s), lower], wl_send, wl_recv, s, x_dev
        )

    def direct_x(s):
        return copy(kv.at[s, chip], dx_send, dx_recv, s, x_dev)

    def direct_y(s):
        return copy(kv.at[s, chip], dy_send, dy_recv, s, y_dev)

    def relay_y(s):
        return copy(kv.at[s, x_chip, 0], rk_send, rk_recv, s, y_dev)

    def relay_x(s):
        return copy(kv.at[s, y_chip, 1], rv_send, rv_recv, s, x_dev)

    def swap_att(s):
        return copy(att_send.at[s], as_send, as_recv, s, sibling, att_in.at[s])

    def z_index(s, step):
        return s * (n_mdl - 1) + step

    def z_right(s, step):
        return copy(
            att.at[mdl - step, s], zr_send, zr_recv, z_index(s, step), {"tok": tok, "mdl": mdl + 1}
        )

    def z_left(s, step):
        return copy(
            att.at[mdl + step, s], zl_send, zl_recv, z_index(s, step), {"tok": tok, "mdl": mdl - 1}
        )

    def line_start(right, left, index, step):
        @pl.when((mdl >= step) & (mdl < n_mdl - 1))
        def _():
            right(index, step).start()

        @pl.when((mdl + step < n_mdl) & (mdl > 0))
        def _():
            left(index, step).start()

    def line_arrive(right, left, index, step):
        @pl.when(mdl >= step + 1)
        def _():
            right(index, step).wait_recv()

        @pl.when(mdl + step + 1 < n_mdl)
        def _():
            left(index, step).wait_recv()

    def line_sent(right, left, index, step):
        @pl.when((mdl >= step) & (mdl < n_mdl - 1))
        def _():
            right(index, step).wait_send()

        @pl.when((mdl + step < n_mdl) & (mdl > 0))
        def _():
            left(index, step).wait_send()

    z_start = functools.partial(line_start, z_right, z_left)
    z_arrive = functools.partial(line_arrive, z_right, z_left)
    z_sent = functools.partial(line_sent, z_right, z_left)
    hidden_start = functools.partial(line_start, hidden_right, hidden_left)
    hidden_arrive = functools.partial(line_arrive, hidden_right, hidden_left)
    hidden_sent = functools.partial(line_sent, hidden_right, hidden_left)

    pieces = 4
    piece_rows = tile_rows // pieces

    def piece(i):
        return pl.ds(i * piece_rows, piece_rows)

    out_x = [
        copy(out_w.at[piece(i)], ox_send, ox_recv, i, x_dev, wout.at[chip, core, piece(i)])
        for i in range(pieces)
    ]
    out_y = [
        copy(out_w.at[piece(i)], oy_send, oy_recv, i, y_dev, wout.at[chip, core, piece(i)])
        for i in range(pieces)
    ]
    out_relay = [
        copy(
            wout.at[x_chip if i < pieces // 2 else y_chip, core, piece(i)],
            ou_send, ou_recv, i, y_dev if i < pieces // 2 else x_dev,
        )
        for i in range(pieces)
    ]
    out_pass = [
        copy(out_w, op_send, op_recv, 0, sibling, wout.at[chip, core]),
        copy(wout.at[x_chip, core], op_send, op_recv, 1, sibling),
        copy(wout.at[y_chip, core], op_send, op_recv, 2, sibling),
        copy(wout.at[far_chip, core], op_send, op_recv, 3, sibling),
    ]

    for r in range(blocks):
        hidden_start(r, 0)

    def send_weights(s):
        if s % 2 == 0:
            for one in own_tiles[3 * (s // 2) : 3 * (s // 2) + 3]:
                one.wait()
        else:
            for one in swap_tiles[3 * (s // 2) : 3 * (s // 2) + 3]:
                one.wait_recv()
        weight_x(s).start()
        weight_y(s).start()

    for one in swap_tiles[:3]:
        one.start()
    send_weights(0)
    for one in swap_tiles[3:]:
        one.start()
    own_out.start()
    send_weights(1)

    def weight_event(s):
        weight_x(s).wait_recv()
        weight_y(s).wait_recv()
        weight_relay_y(s).start()
        weight_relay_x(s).start()
        if s + 2 < subs:
            send_weights(s + 2)

    lane = lax.broadcasted_iota(jnp.int32, (1, lanes), 1)
    first = lane < head_width
    early = lane % head_width < head_width // 2
    spot = lane % head_width
    bound = TEXT + lengths[0]

    def request_terms(start, count, same, differs):
        ids = start + lax.broadcasted_iota(jnp.int32, (count, lanes), 0)
        later = ids >= bound
        zero_side = jnp.where(later, differs, same)
        one_side = jnp.where(later, same, differs)
        return jnp.where(spot == 0, zero_side, jnp.where(spot == 1, one_side, 0.0))

    def bias_step(index, carry):
        kbias[index] = request_terms(index * rows, rows, 0.0, -16384.0).astype(jnp.bfloat16)
        return carry

    lax.fori_loop(0, total_rows // rows, bias_step, 0)

    def clear(s, carry):
        acc[s] = jnp.zeros(acc.shape[1:], jnp.float32)
        return carry

    lax.fori_loop(0, subs, clear, 0)

    def wide_gain(gain):
        return jnp.concatenate([gain[...], gain[...]], axis=1)

    def head_mean(terms):
        one = jnp.sum(jnp.where(first, terms, 0.0), axis=1, keepdims=True)
        two = jnp.sum(jnp.where(first, 0.0, terms), axis=1, keepdims=True)
        return jnp.where(first, one, two) * (1.0 / head_width)

    def finished(summed, gain, half):
        center = summed - head_mean(summed)
        normal = center * lax.rsqrt(head_mean(center * center) + 1e-06) * gain
        partner = jnp.where(
            early,
            pltpu.roll(normal, lanes - head_width // 2, axis=1),
            pltpu.roll(normal, head_width // 2, axis=1),
        )
        return normal * cs[half, 0] + partner * cs[half, 1]

    quarter = head_width // 2
    pair = lane % quarter
    one_count = quarter // 4
    two_count = (quarter - one_count) // 2
    three_count = quarter - one_count - two_count
    is_one, is_two = pair < one_count, pair < one_count + two_count
    local = pair - jnp.where(is_one, 0, jnp.where(is_two, one_count, one_count + two_count))
    count = jnp.where(is_one, one_count, jnp.where(is_two, two_count, three_count))
    power = local.astype(jnp.float32) / count.astype(jnp.float32)
    rates = jnp.exp(power * -9.210340371976184)
    places = jnp.transpose(
        jnp.concatenate(
            [positions[...].astype(jnp.float32), jnp.zeros((5, rows), jnp.float32)], axis=0
        )
    )
    angles = rates * jnp.where(
        is_one, places[:, 0:1], jnp.where(is_two, places[:, 1:2], places[:, 2:3])
    )

    def textual(start, count):
        ids = tok * rows + start + lax.broadcasted_iota(jnp.int32, (count, 1), 0)
        place = jnp.where(ids >= bound, ids - bound, ids)
        return place < TEXT

    is_text = textual(0, rows)
    cs[core, 0] = jnp.where(is_text, 1.0, jnp.cos(angles))
    sine = jnp.sin(angles)
    cs[core, 1] = jnp.where(is_text, 0.0, jnp.where(early, -sine, sine))
    swap_turns.start()

    def normalize(r):
        wide = jnp.concatenate([hid[z, block_of(r), :] for z in range(n_mdl)], axis=1)
        values_in = wide.astype(jnp.float32)
        center = values_in - jnp.mean(values_in, axis=1, keepdims=True)
        spread = jnp.mean(center * center, axis=1, keepdims=True)
        normal = center * lax.rsqrt(spread + 1e-05)
        text_rows = textual(r * block_rows, block_rows)
        shift = jnp.where(text_rows, modulation[3:4, :], modulation[0:1, :])
        scale = jnp.where(text_rows, modulation[4:5, :], modulation[1:2, :])
        nrm[core, block_of(r), :] = (normal * (1.0 + scale) + shift).astype(jnp.bfloat16)
        swap_normed(r).start()

    def hidden_hop(r, step):
        hidden_arrive(r, step - 1)
        if step < n_mdl - 1:
            hidden_start(r, step)
        else:
            if r == 0:
                own_hidden.wait()
            normalize(r)

    hidden_hop(0, 1)
    weight_event(0)
    hidden_hop(1, 1)
    hidden_hop(2, 1)
    weight_event(1)
    hidden_hop(3, 1)
    hidden_hop(0, 2)
    weight_event(2)
    hidden_hop(1, 2)
    hidden_hop(2, 2)
    hidden_hop(3, 2)
    weight_event(3)
    hidden_hop(0, 3)
    hidden_hop(1, 3)
    weight_event(4)
    hidden_hop(2, 3)
    hidden_hop(3, 3)
    for s in range(4):
        weight_relay_y(s).wait_recv()
        weight_relay_x(s).wait_recv()

    def weight_of(p, m):
        return weights[p, m].reshape(depth, lanes)

    def project_pair(s, carry):
        p, half = s // 2, half_of(s)

        @pl.when(s == 1)
        def _():
            weight_event(subs - 1)
            for r in range(blocks):
                swap_normed(r).wait_recv()
            swap_turns.wait_recv()

        @pl.when(s == subs - 2)
        def _():
            for late in (subs - 2, subs - 1):
                weight_relay_y(late).wait_recv()
                weight_relay_x(late).wait_recv()

        summed = jnp.dot(
            nrm[half],
            jnp.concatenate([weight_of(p, 0), weight_of(p, 1)], axis=1),
            preferred_element_type=jnp.float32,
        )
        keys = finished(summed[:, :lanes], wide_gain(key_gain), half)
        values = pltpu.roll(summed[:, lanes:], head_width, axis=1)
        kv[2 * p, chip, half] = jnp.where(first, keys, values).astype(jnp.bfloat16)
        kv[2 * p + 1, chip, half] = jnp.where(first, values, keys).astype(jnp.bfloat16)

        @pl.when(s == 1)
        def _():
            for ready in range(2):
                direct_x(ready).start()
                direct_y(ready).start()

        return carry

    lax.fori_loop(0, subs, project_pair, 0)

    def project_query(half, carry):
        where = pl.ds(pl.multiple_of(half * rows, rows), rows)
        terms = request_terms((chip * 2 + half) * rows, rows, 0.0, 1.0)
        terms = jnp.where(spot < 2, 1.0 - terms, 0.0)
        gain = wide_gain(query_gain) * (head_width ** (-0.5) * 1.4426950408889634)
        for start in range(0, pairs, 2):
            group = range(start, min(start + 2, pairs))
            summed = jnp.dot(
                nrm[half],
                jnp.concatenate([weight_of(p, 2) for p in group], axis=1),
                preferred_element_type=jnp.float32,
            )
            for part, p in enumerate(group):
                query = finished(summed[:, part * lanes : (part + 1) * lanes], gain, half)
                qx[2 * p, where, :] = jnp.where(first, query, terms).astype(jnp.bfloat16)
                qx[2 * p + 1, where, :] = jnp.where(first, terms, query).astype(jnp.bfloat16)
        return carry

    lax.fori_loop(0, 2, project_query, 0)

    most = TEXT + (total_rows - 2 * TEXT) * 5 // 8
    last_first = -(-most // rows)
    first_last = (total_rows - most) // rows

    def needed(row_block, key_block):
        return (
            ((row_block < first_last) & (key_block < last_first))
            | ((row_block >= last_first) & (key_block >= first_last))
            | ((row_block >= first_last) & (row_block < last_first))
        )

    def attend_rows(where, s, source, halves):
        mine = (lane + (s % 2) * head_width) % lanes < head_width
        added = None
        for half in halves:
            block = kv[s, source, half]
            score = lax.dot_general(
                qx[s, where, :],
                jnp.where(mine, block, kbias[source * 2 + half]),
                (((1,), (1,)), ((), ())),
                preferred_element_type=jnp.float32,
            )
            part = jnp.dot(
                jnp.exp2(score).astype(jnp.bfloat16),
                jnp.where(mine, jnp.ones_like(block), block),
                preferred_element_type=jnp.float32,
            )
            added = part if added is None else added + part
        acc[s, where, :] += added

    def attend_unit(s, source, valid):
        row_block, key_block = chip * 2, source * 2
        whole = (
            needed(row_block, key_block)
            & needed(row_block, key_block + 1)
            & needed(row_block + 1, key_block)
            & needed(row_block + 1, key_block + 1)
        )

        @pl.when(valid & whole)
        def _():
            attend_rows(pl.ds(0, 2 * rows), s, source, (0, 1))

        @pl.when(valid & jnp.logical_not(whole))
        def _():
            def quarter_unit(number, inner):
                r, half = number // 2, number % 2

                @pl.when(needed(row_block + r, key_block + half))
                def _():
                    attend_rows(
                        pl.ds(pl.multiple_of(r * rows, rows), rows), s, source, (half,)
                    )

                return inner

            lax.fori_loop(0, 4, quarter_unit, 0)

    def finish_head(s):
        moved = (s + 1) % 2 != core

        def rows_of(index):
            where = pl.ds(pl.multiple_of(index * rows, rows), rows)
            both = acc[s, where, :]
            ratio = both / pltpu.roll(both, head_width, axis=1)
            return jnp.where(moved, pltpu.roll(ratio, head_width, axis=1), ratio).astype(
                jnp.bfloat16
            )

        att_send[s] = rows_of(other)
        swap_att(s).start()
        att[mdl, s] = rows_of(core)

    def share_head(s):
        swap_att(s).wait_recv()
        att[mdl, s] = jnp.where(lane // head_width == core, att[mdl, s], att_in[s])
        z_start(s, 0)

    def pass_on(s, step):
        z_arrive(s, step - 1)
        z_start(s, step)

    def turn(s, carry):
        def visit(j, inner):
            source = jnp.where(
                j == 0, chip, jnp.where(j == 1, x_chip, jnp.where(j == 2, y_chip, far_chip))
            )
            unit = jnp.where(j == 3, s - 1, s)
            valid = (unit >= 0) & (unit < subs)
            unit = jnp.where(valid, unit, 0)

            @pl.when((j == 0) & (s >= 2))
            def _():
                share_head(s - 2)

            @pl.when((s < subs) & (((j == 1) & (s > 0)) | ((j == 0) & (s == 0))))
            def _():
                direct_x(s).wait_recv()
                direct_y(s).wait_recv()
                relay_y(s).start()
                relay_x(s).start()

                @pl.when(s + 2 < subs)
                def _():
                    direct_x(s + 2).start()
                    direct_y(s + 2).start()

                @pl.when(s + 2 == subs)
                def _():
                    out_x[0].start()
                    out_y[0].start()
                    out_pass[0].start()

                @pl.when(s + 1 == subs)
                def _():
                    for i in range(1, pieces):
                        out_x[i].start()
                        out_y[i].start()

            @pl.when((j == 2) & (s >= 3))
            def _():
                pass_on(s - 3, 2)

            @pl.when((j == 3) & (s >= 2))
            def _():
                pass_on(s - 2, 1)

            @pl.when((j == 3) & (s >= 1))
            def _():
                relay_y(s - 1).wait_recv()
                relay_x(s - 1).wait_recv()

            attend_unit(unit, source, valid)

            @pl.when((j == 3) & (s >= 1))
            def _():
                finish_head(s - 1)

            return inner

        return lax.fori_loop(0, 4, visit, carry)

    lax.fori_loop(0, subs + 1, turn, 0)

    def out_event(i):
        out_x[i].wait_recv()
        out_y[i].wait_recv()
        out_relay[i].start()

    final = subs - 1
    share_head(final)
    out_event(0)
    pass_on(final - 1, 2)
    out_event(1)
    pass_on(final, 1)
    out_event(2)
    pass_on(final, 2)
    out_event(3)
    out_pass[1].start()
    out_pass[2].start()
    own_out.wait()

    def combine(block):
        tall = [
            wout[block, side, s * head_width : (s + 1) * head_width, :]
            for s in range(subs)
            for side in range(2)
        ]
        return jnp.dot(
            jnp.concatenate([att[block, s] for s in range(subs)], axis=1),
            jnp.concatenate(tall, axis=0),
            preferred_element_type=jnp.float32,
        )

    for s in range(subs):
        z_arrive(s, n_mdl - 2)
    out_pass[0].wait_recv()
    out_acc[...] = combine(chip)
    out_pass[1].wait_recv()
    out_acc[...] += combine(x_chip)
    out_pass[2].wait_recv()
    out_acc[...] += combine(y_chip)
    for one in out_relay:
        one.wait_recv()
    out_pass[3].start()
    out_pass[3].wait_recv()
    projected = out_acc[...] + combine(far_chip)
    own_columns = pl.ds(pl.multiple_of(mdl * width, lanes), width)
    gate = jnp.where(is_text, modulation[5:6, own_columns], modulation[2:3, own_columns])
    result[...] = (hid[mdl].astype(jnp.float32) + gate * projected).astype(jnp.bfloat16)

    swap_turns.wait_send()
    for r in range(blocks):
        swap_normed(r).wait_send()
        for step in range(n_mdl - 1):
            hidden_sent(r, step)
    for one in swap_tiles:
        one.wait_send()
    for s in range(subs):
        weight_x(s).wait_send()
        weight_y(s).wait_send()
        weight_relay_y(s).wait_send()
        weight_relay_x(s).wait_send()
        direct_x(s).wait_send()
        direct_y(s).wait_send()
        relay_y(s).wait_send()
        relay_x(s).wait_send()
        swap_att(s).wait_send()
        for step in range(n_mdl - 1):
            z_sent(s, step)
    for one in out_x + out_y + out_relay + out_pass:
        one.wait_send()


def fused(
    mesh, lengths, hidden, positions, modulation, weights, out_weight, gains, collective_id
):
    n_tok, n_mdl = mesh.shape["tok"], mesh.shape["mdl"]
    rows, width = hidden.shape
    depth = width * n_mdl
    lanes = 2 * gains[0].shape[1]
    pairs = width // (2 * lanes)
    total_rows = rows * n_tok
    chips = n_tok // 2
    subs = 2 * pairs
    blocks = 4
    bf, f32 = jnp.bfloat16, jnp.float32
    anywhere = pl.BlockSpec(memory_space=pl.ANY)
    inside = pl.BlockSpec(memory_space=pltpu.VMEM)

    def sems(count):
        return [pltpu.SemaphoreType.DMA((count,))]

    return pl.pallas_call(
        functools.partial(fused_kernel, n_mdl, total_rows),
        out_shape=jax.ShapeDtypeStruct((rows, width), bf),
        in_specs=[pl.BlockSpec(memory_space=pltpu.SMEM), anywhere]
        + [inside] * 2
        + [anywhere] * 4
        + [inside] * 2,
        out_specs=inside,
        scratch_shapes=[
            pltpu.VMEM((n_mdl, rows, width), bf),
            pltpu.VMEM((2, rows, depth), bf),
            pltpu.VMEM((2, 2, rows, lanes), f32),
            pltpu.VMEM((pairs, 3, chips, 2, out_weight.shape[0], lanes), bf),
            pltpu.VMEM((2 * pairs, 2 * rows, lanes), bf),
            pltpu.VMEM((subs, chips, 2, rows, lanes), bf),
            pltpu.VMEM((n_tok, rows, lanes), bf),
            pltpu.VMEM((subs, 2 * rows, lanes), f32),
            pltpu.VMEM((n_mdl, subs, rows, lanes), bf),
            pltpu.VMEM((subs, rows, lanes), bf),
            pltpu.VMEM((subs, rows, lanes), bf),
            pltpu.VMEM((chips, 2) + out_weight.shape, bf),
            pltpu.VMEM((rows, width), f32),
        ]
        + sems(2)
        + sems(3 * pairs)
        + sems(1) * 2
        + sems(blocks * (n_mdl - 1)) * 4
        + sems(blocks) * 2
        + sems(3 * pairs) * 2
        + sems(subs) * 8
        + sems(subs) * 8
        + sems(subs) * 2
        + sems(subs * (n_mdl - 1)) * 4
        + sems(4) * 8,
        compiler_params=pltpu.CompilerParams(
            collective_id=collective_id, has_side_effects=True, vmem_limit_bytes=60 * 2**20
        ),
        name="fused",
    )(lengths, hidden, positions, modulation, *weights, out_weight, *gains)


def shards(
    mesh,
    hidden_states,
    lengths,
    positions,
    modulation,
    query_weight,
    key_weight,
    value_weight,
    out_weight,
    query_gain,
    key_gain,
):
    own_rows = hidden_states.shape[0]
    head_width = query_gain.shape[0]
    if mesh.shape["tok"] == 8 and mesh.shape["mdl"] == 4:
        return fused(
            mesh,
            lengths,
            hidden_states,
            positions,
            modulation,
            (key_weight, value_weight, query_weight),
            out_weight,
            [gain[None, :] for gain in (key_gain, query_gain)],
            0,
        )
    full_rows = lax.all_gather(hidden_states, "mdl", axis=1, tiled=True)
    key_full, value_full, query_full = gather_all(
        mesh, [key_weight, value_weight, query_weight], [], 0
    )
    row_index = lax.axis_index("tok") * own_rows + jnp.arange(own_rows, dtype=jnp.int32)
    request, is_text, bound = token_labels(row_index, lengths)
    normed = modulate(full_rows, modulation, is_text)
    angles = pair_angles(positions, head_width // 2)
    textual = is_text[:, None]
    cosine = jnp.tile(jnp.where(textual, 1.0, jnp.cos(angles)), (1, 4))
    sine = jnp.where(textual, 0.0, jnp.sin(angles))
    sine = jnp.tile(jnp.concatenate([-sine, sine], axis=1), (1, 2))
    keys, values, query_flat = project_and_gather(
        mesh,
        normed,
        (key_full, value_full, query_full),
        [jnp.tile(gain, 2)[None, :] for gain in (key_gain, query_gain)],
        cosine,
        sine,
        head_width,
        1,
    )
    first_row = lax.axis_index("tok") * own_rows
    first, second = (
        attend(query_flat, keys, values, bound, first_row, head_width, part, 2)
        for part in range(2)
    )
    first_heads = lax.all_gather(first, "mdl", axis=1, tiled=True)
    out_full, second_heads = gather_all(mesh, [out_weight], [second], 2)
    out_width = out_weight.shape[1]
    projected = jnp.concatenate(
        [
            jnp.dot(heads, out_full, preferred_element_type=jnp.float32)
            for heads in (first_heads, second_heads)
        ],
        axis=0,
    )
    gate_rows = lax.dynamic_slice_in_dim(
        modulation, lax.axis_index("mdl") * out_width, out_width, 1
    )
    gate = jnp.where(is_text[:, None], gate_rows[5][None, :], gate_rows[2][None, :])
    return (hidden_states.astype(jnp.float32) + gate * projected).astype(jnp.bfloat16)


def solution(mesh):
    return jax.shard_map(
        functools.partial(shards, mesh),
        mesh=mesh,
        in_specs=(
            P("tok", "mdl"),
            P(),
            P(None, "tok"),
            P(),
            P("tok", "mdl"),
            P("tok", "mdl"),
            P("tok", "mdl"),
            P("tok", "mdl"),
            P(),
            P(),
        ),
        out_specs=P("tok", "mdl"),
        check_vma=False,
    )
```

```python
import functools
import jax
import jax.numpy as jnp
from jax import lax
from jax.experimental import pallas as pl
from jax.experimental.pallas import tpu as pltpu
from jax.sharding import PartitionSpec as P

TEXT = 226


def token_labels(row_index, lengths):
    bound = TEXT + lengths[0]
    request = (row_index >= bound).astype(jnp.int32)
    place = row_index - request * bound
    return (request, place < TEXT, bound)


def modulate(rows_bf, modulation, is_text):
    values = rows_bf.astype(jnp.float32)
    center = values - jnp.mean(values, axis=1, keepdims=True)
    spread = jnp.mean(center * center, axis=1, keepdims=True)
    normal = center * lax.rsqrt(spread + 1e-05)
    textual = is_text[:, None]
    shift = jnp.where(textual, modulation[3][None, :], modulation[0][None, :])
    scale = jnp.where(textual, modulation[4][None, :], modulation[1][None, :])
    return (normal * (1.0 + scale) + shift).astype(jnp.bfloat16)


def pair_angles(positions, pairs):
    index = jnp.arange(pairs, dtype=jnp.int32)
    first = pairs // 4
    second = (pairs - first) // 2
    third = pairs - first - second
    component = jnp.where(index < first, 0, jnp.where(index < first + second, 1, 2))
    local = index - jnp.where(component == 0, 0, jnp.where(component == 1, first, first + second))
    count = jnp.where(component == 0, first, jnp.where(component == 1, second, third))
    rates = jnp.power(jnp.float32(10000.0), -local.astype(jnp.float32) / count.astype(jnp.float32))
    places = positions.astype(jnp.float32)
    chosen = jnp.where(
        component[:, None] == 0,
        places[0][None, :],
        jnp.where(component[:, None] == 1, places[1][None, :], places[2][None, :]),
    )
    return jnp.transpose(chosen * rates[:, None])


def gather_kernel(n_tok, n_mdl, n_row, n_col, *refs):
    count = n_row + n_col
    ins, outs = refs[:count], refs[count : 2 * count]
    exchange(
        n_tok, n_mdl, ins[:n_row], ins[n_row:], outs[:n_row], outs[n_row:], refs[2 * count :]
    )


def exchange(
    n_tok, n_mdl, rows_in, cols_in, rows_out, cols_out, semaphores, prepare=None, between=None
):
    n_row, n_col = len(rows_in), len(cols_in)
    (
        local_sem,
        send1,
        recv1,
        send2,
        recv2,
        send3,
        recv3,
        to_right,
        from_left,
        to_left,
        from_right,
    ) = semaphores
    square = n_tok == 8
    chips = n_tok // 2
    tok, mdl = lax.axis_index("tok"), lax.axis_index("mdl")
    chip, core = tok // 2, tok % 2
    sibling = chip * 2 + 1 - core

    def chip_at(step):
        if square:
            return (chip, chip + 1 - 2 * (chip % 2), (chip + 2) % 4, 3 - chip)[step]
        return (chip + step) % chips

    def source_at(step):
        return chip_at(step) if square else chip_at(chips - step)

    barrier = pltpu.get_barrier_semaphore()
    greeted = 0
    if n_row:
        for step in (1, 2) if square else range(1, chips):
            pl.semaphore_signal(
                barrier, inc=1, device_id={"tok": chip_at(step) * 2 + core, "mdl": mdl}
            )
            greeted += 1
        pl.semaphore_signal(barrier, inc=1, device_id={"tok": sibling, "mdl": mdl})
        greeted += 1
    if n_col:
        for side in (1, n_mdl - 1):
            pl.semaphore_signal(
                barrier, inc=1, device_id={"tok": tok, "mdl": (mdl + side) % n_mdl}
            )
            greeted += 1
    pl.semaphore_wait(barrier, greeted)

    def row_block(number, owner):
        size = rows_in[number].shape[0]
        return rows_out[number].at[pl.ds(pl.multiple_of(owner * size, size), size), :]

    def col_block(number, owner):
        size = cols_in[number].shape[1]
        return cols_out[number].at[:, pl.ds(pl.multiple_of(owner * size, size), size)]

    def direct(number, step):
        target = chip_at(step) * 2 + core if step else sibling
        return pltpu.make_async_remote_copy(
            src_ref=rows_in[number],
            dst_ref=row_block(number, tok),
            send_sem=send1.at[number, step],
            recv_sem=recv1.at[number, step],
            device_id={"tok": target, "mdl": mdl},
        )

    def passed(number, step):
        block = row_block(number, source_at(step) * 2 + core)
        return pltpu.make_async_remote_copy(
            src_ref=block,
            dst_ref=block,
            send_sem=send2.at[number, step],
            recv_sem=recv2.at[number, step],
            device_id={"tok": sibling, "mdl": mdl},
        )

    def relayed(number, step):
        half = rows_in[number].shape[0] // 2
        first = (source_at(step) * 2 + core) * 2 * half + (step - 1) * half
        block = rows_out[number].at[pl.ds(pl.multiple_of(first, half), half), :]
        return pltpu.make_async_remote_copy(
            src_ref=block,
            dst_ref=block,
            send_sem=send3.at[number, step],
            recv_sem=recv3.at[number, step],
            device_id={"tok": chip_at(3 - step) * 2 + core, "mdl": mdl},
        )

    directs = (1, 2) if square else range(1, chips)

    def rightward(number, step):
        block = col_block(number, mdl - step)
        return pltpu.make_async_remote_copy(
            src_ref=block if step else cols_in[number],
            dst_ref=block,
            send_sem=to_right.at[number, step],
            recv_sem=from_left.at[number, step],
            device_id={"tok": tok, "mdl": mdl + 1},
        )

    def leftward(number, step):
        block = col_block(number, mdl + step)
        return pltpu.make_async_remote_copy(
            src_ref=block if step else cols_in[number],
            dst_ref=block,
            send_sem=to_left.at[number, step],
            recv_sem=from_right.at[number, step],
            device_id={"tok": tok, "mdl": mdl - 1},
        )

    def right_if(step):
        return (mdl >= step) & (mdl < n_mdl - 1)

    def left_if(step):
        return (mdl + step < n_mdl) & (mdl > 0)

    for number in range(n_col):
        @pl.when(right_if(0))
        def _():
            rightward(number, 0).start()

        @pl.when(left_if(0))
        def _():
            leftward(number, 0).start()

    locals_ = []
    for number in range(n_col):
        locals_.append(
            pltpu.make_async_copy(
                cols_in[number], col_block(number, mdl), local_sem.at[n_row + number]
            )
        )
        locals_[-1].start()
    for number in range(n_row):
        if prepare is not None:
            prepare(number)
        for step in directs:
            direct(number, step).start()
        direct(number, 0).start()
        locals_.append(
            pltpu.make_async_copy(rows_in[number], row_block(number, tok), local_sem.at[number])
        )
        locals_[-1].start()

    def finish_diagonal(number):
        for step in (1, 2):
            relayed(number, step).wait_recv()
        passed(number, 3).start()

    for turn in range(max(n_row, n_mdl - 2 if n_col else 0)):
        hop = turn + 1
        if hop < n_mdl - 1:
            for number in range(n_col):
                @pl.when(mdl >= hop)
                def _():
                    rightward(number, hop - 1).wait_recv()

                @pl.when(right_if(hop))
                def _():
                    rightward(number, hop).start()

                @pl.when(mdl + hop < n_mdl)
                def _():
                    leftward(number, hop - 1).wait_recv()

                @pl.when(left_if(hop))
                def _():
                    leftward(number, hop).start()

        if turn < n_row:
            for step in directs:
                direct(turn, step).wait_recv()
                if square:
                    relayed(turn, step).start()
                passed(turn, step).start()
            if square and turn > 0:
                finish_diagonal(turn - 1)
        if between is not None:
            between(turn)

    if square and n_row:
        finish_diagonal(n_row - 1)
    for copy in locals_:
        copy.wait()
    for number in range(n_col):
        @pl.when(mdl >= n_mdl - 1)
        def _():
            rightward(number, n_mdl - 2).wait_recv()

        @pl.when(mdl + n_mdl - 1 < n_mdl)
        def _():
            leftward(number, n_mdl - 2).wait_recv()

    for number in range(n_row):
        direct(number, 0).wait()
        for step in directs:
            direct(number, step).wait_send()
            if square:
                relayed(number, step).wait_send()
        for step in range(1, chips):
            passed(number, step).wait()
    for number in range(n_col):
        for step in range(n_mdl - 1):
            @pl.when(right_if(step))
            def _():
                rightward(number, step).wait_send()

            @pl.when(left_if(step))
            def _():
                leftward(number, step).wait_send()


def exchange_semaphores(n_tok, n_mdl, n_row, n_col):
    row_sem = pltpu.SemaphoreType.DMA((max(n_row, 1), n_tok // 2))
    col_sem = pltpu.SemaphoreType.DMA((max(n_col, 1), n_mdl))
    return [pltpu.SemaphoreType.DMA((n_row + n_col,))] + [row_sem] * 6 + [col_sem] * 4


def project_kernel(n_tok, n_mdl, head_width, *refs):
    normed, key_w, value_w, query_w, key_gain, query_gain, cosine, sine = refs[:8]
    keys_out, values_out, query_out = refs[8:11]
    keys, values, query, key_held, value_held, query_held, load_sem = refs[11:18]
    width = keys.shape[1]
    lanes = 2 * head_width
    block = 256 if width % 256 == 0 else lanes
    loads = [
        pltpu.make_async_copy(source, held, load_sem.at[number])
        for number, (source, held) in enumerate(
            ((key_w, key_held), (value_w, value_held), (query_w, query_held))
        )
    ]
    for load in loads:
        load.start()
    lane = lax.broadcasted_iota(jnp.int32, (1, lanes), 1)
    first = lane < head_width
    early = lane % head_width < head_width // 2

    def head_mean(terms):
        one = jnp.sum(jnp.where(first, terms, 0.0), axis=1, keepdims=True)
        other = jnp.sum(jnp.where(first, 0.0, terms), axis=1, keepdims=True)
        return jnp.where(first, one, other) * (1.0 / head_width)

    def finished(summed, gain):
        center = summed - head_mean(summed)
        normal = center * lax.rsqrt(head_mean(center * center) + 1e-06) * gain[...]
        partner = jnp.where(
            early,
            pltpu.roll(normal, lanes - head_width // 2, axis=1),
            pltpu.roll(normal, head_width // 2, axis=1),
        )
        return normal * cosine[...] + partner * sine[...]

    def project(held, gain, target):
        def step(number, carry):
            columns = pl.ds(pl.multiple_of(number * block, block), block)
            summed = jnp.dot(
                normed[...], held[:, columns], preferred_element_type=jnp.float32
            )
            if gain is not None:
                summed = jnp.concatenate(
                    [
                        finished(summed[:, start : start + lanes], gain)
                        for start in range(0, block, lanes)
                    ],
                    axis=1,
                )
            target[:, columns] = summed.astype(jnp.bfloat16)
            return carry

        lax.fori_loop(0, width // block, step, 0)

    def prepare(number):
        loads[number].wait()
        if number == 0:
            project(key_held, key_gain, keys)
        else:
            project(value_held, None, values)

    query_copy = pltpu.make_async_copy(query, query_out, load_sem.at[3])

    def between(turn):
        if turn == 0:
            loads[2].wait()
            project(query_held, query_gain, query)
            query_copy.start()

    exchange(
        n_tok,
        n_mdl,
        (keys, values),
        (),
        (keys_out, values_out),
        (),
        refs[18:],
        prepare,
        between,
    )
    query_copy.wait()


def project_and_gather(mesh, normed, weights, gains, cosine, sine, head_width, collective_id):
    n_tok, n_mdl = mesh.shape["tok"], mesh.shape["mdl"]
    own_rows, depth = normed.shape
    width = weights[0].shape[1]
    full = jax.ShapeDtypeStruct((own_rows * n_tok, width), jnp.bfloat16)
    own = jax.ShapeDtypeStruct((own_rows, width), jnp.bfloat16)
    anywhere = pl.BlockSpec(memory_space=pl.ANY)
    inside = pl.BlockSpec(memory_space=pltpu.VMEM)
    return pl.pallas_call(
        functools.partial(project_kernel, n_tok, n_mdl, head_width),
        out_shape=[full, full, own],
        in_specs=[inside] + [anywhere] * 3 + [inside] * 4,
        out_specs=[anywhere] * 3,
        scratch_shapes=[pltpu.VMEM((own_rows, width), jnp.bfloat16)] * 3
        + [pltpu.VMEM((depth, width), jnp.bfloat16)] * 3
        + [pltpu.SemaphoreType.DMA((4,))]
        + exchange_semaphores(n_tok, n_mdl, 2, 0),
        compiler_params=pltpu.CompilerParams(
            collective_id=collective_id, has_side_effects=True, vmem_limit_bytes=48 * 2**20
        ),
        name="project_and_gather",
    )(normed, *weights, *gains, cosine, sine)


def gather_all(mesh, over_tok, over_mdl, collective_id):
    n_tok, n_mdl = mesh.shape["tok"], mesh.shape["mdl"]
    n_row, n_col = len(over_tok), len(over_mdl)
    shapes = [
        jax.ShapeDtypeStruct((one.shape[0] * n_tok, one.shape[1]), one.dtype) for one in over_tok
    ] + [jax.ShapeDtypeStruct((one.shape[0], one.shape[1] * n_mdl), one.dtype) for one in over_mdl]
    return pl.pallas_call(
        functools.partial(gather_kernel, n_tok, n_mdl, n_row, n_col),
        out_shape=shapes,
        in_specs=[pl.BlockSpec(memory_space=pl.ANY)] * (n_row + n_col),
        out_specs=[pl.BlockSpec(memory_space=pl.ANY)] * (n_row + n_col),
        scratch_shapes=exchange_semaphores(n_tok, n_mdl, n_row, n_col),
        compiler_params=pltpu.CompilerParams(collective_id=collective_id, has_side_effects=True),
        name=f"gather_{collective_id}",
    )(*over_tok, *over_mdl)


def attend_kernel(rows_at_once, keys_at_once, head_width, meta_ref, q_ref, k_ref, v_ref, o_ref):
    bound, first_row = meta_ref[0], meta_ref[1]
    own_rows, lanes = q_ref.shape
    count = k_ref.shape[0]
    chunks = count // keys_at_once
    per = lanes // head_width
    lane = lax.broadcasted_iota(jnp.int32, (1, lanes), 1) // head_width
    masks = [(lane == head).astype(jnp.float32) for head in range(per)]
    edge = bound // keys_at_once
    edge_start = pl.multiple_of(edge * keys_at_once, keys_at_once)
    edge_keys = edge_start + lax.broadcasted_iota(jnp.int32, (keys_at_once, 1), 0)

    for block in range(own_rows // rows_at_once):
        rows = pl.ds(block * rows_at_once, rows_at_once)
        start = first_row + block * rows_at_once
        row_ids = start + lax.broadcasted_iota(jnp.int32, (rows_at_once, 1), 0)

        def add_chunk(carry, keys, values):
            queries = q_ref[rows, :]
            result = []
            for head in range(per):
                mine = queries * (masks[head] * head_width ** (-0.5)).astype(jnp.bfloat16)
                score = lax.dot_general(
                    mine, keys, (((1,), (1,)), ((), ())), preferred_element_type=jnp.float32
                )
                expo = jnp.exp(score).astype(jnp.bfloat16)
                result.append(
                    carry[head]
                    + jnp.dot(expo, values[head], preferred_element_type=jnp.float32)
                )
            return tuple(result)

        def inner(chunk, carry):
            here = pl.ds(pl.multiple_of(chunk * keys_at_once, keys_at_once), keys_at_once)
            values = v_ref[here, :]
            with_ones = [
                values * mask.astype(jnp.bfloat16) + (1.0 - mask).astype(jnp.bfloat16)
                for mask in masks
            ]
            return add_chunk(carry, k_ref[here, :], with_ones)

        for request in range(2):
            active = start < bound if request == 0 else start + rows_at_once > bound

            @pl.when(active)
            def _():
                here = pl.ds(edge_start, keys_at_once)
                inside = edge_keys < bound if request == 0 else edge_keys >= bound
                wide = v_ref[here, :].astype(jnp.float32)
                with_ones = [
                    jnp.where(inside, wide * mask + (1.0 - mask), 0.0).astype(jnp.bfloat16)
                    for mask in masks
                ]
                zero = jnp.zeros((rows_at_once, lanes), jnp.float32)
                carry = add_chunk((zero,) * per, k_ref[here, :], with_ones)
                if request == 0:
                    low, high = 0, edge
                else:
                    low, high = edge + 1, chunks
                carry = lax.fori_loop(low, high, inner, carry)
                output = zero
                for head in range(per):
                    total = pltpu.roll(carry[head], head_width, axis=1)
                    output = jnp.where(lane == head, carry[head] / total, output)
                if request == 0:
                    o_ref[rows, :] = output.astype(o_ref.dtype)
                else:
                    old = o_ref[rows, :].astype(jnp.float32)
                    o_ref[rows, :] = jnp.where(row_ids >= bound, output, old).astype(o_ref.dtype)


def attend(query, keys, values, bound, first_row, head_width, part, parts):
    width = query.shape[1]
    own_rows = query.shape[0] // parts
    count = keys.shape[0]
    lanes = 2 * head_width
    meta = jnp.stack([bound, first_row + part * own_rows]).astype(jnp.int32)
    block = pl.BlockSpec((own_rows, lanes), lambda pair, meta: (part, pair))
    out_block = pl.BlockSpec((own_rows, lanes), lambda pair, meta: (0, pair))
    full = pl.BlockSpec((count, lanes), lambda pair, meta: (0, pair))
    return pl.pallas_call(
        functools.partial(attend_kernel, 256, 512, head_width),
        out_shape=jax.ShapeDtypeStruct((own_rows, width), jnp.bfloat16),
        grid_spec=pltpu.PrefetchScalarGridSpec(
            num_scalar_prefetch=1,
            grid=(width // lanes,),
            in_specs=[block, full, full],
            out_specs=out_block,
        ),
        compiler_params=pltpu.CompilerParams(vmem_limit_bytes=58 * 2**20),
        cost_estimate=pl.CostEstimate(
            flops=4 * own_rows * count * width,
            bytes_accessed=4 * count * width,
            transcendentals=own_rows * count * width // head_width,
        ),
        name=f"attend_{part}",
    )(meta, query, keys, values)

def fused_kernel(n_mdl, total_rows, *refs):
    (
        lengths, hidden, positions, modulation, key_w, value_w, query_w, out_w, key_gain, query_gain,
        result,
        hid, nrm, cs, weights, qx, kv, kbias, acc, att, att_send, att_in, wout, out_acc,
        load_sem, tile_sem, swap_send, swap_recv,
        hr_send, hr_recv, hl_send, hl_recv, ns_send, ns_recv, ws_send, ws_recv,
        wx_send, wx_recv, wy_send, wy_recv, wr_send, wr_recv, wl_send, wl_recv,
        dx_send, dx_recv, dy_send, dy_recv, rk_send, rk_recv, rv_send, rv_recv,
        as_send, as_recv, zr_send, zr_recv, zl_send, zl_recv,
        ox_send, ox_recv, oy_send, oy_recv, ou_send, ou_recv, op_send, op_recv,
    ) = refs
    rows, width = hidden.shape
    pairs = weights.shape[0]
    depth = nrm.shape[2]
    lanes = weights.shape[-1]
    tile_rows = key_w.shape[0]
    blocks = 4
    block_rows = rows // blocks
    head_width = lanes // 2
    half_cols = pairs * lanes
    subs = 2 * pairs
    tok, mdl = lax.axis_index("tok"), lax.axis_index("mdl")
    chip, core = tok // 2, tok % 2
    other = 1 - core
    x_chip, y_chip, far_chip = chip + 1 - 2 * (chip % 2), (chip + 2) % 4, 3 - chip
    sibling = {"tok": chip * 2 + other, "mdl": mdl}
    x_dev = {"tok": x_chip * 2 + core, "mdl": mdl}
    y_dev = {"tok": y_chip * 2 + core, "mdl": mdl}
    remote = pltpu.make_async_remote_copy

    barrier = pltpu.get_barrier_semaphore()
    for device in (sibling, x_dev, y_dev):
        pl.semaphore_signal(barrier, inc=1, device_id=device)
    for side in (1, n_mdl - 1):
        pl.semaphore_signal(barrier, inc=1, device_id={"tok": tok, "mdl": (mdl + side) % n_mdl})

    own_hidden = pltpu.make_async_copy(hidden, hid.at[mdl], load_sem.at[0])
    own_hidden.start()
    own_out = pltpu.make_async_copy(out_w, wout.at[chip, core], load_sem.at[1])

    def columns(side, p):
        return pl.ds(pl.multiple_of(side * half_cols + p * lanes, lanes), lanes)

    projections = (key_w, value_w, query_w)
    own_tiles, swap_tiles = [], []
    for p in range(pairs):
        for m in range(3):
            number = 3 * p + m
            own_tiles.append(
                pltpu.make_async_copy(
                    projections[m].at[:, columns(core, p)],
                    weights.at[p, m, chip, core],
                    tile_sem.at[number],
                )
            )
            own_tiles[-1].start()
            swap_tiles.append(
                remote(
                    src_ref=projections[m].at[:, columns(other, p)],
                    dst_ref=weights.at[p, m, chip, core],
                    send_sem=ws_send.at[number], recv_sem=ws_recv.at[number], device_id=sibling,
                )
            )

    pl.semaphore_wait(barrier, 5)

    def copy(block, sends, recvs, index, device, target=None):
        return remote(
            src_ref=block, dst_ref=block if target is None else target,
            send_sem=sends.at[index], recv_sem=recvs.at[index], device_id=device,
        )

    def half_of(s):
        return (core + s) % 2

    def block_of(r):
        return pl.ds(r * block_rows, block_rows)

    def hidden_right(r, step):
        target = hid.at[mdl - step, block_of(r)]
        return copy(
            target if step else hidden.at[block_of(r)],
            hr_send, hr_recv, r * (n_mdl - 1) + step, {"tok": tok, "mdl": mdl + 1}, target,
        )

    def hidden_left(r, step):
        target = hid.at[mdl + step, block_of(r)]
        return copy(
            target if step else hidden.at[block_of(r)],
            hl_send, hl_recv, r * (n_mdl - 1) + step, {"tok": tok, "mdl": mdl - 1}, target,
        )

    def swap_normed(r):
        return copy(nrm.at[core, block_of(r)], ns_send, ns_recv, r, sibling)

    swap_turns = copy(cs.at[core], swap_send, swap_recv, 0, sibling)

    def weight_x(s):
        return copy(weights.at[s // 2, :, chip, half_of(s)], wx_send, wx_recv, s, x_dev)

    def weight_y(s):
        return copy(weights.at[s // 2, :, chip, half_of(s)], wy_send, wy_recv, s, y_dev)

    upper, lower = pl.ds(0, tile_rows // 2), pl.ds(tile_rows // 2, tile_rows // 2)

    def weight_relay_y(s):
        return copy(
            weights.at[s // 2, :, x_chip, half_of(s), upper], wr_send, wr_recv, s, y_dev
        )

    def weight_relay_x(s):
        return copy(
            weights.at[s // 2, :, y_chip, half_of(s), lower], wl_send, wl_recv, s, x_dev
        )

    def direct_x(s):
        return copy(kv.at[s, chip], dx_send, dx_recv, s, x_dev)

    def direct_y(s):
        return copy(kv.at[s, chip], dy_send, dy_recv, s, y_dev)

    def relay_y(s):
        return copy(kv.at[s, x_chip, 0], rk_send, rk_recv, s, y_dev)

    def relay_x(s):
        return copy(kv.at[s, y_chip, 1], rv_send, rv_recv, s, x_dev)

    def swap_att(s):
        return copy(att_send.at[s], as_send, as_recv, s, sibling, att_in.at[s])

    def z_index(s, step):
        return s * (n_mdl - 1) + step

    def z_right(s, step):
        return copy(
            att.at[mdl - step, s], zr_send, zr_recv, z_index(s, step), {"tok": tok, "mdl": mdl + 1}
        )

    def z_left(s, step):
        return copy(
            att.at[mdl + step, s], zl_send, zl_recv, z_index(s, step), {"tok": tok, "mdl": mdl - 1}
        )

    def last_rows(i):
        return pl.ds(i * (rows // 2), rows // 2)

    def last_right(i, step):
        return copy(
            att.at[mdl - step, subs - 1, last_rows(i)],
            zr_send, zr_recv, z_index(subs - 1 + i, step), {"tok": tok, "mdl": mdl + 1},
        )

    def last_left(i, step):
        return copy(
            att.at[mdl + step, subs - 1, last_rows(i)],
            zl_send, zl_recv, z_index(subs - 1 + i, step), {"tok": tok, "mdl": mdl - 1},
        )

    def line_start(right, left, index, step):
        @pl.when((mdl >= step) & (mdl < n_mdl - 1))
        def _():
            right(index, step).start()

        @pl.when((mdl + step < n_mdl) & (mdl > 0))
        def _():
            left(index, step).start()

    def line_arrive(right, left, index, step):
        @pl.when(mdl >= step + 1)
        def _():
            right(index, step).wait_recv()

        @pl.when(mdl + step + 1 < n_mdl)
        def _():
            left(index, step).wait_recv()

    def line_sent(right, left, index, step):
        @pl.when((mdl >= step) & (mdl < n_mdl - 1))
        def _():
            right(index, step).wait_send()

        @pl.when((mdl + step < n_mdl) & (mdl > 0))
        def _():
            left(index, step).wait_send()

    z_start = functools.partial(line_start, z_right, z_left)
    z_arrive = functools.partial(line_arrive, z_right, z_left)
    z_sent = functools.partial(line_sent, z_right, z_left)
    last_start = functools.partial(line_start, last_right, last_left)
    last_arrive = functools.partial(line_arrive, last_right, last_left)
    last_sent = functools.partial(line_sent, last_right, last_left)
    hidden_start = functools.partial(line_start, hidden_right, hidden_left)
    hidden_arrive = functools.partial(line_arrive, hidden_right, hidden_left)
    hidden_sent = functools.partial(line_sent, hidden_right, hidden_left)

    pieces = 4
    piece_rows = tile_rows // pieces

    def piece(i):
        return pl.ds(i * piece_rows, piece_rows)

    out_x = [
        copy(out_w.at[piece(i)], ox_send, ox_recv, i, x_dev, wout.at[chip, core, piece(i)])
        for i in range(pieces)
    ]
    out_y = [
        copy(out_w.at[piece(i)], oy_send, oy_recv, i, y_dev, wout.at[chip, core, piece(i)])
        for i in range(pieces)
    ]
    out_relay = [
        copy(
            wout.at[x_chip if i < pieces // 2 else y_chip, core, piece(i)],
            ou_send, ou_recv, i, y_dev if i < pieces // 2 else x_dev,
        )
        for i in range(pieces)
    ]
    out_pass = [
        copy(out_w, op_send, op_recv, 0, sibling, wout.at[chip, core]),
        copy(wout.at[x_chip, core], op_send, op_recv, 1, sibling),
        copy(wout.at[y_chip, core], op_send, op_recv, 2, sibling),
        copy(wout.at[far_chip, core], op_send, op_recv, 3, sibling),
    ]

    for r in range(blocks):
        hidden_start(r, 0)

    def send_weights(s):
        if s % 2 == 0:
            for one in own_tiles[3 * (s // 2) : 3 * (s // 2) + 3]:
                one.wait()
        else:
            for one in swap_tiles[3 * (s // 2) : 3 * (s // 2) + 3]:
                one.wait_recv()
        weight_x(s).start()
        weight_y(s).start()

    for one in swap_tiles[:3]:
        one.start()
    send_weights(0)
    for one in swap_tiles[3:]:
        one.start()
    own_out.start()
    send_weights(1)

    def weight_event(s):
        weight_x(s).wait_recv()
        weight_y(s).wait_recv()
        weight_relay_y(s).start()
        weight_relay_x(s).start()
        if s + 2 < subs:
            send_weights(s + 2)

    lane = lax.broadcasted_iota(jnp.int32, (1, lanes), 1)
    first = lane < head_width
    early = lane % head_width < head_width // 2
    spot = lane % head_width
    bound = TEXT + lengths[0]

    def request_terms(start, count, same, differs):
        ids = start + lax.broadcasted_iota(jnp.int32, (count, lanes), 0)
        later = ids >= bound
        zero_side = jnp.where(later, differs, same)
        one_side = jnp.where(later, same, differs)
        return jnp.where(spot == 0, zero_side, jnp.where(spot == 1, one_side, 0.0))

    def bias_step(index, carry):
        kbias[index] = request_terms(index * rows, rows, 0.0, -16384.0).astype(jnp.bfloat16)
        return carry

    lax.fori_loop(0, total_rows // rows, bias_step, 0)

    def clear(s, carry):
        acc[s] = jnp.zeros(acc.shape[1:], jnp.float32)
        return carry

    lax.fori_loop(0, subs, clear, 0)

    def wide_gain(gain):
        return jnp.concatenate([gain[...], gain[...]], axis=1)

    def head_mean(terms):
        one = jnp.sum(jnp.where(first, terms, 0.0), axis=1, keepdims=True)
        two = jnp.sum(jnp.where(first, 0.0, terms), axis=1, keepdims=True)
        return jnp.where(first, one, two) * (1.0 / head_width)

    def finished(summed, gain, turns):
        center = summed - head_mean(summed)
        normal = center * lax.rsqrt(head_mean(center * center) + 1e-06) * gain
        partner = jnp.where(
            early,
            pltpu.roll(normal, lanes - head_width // 2, axis=1),
            pltpu.roll(normal, head_width // 2, axis=1),
        )
        return normal * turns[0] + partner * turns[1]

    quarter = head_width // 2
    pair = lane % quarter
    one_count = quarter // 4
    two_count = (quarter - one_count) // 2
    three_count = quarter - one_count - two_count
    is_one, is_two = pair < one_count, pair < one_count + two_count
    local = pair - jnp.where(is_one, 0, jnp.where(is_two, one_count, one_count + two_count))
    count = jnp.where(is_one, one_count, jnp.where(is_two, two_count, three_count))
    power = local.astype(jnp.float32) / count.astype(jnp.float32)
    rates = jnp.exp(power * -9.210340371976184)
    places = jnp.transpose(
        jnp.concatenate(
            [positions[...].astype(jnp.float32), jnp.zeros((5, rows), jnp.float32)], axis=0
        )
    )
    angles = rates * jnp.where(
        is_one, places[:, 0:1], jnp.where(is_two, places[:, 1:2], places[:, 2:3])
    )

    def textual(start, count):
        ids = tok * rows + start + lax.broadcasted_iota(jnp.int32, (count, 1), 0)
        place = jnp.where(ids >= bound, ids - bound, ids)
        return place < TEXT

    is_text = textual(0, rows)
    cs[core, 0] = jnp.where(is_text, 1.0, jnp.cos(angles))
    sine = jnp.sin(angles)
    cs[core, 1] = jnp.where(is_text, 0.0, jnp.where(early, -sine, sine))
    swap_turns.start()

    def normalize(r):
        wide = jnp.concatenate([hid[z, block_of(r), :] for z in range(n_mdl)], axis=1)
        values_in = wide.astype(jnp.float32)
        center = values_in - jnp.mean(values_in, axis=1, keepdims=True)
        spread = jnp.mean(center * center, axis=1, keepdims=True)
        normal = center * lax.rsqrt(spread + 1e-05)
        text_rows = textual(r * block_rows, block_rows)
        shift = jnp.where(text_rows, modulation[3:4, :], modulation[0:1, :])
        scale = jnp.where(text_rows, modulation[4:5, :], modulation[1:2, :])
        nrm[core, block_of(r), :] = (normal * (1.0 + scale) + shift).astype(jnp.bfloat16)
        swap_normed(r).start()

    def hidden_hop(r, step):
        hidden_arrive(r, step - 1)
        if step < n_mdl - 1:
            hidden_start(r, step)
        else:
            if r == 0:
                own_hidden.wait()
            normalize(r)

    def weight_arrive(s):
        weight_relay_y(s).wait_recv()
        weight_relay_x(s).wait_recv()

    def project(p, half, start, size):
        where = pl.ds(start, size)
        here = pl.ds(pl.multiple_of(half * rows + start, size), size)
        tall = [weights[p, m].reshape(depth, lanes) for m in range(3)]
        summed = jnp.dot(
            nrm[half, where, :], jnp.concatenate(tall, axis=1), preferred_element_type=jnp.float32
        )
        turns = cs[half, 0, where, :], cs[half, 1, where, :]
        keys = finished(summed[:, :lanes], wide_gain(key_gain), turns)
        values = pltpu.roll(summed[:, lanes : 2 * lanes], head_width, axis=1)
        kv[2 * p, chip, half, where, :] = jnp.where(first, keys, values).astype(jnp.bfloat16)
        kv[2 * p + 1, chip, half, where, :] = jnp.where(first, values, keys).astype(jnp.bfloat16)
        gain = wide_gain(query_gain) * (head_width ** (-0.5) * 1.4426950408889634)
        query = finished(summed[:, 2 * lanes :], gain, turns)
        terms = request_terms((chip * 2 + half) * rows + start, size, 0.0, 1.0)
        terms = jnp.where(spot < 2, 1.0 - terms, 0.0)
        qx[2 * p, here, :] = jnp.where(first, query, terms).astype(jnp.bfloat16)
        qx[2 * p + 1, here, :] = jnp.where(first, terms, query).astype(jnp.bfloat16)

    def project_own(p, r, count):
        project(p, core, r * block_rows, count * block_rows)

    def project_other(p, r, count):
        project(p, other, r * block_rows, count * block_rows)

    hidden_hop(0, 1)
    weight_event(0)
    hidden_hop(1, 1)
    hidden_hop(2, 1)
    weight_event(1)
    hidden_hop(3, 1)
    hidden_hop(0, 2)
    weight_event(2)
    hidden_hop(1, 2)
    hidden_hop(2, 2)
    hidden_hop(3, 2)
    weight_event(3)
    weight_arrive(0)
    weight_arrive(1)
    swap_turns.wait_recv()
    hidden_hop(0, 3)
    project_own(0, 0, 1)
    hidden_hop(1, 3)
    project_own(0, 1, 1)
    weight_event(4)
    swap_normed(0).wait_recv()
    project_other(0, 0, 1)
    hidden_hop(2, 3)
    project_own(0, 2, 1)
    swap_normed(1).wait_recv()
    project_other(0, 1, 1)
    swap_normed(2).wait_recv()
    project_other(0, 2, 1)
    hidden_hop(3, 3)
    project_own(0, 3, 1)
    weight_event(5)
    swap_normed(3).wait_recv()
    project_other(0, 3, 1)
    for s in range(2):
        direct_x(s).start()
        direct_y(s).start()
    for s in range(2, subs):
        weight_arrive(s)

    def project_rest(number, carry):
        project(1 + number // 2, number % 2, 0, rows)
        return carry

    lax.fori_loop(0, 2 * (pairs - 1), project_rest, 0)

    most = TEXT + (total_rows - 2 * TEXT) * 5 // 8
    last_first = -(-most // rows)
    first_last = (total_rows - most) // rows

    def needed(row_block, key_block):
        return (
            ((row_block < first_last) & (key_block < last_first))
            | ((row_block >= last_first) & (key_block >= first_last))
            | ((row_block >= first_last) & (row_block < last_first))
        )

    def attend_rows(where, s, source, halves):
        mine = (lane + (s % 2) * head_width) % lanes < head_width
        added = None
        for half in halves:
            block = kv[s, source, half]
            score = lax.dot_general(
                qx[s, where, :],
                jnp.where(mine, block, kbias[source * 2 + half]),
                (((1,), (1,)), ((), ())),
                preferred_element_type=jnp.float32,
            )
            part = jnp.dot(
                jnp.exp2(score).astype(jnp.bfloat16),
                jnp.where(mine, jnp.ones_like(block), block),
                preferred_element_type=jnp.float32,
            )
            added = part if added is None else added + part
        acc[s, where, :] += added

    def attend_block(s, source, r):
        where = pl.ds(pl.multiple_of(r * rows, rows), rows)
        low = needed(chip * 2 + r, source * 2)
        high = needed(chip * 2 + r, source * 2 + 1)

        @pl.when(low & high)
        def _():
            attend_rows(where, s, source, (0, 1))

        @pl.when(low != high)
        def _():
            attend_rows(where, s, source, (jnp.where(low, 0, 1),))

    def attend_unit(s, source):
        row_block, key_block = chip * 2, source * 2
        whole = (
            needed(row_block, key_block)
            & needed(row_block, key_block + 1)
            & needed(row_block + 1, key_block)
            & needed(row_block + 1, key_block + 1)
        )

        @pl.when(whole)
        def _():
            attend_rows(pl.ds(0, 2 * rows), s, source, (0, 1))

        @pl.when(jnp.logical_not(whole))
        def _():
            def one_block(r, inner):
                attend_block(s, source, r)
                return inner

            lax.fori_loop(0, 2, one_block, 0)

    def finish_head(s):
        moved = (s + 1) % 2 != core

        def one_side(turn, inner):
            r = jnp.where(turn == 0, other, core)
            attend_block(s, far_chip, r)
            both = acc[s, pl.ds(pl.multiple_of(r * rows, rows), rows), :]
            ratio = both / pltpu.roll(both, head_width, axis=1)
            ratio = jnp.where(moved, pltpu.roll(ratio, head_width, axis=1), ratio)
            ratio = ratio.astype(jnp.bfloat16)

            @pl.when(turn == 0)
            def _():
                att_send[s] = ratio
                swap_att(s).start()

            @pl.when(turn == 1)
            def _():
                swap_att(s).wait_recv()
                att[mdl, s] = jnp.where(lane // head_width == core, ratio, att_in[s])

            return inner

        lax.fori_loop(0, 2, one_side, 0)

    def pass_on(s, step):
        z_arrive(s, step - 1)
        z_start(s, step)

    final = subs - 1

    def turn(s, carry):
        def visit(j, inner):
            source = jnp.where(j == 0, chip, jnp.where(j == 1, x_chip, y_chip))

            @pl.when((s < subs) & (((j == 1) & (s > 0)) | ((j == 0) & (s == 0))))
            def _():
                direct_x(s).wait_recv()
                direct_y(s).wait_recv()
                relay_y(s).start()
                relay_x(s).start()

                @pl.when(s + 2 < subs)
                def _():
                    direct_x(s + 2).start()
                    direct_y(s + 2).start()

                @pl.when(s + 2 == subs)
                def _():
                    out_x[0].start()
                    out_y[0].start()
                    out_pass[0].start()

                @pl.when(s + 1 == subs)
                def _():
                    for i in range(1, pieces):
                        out_x[i].start()
                        out_y[i].start()

            @pl.when((j == 2) & (s >= 2))
            def _():
                pass_on(s - 2, 1)

            @pl.when(s < subs)
            def _():
                attend_unit(s, source)

            return inner

        lax.fori_loop(0, 3, visit, 0)

        @pl.when(s >= 1)
        def _():
            relay_y(s - 1).wait_recv()
            relay_x(s - 1).wait_recv()
            finish_head(s - 1)

            @pl.when(s - 1 < final)
            def _():
                z_start(s - 1, 0)

            @pl.when(s - 1 == final)
            def _():
                last_start(0, 0)
                last_start(1, 0)

        @pl.when(s >= 2)
        def _():
            pass_on(s - 2, 2)

        return carry

    lax.fori_loop(0, subs + 1, turn, 0)

    def out_event(i):
        out_x[i].wait_recv()
        out_y[i].wait_recv()
        out_relay[i].start()

    def last_on(i, step):
        last_arrive(i, step - 1)
        last_start(i, step)

    out_event(0)
    out_event(1)
    last_on(0, 1)
    last_on(1, 1)
    out_event(2)
    last_on(0, 2)
    out_event(3)
    last_on(1, 2)
    out_pass[1].start()
    out_pass[2].start()
    own_out.wait()

    def combine(block):
        tall = [
            wout[block, side, s * head_width : (s + 1) * head_width, :]
            for s in range(subs)
            for side in range(2)
        ]
        return jnp.dot(
            jnp.concatenate([att[block, s] for s in range(subs)], axis=1),
            jnp.concatenate(tall, axis=0),
            preferred_element_type=jnp.float32,
        )

    for s in range(final):
        z_arrive(s, n_mdl - 2)
    for i in range(2):
        last_arrive(i, n_mdl - 2)
    out_pass[0].wait_recv()
    out_acc[...] = combine(chip)
    out_pass[1].wait_recv()
    out_acc[...] += combine(x_chip)
    out_pass[2].wait_recv()
    out_acc[...] += combine(y_chip)
    for one in out_relay:
        one.wait_recv()
    out_pass[3].start()
    out_pass[3].wait_recv()
    projected = out_acc[...] + combine(far_chip)
    own_columns = pl.ds(pl.multiple_of(mdl * width, lanes), width)
    gate = jnp.where(is_text, modulation[5:6, own_columns], modulation[2:3, own_columns])
    result[...] = (hid[mdl].astype(jnp.float32) + gate * projected).astype(jnp.bfloat16)

    swap_turns.wait_send()
    for r in range(blocks):
        swap_normed(r).wait_send()
        for step in range(n_mdl - 1):
            hidden_sent(r, step)
    for one in swap_tiles:
        one.wait_send()
    for s in range(subs):
        weight_x(s).wait_send()
        weight_y(s).wait_send()
        weight_relay_y(s).wait_send()
        weight_relay_x(s).wait_send()
        direct_x(s).wait_send()
        direct_y(s).wait_send()
        relay_y(s).wait_send()
        relay_x(s).wait_send()
        swap_att(s).wait_send()
    for step in range(n_mdl - 1):
        for s in range(final):
            z_sent(s, step)
        for i in range(2):
            last_sent(i, step)
    for one in out_x + out_y + out_relay + out_pass:
        one.wait_send()


def fused(
    mesh, lengths, hidden, positions, modulation, weights, out_weight, gains, collective_id
):
    n_tok, n_mdl = mesh.shape["tok"], mesh.shape["mdl"]
    rows, width = hidden.shape
    depth = width * n_mdl
    lanes = 2 * gains[0].shape[1]
    pairs = width // (2 * lanes)
    total_rows = rows * n_tok
    chips = n_tok // 2
    subs = 2 * pairs
    blocks = 4
    bf, f32 = jnp.bfloat16, jnp.float32
    anywhere = pl.BlockSpec(memory_space=pl.ANY)
    inside = pl.BlockSpec(memory_space=pltpu.VMEM)

    def sems(count):
        return [pltpu.SemaphoreType.DMA((count,))]

    return pl.pallas_call(
        functools.partial(fused_kernel, n_mdl, total_rows),
        out_shape=jax.ShapeDtypeStruct((rows, width), bf),
        in_specs=[pl.BlockSpec(memory_space=pltpu.SMEM), anywhere]
        + [inside] * 2
        + [anywhere] * 4
        + [inside] * 2,
        out_specs=inside,
        scratch_shapes=[
            pltpu.VMEM((n_mdl, rows, width), bf),
            pltpu.VMEM((2, rows, depth), bf),
            pltpu.VMEM((2, 2, rows, lanes), f32),
            pltpu.VMEM((pairs, 3, chips, 2, out_weight.shape[0], lanes), bf),
            pltpu.VMEM((2 * pairs, 2 * rows, lanes), bf),
            pltpu.VMEM((subs, chips, 2, rows, lanes), bf),
            pltpu.VMEM((n_tok, rows, lanes), bf),
            pltpu.VMEM((subs, 2 * rows, lanes), f32),
            pltpu.VMEM((n_mdl, subs, rows, lanes), bf),
            pltpu.VMEM((subs, rows, lanes), bf),
            pltpu.VMEM((subs, rows, lanes), bf),
            pltpu.VMEM((chips, 2) + out_weight.shape, bf),
            pltpu.VMEM((rows, width), f32),
        ]
        + sems(2)
        + sems(3 * pairs)
        + sems(1) * 2
        + sems(blocks * (n_mdl - 1)) * 4
        + sems(blocks) * 2
        + sems(3 * pairs) * 2
        + sems(subs) * 8
        + sems(subs) * 8
        + sems(subs) * 2
        + sems((subs + 1) * (n_mdl - 1)) * 4
        + sems(4) * 8,
        compiler_params=pltpu.CompilerParams(
            collective_id=collective_id, has_side_effects=True, vmem_limit_bytes=60 * 2**20
        ),
        name="fused",
    )(lengths, hidden, positions, modulation, *weights, out_weight, *gains)


def shards(
    mesh,
    hidden_states,
    lengths,
    positions,
    modulation,
    query_weight,
    key_weight,
    value_weight,
    out_weight,
    query_gain,
    key_gain,
):
    own_rows = hidden_states.shape[0]
    head_width = query_gain.shape[0]
    if mesh.shape["tok"] == 8 and mesh.shape["mdl"] == 4:
        return fused(
            mesh,
            lengths,
            hidden_states,
            positions,
            modulation,
            (key_weight, value_weight, query_weight),
            out_weight,
            [gain[None, :] for gain in (key_gain, query_gain)],
            0,
        )
    full_rows = lax.all_gather(hidden_states, "mdl", axis=1, tiled=True)
    key_full, value_full, query_full = gather_all(
        mesh, [key_weight, value_weight, query_weight], [], 0
    )
    row_index = lax.axis_index("tok") * own_rows + jnp.arange(own_rows, dtype=jnp.int32)
    request, is_text, bound = token_labels(row_index, lengths)
    normed = modulate(full_rows, modulation, is_text)
    angles = pair_angles(positions, head_width // 2)
    textual = is_text[:, None]
    cosine = jnp.tile(jnp.where(textual, 1.0, jnp.cos(angles)), (1, 4))
    sine = jnp.where(textual, 0.0, jnp.sin(angles))
    sine = jnp.tile(jnp.concatenate([-sine, sine], axis=1), (1, 2))
    keys, values, query_flat = project_and_gather(
        mesh,
        normed,
        (key_full, value_full, query_full),
        [jnp.tile(gain, 2)[None, :] for gain in (key_gain, query_gain)],
        cosine,
        sine,
        head_width,
        1,
    )
    first_row = lax.axis_index("tok") * own_rows
    first, second = (
        attend(query_flat, keys, values, bound, first_row, head_width, part, 2)
        for part in range(2)
    )
    first_heads = lax.all_gather(first, "mdl", axis=1, tiled=True)
    out_full, second_heads = gather_all(mesh, [out_weight], [second], 2)
    out_width = out_weight.shape[1]
    projected = jnp.concatenate(
        [
            jnp.dot(heads, out_full, preferred_element_type=jnp.float32)
            for heads in (first_heads, second_heads)
        ],
        axis=0,
    )
    gate_rows = lax.dynamic_slice_in_dim(
        modulation, lax.axis_index("mdl") * out_width, out_width, 1
    )
    gate = jnp.where(is_text[:, None], gate_rows[5][None, :], gate_rows[2][None, :])
    return (hidden_states.astype(jnp.float32) + gate * projected).astype(jnp.bfloat16)


def solution(mesh):
    return jax.shard_map(
        functools.partial(shards, mesh),
        mesh=mesh,
        in_specs=(
            P("tok", "mdl"),
            P(),
            P(None, "tok"),
            P(),
            P("tok", "mdl"),
            P("tok", "mdl"),
            P("tok", "mdl"),
            P("tok", "mdl"),
            P(),
            P(),
        ),
        out_specs=P("tok", "mdl"),
        check_vma=False,
    )
```

```python
import functools
import jax
import jax.numpy as jnp
from jax import lax
from jax.experimental import pallas as pl
from jax.experimental.pallas import tpu as pltpu
from jax.sharding import PartitionSpec as P

TEXT = 226


def token_labels(row_index, lengths):
    bound = TEXT + lengths[0]
    request = (row_index >= bound).astype(jnp.int32)
    place = row_index - request * bound
    return (request, place < TEXT, bound)


def modulate(rows_bf, modulation, is_text):
    values = rows_bf.astype(jnp.float32)
    center = values - jnp.mean(values, axis=1, keepdims=True)
    spread = jnp.mean(center * center, axis=1, keepdims=True)
    normal = center * lax.rsqrt(spread + 1e-05)
    textual = is_text[:, None]
    shift = jnp.where(textual, modulation[3][None, :], modulation[0][None, :])
    scale = jnp.where(textual, modulation[4][None, :], modulation[1][None, :])
    return (normal * (1.0 + scale) + shift).astype(jnp.bfloat16)


def pair_angles(positions, pairs):
    index = jnp.arange(pairs, dtype=jnp.int32)
    first = pairs // 4
    second = (pairs - first) // 2
    third = pairs - first - second
    component = jnp.where(index < first, 0, jnp.where(index < first + second, 1, 2))
    local = index - jnp.where(component == 0, 0, jnp.where(component == 1, first, first + second))
    count = jnp.where(component == 0, first, jnp.where(component == 1, second, third))
    rates = jnp.power(jnp.float32(10000.0), -local.astype(jnp.float32) / count.astype(jnp.float32))
    places = positions.astype(jnp.float32)
    chosen = jnp.where(
        component[:, None] == 0,
        places[0][None, :],
        jnp.where(component[:, None] == 1, places[1][None, :], places[2][None, :]),
    )
    return jnp.transpose(chosen * rates[:, None])


def gather_kernel(n_tok, n_mdl, n_row, n_col, *refs):
    count = n_row + n_col
    ins, outs = refs[:count], refs[count : 2 * count]
    exchange(
        n_tok, n_mdl, ins[:n_row], ins[n_row:], outs[:n_row], outs[n_row:], refs[2 * count :]
    )


def exchange(
    n_tok, n_mdl, rows_in, cols_in, rows_out, cols_out, semaphores, prepare=None, between=None
):
    n_row, n_col = len(rows_in), len(cols_in)
    (
        local_sem,
        send1,
        recv1,
        send2,
        recv2,
        send3,
        recv3,
        to_right,
        from_left,
        to_left,
        from_right,
    ) = semaphores
    square = n_tok == 8
    chips = n_tok // 2
    tok, mdl = lax.axis_index("tok"), lax.axis_index("mdl")
    chip, core = tok // 2, tok % 2
    sibling = chip * 2 + 1 - core

    def chip_at(step):
        if square:
            return (chip, chip + 1 - 2 * (chip % 2), (chip + 2) % 4, 3 - chip)[step]
        return (chip + step) % chips

    def source_at(step):
        return chip_at(step) if square else chip_at(chips - step)

    barrier = pltpu.get_barrier_semaphore()
    greeted = 0
    if n_row:
        for step in (1, 2) if square else range(1, chips):
            pl.semaphore_signal(
                barrier, inc=1, device_id={"tok": chip_at(step) * 2 + core, "mdl": mdl}
            )
            greeted += 1
        pl.semaphore_signal(barrier, inc=1, device_id={"tok": sibling, "mdl": mdl})
        greeted += 1
    if n_col:
        for side in (1, n_mdl - 1):
            pl.semaphore_signal(
                barrier, inc=1, device_id={"tok": tok, "mdl": (mdl + side) % n_mdl}
            )
            greeted += 1
    pl.semaphore_wait(barrier, greeted)

    def row_block(number, owner):
        size = rows_in[number].shape[0]
        return rows_out[number].at[pl.ds(pl.multiple_of(owner * size, size), size), :]

    def col_block(number, owner):
        size = cols_in[number].shape[1]
        return cols_out[number].at[:, pl.ds(pl.multiple_of(owner * size, size), size)]

    def direct(number, step):
        target = chip_at(step) * 2 + core if step else sibling
        return pltpu.make_async_remote_copy(
            src_ref=rows_in[number],
            dst_ref=row_block(number, tok),
            send_sem=send1.at[number, step],
            recv_sem=recv1.at[number, step],
            device_id={"tok": target, "mdl": mdl},
        )

    def passed(number, step):
        block = row_block(number, source_at(step) * 2 + core)
        return pltpu.make_async_remote_copy(
            src_ref=block,
            dst_ref=block,
            send_sem=send2.at[number, step],
            recv_sem=recv2.at[number, step],
            device_id={"tok": sibling, "mdl": mdl},
        )

    def relayed(number, step):
        half = rows_in[number].shape[0] // 2
        first = (source_at(step) * 2 + core) * 2 * half + (step - 1) * half
        block = rows_out[number].at[pl.ds(pl.multiple_of(first, half), half), :]
        return pltpu.make_async_remote_copy(
            src_ref=block,
            dst_ref=block,
            send_sem=send3.at[number, step],
            recv_sem=recv3.at[number, step],
            device_id={"tok": chip_at(3 - step) * 2 + core, "mdl": mdl},
        )

    directs = (1, 2) if square else range(1, chips)

    def rightward(number, step):
        block = col_block(number, mdl - step)
        return pltpu.make_async_remote_copy(
            src_ref=block if step else cols_in[number],
            dst_ref=block,
            send_sem=to_right.at[number, step],
            recv_sem=from_left.at[number, step],
            device_id={"tok": tok, "mdl": mdl + 1},
        )

    def leftward(number, step):
        block = col_block(number, mdl + step)
        return pltpu.make_async_remote_copy(
            src_ref=block if step else cols_in[number],
            dst_ref=block,
            send_sem=to_left.at[number, step],
            recv_sem=from_right.at[number, step],
            device_id={"tok": tok, "mdl": mdl - 1},
        )

    def right_if(step):
        return (mdl >= step) & (mdl < n_mdl - 1)

    def left_if(step):
        return (mdl + step < n_mdl) & (mdl > 0)

    for number in range(n_col):
        @pl.when(right_if(0))
        def _():
            rightward(number, 0).start()

        @pl.when(left_if(0))
        def _():
            leftward(number, 0).start()

    locals_ = []
    for number in range(n_col):
        locals_.append(
            pltpu.make_async_copy(
                cols_in[number], col_block(number, mdl), local_sem.at[n_row + number]
            )
        )
        locals_[-1].start()
    for number in range(n_row):
        if prepare is not None:
            prepare(number)
        for step in directs:
            direct(number, step).start()
        direct(number, 0).start()
        locals_.append(
            pltpu.make_async_copy(rows_in[number], row_block(number, tok), local_sem.at[number])
        )
        locals_[-1].start()

    def finish_diagonal(number):
        for step in (1, 2):
            relayed(number, step).wait_recv()
        passed(number, 3).start()

    for turn in range(max(n_row, n_mdl - 2 if n_col else 0)):
        hop = turn + 1
        if hop < n_mdl - 1:
            for number in range(n_col):
                @pl.when(mdl >= hop)
                def _():
                    rightward(number, hop - 1).wait_recv()

                @pl.when(right_if(hop))
                def _():
                    rightward(number, hop).start()

                @pl.when(mdl + hop < n_mdl)
                def _():
                    leftward(number, hop - 1).wait_recv()

                @pl.when(left_if(hop))
                def _():
                    leftward(number, hop).start()

        if turn < n_row:
            for step in directs:
                direct(turn, step).wait_recv()
                if square:
                    relayed(turn, step).start()
                passed(turn, step).start()
            if square and turn > 0:
                finish_diagonal(turn - 1)
        if between is not None:
            between(turn)

    if square and n_row:
        finish_diagonal(n_row - 1)
    for copy in locals_:
        copy.wait()
    for number in range(n_col):
        @pl.when(mdl >= n_mdl - 1)
        def _():
            rightward(number, n_mdl - 2).wait_recv()

        @pl.when(mdl + n_mdl - 1 < n_mdl)
        def _():
            leftward(number, n_mdl - 2).wait_recv()

    for number in range(n_row):
        direct(number, 0).wait()
        for step in directs:
            direct(number, step).wait_send()
            if square:
                relayed(number, step).wait_send()
        for step in range(1, chips):
            passed(number, step).wait()
    for number in range(n_col):
        for step in range(n_mdl - 1):
            @pl.when(right_if(step))
            def _():
                rightward(number, step).wait_send()

            @pl.when(left_if(step))
            def _():
                leftward(number, step).wait_send()


def exchange_semaphores(n_tok, n_mdl, n_row, n_col):
    row_sem = pltpu.SemaphoreType.DMA((max(n_row, 1), n_tok // 2))
    col_sem = pltpu.SemaphoreType.DMA((max(n_col, 1), n_mdl))
    return [pltpu.SemaphoreType.DMA((n_row + n_col,))] + [row_sem] * 6 + [col_sem] * 4


def project_kernel(n_tok, n_mdl, head_width, *refs):
    normed, key_w, value_w, query_w, key_gain, query_gain, cosine, sine = refs[:8]
    keys_out, values_out, query_out = refs[8:11]
    keys, values, query, key_held, value_held, query_held, load_sem = refs[11:18]
    width = keys.shape[1]
    lanes = 2 * head_width
    block = 256 if width % 256 == 0 else lanes
    loads = [
        pltpu.make_async_copy(source, held, load_sem.at[number])
        for number, (source, held) in enumerate(
            ((key_w, key_held), (value_w, value_held), (query_w, query_held))
        )
    ]
    for load in loads:
        load.start()
    lane = lax.broadcasted_iota(jnp.int32, (1, lanes), 1)
    first = lane < head_width
    early = lane % head_width < head_width // 2

    def head_mean(terms):
        one = jnp.sum(jnp.where(first, terms, 0.0), axis=1, keepdims=True)
        other = jnp.sum(jnp.where(first, 0.0, terms), axis=1, keepdims=True)
        return jnp.where(first, one, other) * (1.0 / head_width)

    def finished(summed, gain):
        center = summed - head_mean(summed)
        normal = center * lax.rsqrt(head_mean(center * center) + 1e-06) * gain[...]
        partner = jnp.where(
            early,
            pltpu.roll(normal, lanes - head_width // 2, axis=1),
            pltpu.roll(normal, head_width // 2, axis=1),
        )
        return normal * cosine[...] + partner * sine[...]

    def project(held, gain, target):
        def step(number, carry):
            columns = pl.ds(pl.multiple_of(number * block, block), block)
            summed = jnp.dot(
                normed[...], held[:, columns], preferred_element_type=jnp.float32
            )
            if gain is not None:
                summed = jnp.concatenate(
                    [
                        finished(summed[:, start : start + lanes], gain)
                        for start in range(0, block, lanes)
                    ],
                    axis=1,
                )
            target[:, columns] = summed.astype(jnp.bfloat16)
            return carry

        lax.fori_loop(0, width // block, step, 0)

    def prepare(number):
        loads[number].wait()
        if number == 0:
            project(key_held, key_gain, keys)
        else:
            project(value_held, None, values)

    query_copy = pltpu.make_async_copy(query, query_out, load_sem.at[3])

    def between(turn):
        if turn == 0:
            loads[2].wait()
            project(query_held, query_gain, query)
            query_copy.start()

    exchange(
        n_tok,
        n_mdl,
        (keys, values),
        (),
        (keys_out, values_out),
        (),
        refs[18:],
        prepare,
        between,
    )
    query_copy.wait()


def project_and_gather(mesh, normed, weights, gains, cosine, sine, head_width, collective_id):
    n_tok, n_mdl = mesh.shape["tok"], mesh.shape["mdl"]
    own_rows, depth = normed.shape
    width = weights[0].shape[1]
    full = jax.ShapeDtypeStruct((own_rows * n_tok, width), jnp.bfloat16)
    own = jax.ShapeDtypeStruct((own_rows, width), jnp.bfloat16)
    anywhere = pl.BlockSpec(memory_space=pl.ANY)
    inside = pl.BlockSpec(memory_space=pltpu.VMEM)
    return pl.pallas_call(
        functools.partial(project_kernel, n_tok, n_mdl, head_width),
        out_shape=[full, full, own],
        in_specs=[inside] + [anywhere] * 3 + [inside] * 4,
        out_specs=[anywhere] * 3,
        scratch_shapes=[pltpu.VMEM((own_rows, width), jnp.bfloat16)] * 3
        + [pltpu.VMEM((depth, width), jnp.bfloat16)] * 3
        + [pltpu.SemaphoreType.DMA((4,))]
        + exchange_semaphores(n_tok, n_mdl, 2, 0),
        compiler_params=pltpu.CompilerParams(
            collective_id=collective_id, has_side_effects=True, vmem_limit_bytes=48 * 2**20
        ),
        name="project_and_gather",
    )(normed, *weights, *gains, cosine, sine)


def gather_all(mesh, over_tok, over_mdl, collective_id):
    n_tok, n_mdl = mesh.shape["tok"], mesh.shape["mdl"]
    n_row, n_col = len(over_tok), len(over_mdl)
    shapes = [
        jax.ShapeDtypeStruct((one.shape[0] * n_tok, one.shape[1]), one.dtype) for one in over_tok
    ] + [jax.ShapeDtypeStruct((one.shape[0], one.shape[1] * n_mdl), one.dtype) for one in over_mdl]
    return pl.pallas_call(
        functools.partial(gather_kernel, n_tok, n_mdl, n_row, n_col),
        out_shape=shapes,
        in_specs=[pl.BlockSpec(memory_space=pl.ANY)] * (n_row + n_col),
        out_specs=[pl.BlockSpec(memory_space=pl.ANY)] * (n_row + n_col),
        scratch_shapes=exchange_semaphores(n_tok, n_mdl, n_row, n_col),
        compiler_params=pltpu.CompilerParams(collective_id=collective_id, has_side_effects=True),
        name=f"gather_{collective_id}",
    )(*over_tok, *over_mdl)


def attend_kernel(rows_at_once, keys_at_once, head_width, meta_ref, q_ref, k_ref, v_ref, o_ref):
    bound, first_row = meta_ref[0], meta_ref[1]
    own_rows, lanes = q_ref.shape
    count = k_ref.shape[0]
    chunks = count // keys_at_once
    per = lanes // head_width
    lane = lax.broadcasted_iota(jnp.int32, (1, lanes), 1) // head_width
    masks = [(lane == head).astype(jnp.float32) for head in range(per)]
    edge = bound // keys_at_once
    edge_start = pl.multiple_of(edge * keys_at_once, keys_at_once)
    edge_keys = edge_start + lax.broadcasted_iota(jnp.int32, (keys_at_once, 1), 0)

    for block in range(own_rows // rows_at_once):
        rows = pl.ds(block * rows_at_once, rows_at_once)
        start = first_row + block * rows_at_once
        row_ids = start + lax.broadcasted_iota(jnp.int32, (rows_at_once, 1), 0)

        def add_chunk(carry, keys, values):
            queries = q_ref[rows, :]
            result = []
            for head in range(per):
                mine = queries * (masks[head] * head_width ** (-0.5)).astype(jnp.bfloat16)
                score = lax.dot_general(
                    mine, keys, (((1,), (1,)), ((), ())), preferred_element_type=jnp.float32
                )
                expo = jnp.exp(score).astype(jnp.bfloat16)
                result.append(
                    carry[head]
                    + jnp.dot(expo, values[head], preferred_element_type=jnp.float32)
                )
            return tuple(result)

        def inner(chunk, carry):
            here = pl.ds(pl.multiple_of(chunk * keys_at_once, keys_at_once), keys_at_once)
            values = v_ref[here, :]
            with_ones = [
                values * mask.astype(jnp.bfloat16) + (1.0 - mask).astype(jnp.bfloat16)
                for mask in masks
            ]
            return add_chunk(carry, k_ref[here, :], with_ones)

        for request in range(2):
            active = start < bound if request == 0 else start + rows_at_once > bound

            @pl.when(active)
            def _():
                here = pl.ds(edge_start, keys_at_once)
                inside = edge_keys < bound if request == 0 else edge_keys >= bound
                wide = v_ref[here, :].astype(jnp.float32)
                with_ones = [
                    jnp.where(inside, wide * mask + (1.0 - mask), 0.0).astype(jnp.bfloat16)
                    for mask in masks
                ]
                zero = jnp.zeros((rows_at_once, lanes), jnp.float32)
                carry = add_chunk((zero,) * per, k_ref[here, :], with_ones)
                if request == 0:
                    low, high = 0, edge
                else:
                    low, high = edge + 1, chunks
                carry = lax.fori_loop(low, high, inner, carry)
                output = zero
                for head in range(per):
                    total = pltpu.roll(carry[head], head_width, axis=1)
                    output = jnp.where(lane == head, carry[head] / total, output)
                if request == 0:
                    o_ref[rows, :] = output.astype(o_ref.dtype)
                else:
                    old = o_ref[rows, :].astype(jnp.float32)
                    o_ref[rows, :] = jnp.where(row_ids >= bound, output, old).astype(o_ref.dtype)


def attend(query, keys, values, bound, first_row, head_width, part, parts):
    width = query.shape[1]
    own_rows = query.shape[0] // parts
    count = keys.shape[0]
    lanes = 2 * head_width
    meta = jnp.stack([bound, first_row + part * own_rows]).astype(jnp.int32)
    block = pl.BlockSpec((own_rows, lanes), lambda pair, meta: (part, pair))
    out_block = pl.BlockSpec((own_rows, lanes), lambda pair, meta: (0, pair))
    full = pl.BlockSpec((count, lanes), lambda pair, meta: (0, pair))
    return pl.pallas_call(
        functools.partial(attend_kernel, 256, 512, head_width),
        out_shape=jax.ShapeDtypeStruct((own_rows, width), jnp.bfloat16),
        grid_spec=pltpu.PrefetchScalarGridSpec(
            num_scalar_prefetch=1,
            grid=(width // lanes,),
            in_specs=[block, full, full],
            out_specs=out_block,
        ),
        compiler_params=pltpu.CompilerParams(vmem_limit_bytes=58 * 2**20),
        cost_estimate=pl.CostEstimate(
            flops=4 * own_rows * count * width,
            bytes_accessed=4 * count * width,
            transcendentals=own_rows * count * width // head_width,
        ),
        name=f"attend_{part}",
    )(meta, query, keys, values)

def fused_kernel(n_mdl, total_rows, *refs):
    (
        lengths, hidden, positions, modulation, key_w, value_w, query_w, out_w, key_gain, query_gain,
        result,
        hid, nrm, cs, weights, qx, kv, kbias, acc, att, att_send, att_in, wout, out_acc, average,
        load_sem, tile_sem, swap_send, swap_recv,
        hr_send, hr_recv, hl_send, hl_recv, ns_send, ns_recv, ws_send, ws_recv,
        wx_send, wx_recv, wy_send, wy_recv, wr_send, wr_recv, wl_send, wl_recv,
        dx_send, dx_recv, dy_send, dy_recv, rk_send, rk_recv, rv_send, rv_recv,
        as_send, as_recv, zr_send, zr_recv, zl_send, zl_recv,
        ox_send, ox_recv, oy_send, oy_recv, ou_send, ou_recv, op_send, op_recv,
    ) = refs
    rows, width = hidden.shape
    pairs = weights.shape[0]
    depth = nrm.shape[2]
    lanes = weights.shape[-1]
    tile_rows = key_w.shape[0]
    blocks = 4
    block_rows = rows // blocks
    head_width = lanes // 2
    half_cols = pairs * lanes
    subs = 2 * pairs
    tok, mdl = lax.axis_index("tok"), lax.axis_index("mdl")
    chip, core = tok // 2, tok % 2
    other = 1 - core
    x_chip, y_chip, far_chip = chip + 1 - 2 * (chip % 2), (chip + 2) % 4, 3 - chip
    sibling = {"tok": chip * 2 + other, "mdl": mdl}
    x_dev = {"tok": x_chip * 2 + core, "mdl": mdl}
    y_dev = {"tok": y_chip * 2 + core, "mdl": mdl}
    remote = pltpu.make_async_remote_copy

    barrier = pltpu.get_barrier_semaphore()
    for device in (sibling, x_dev, y_dev):
        pl.semaphore_signal(barrier, inc=1, device_id=device)
    for side in (1, n_mdl - 1):
        pl.semaphore_signal(barrier, inc=1, device_id={"tok": tok, "mdl": (mdl + side) % n_mdl})

    own_hidden = pltpu.make_async_copy(hidden, hid.at[mdl], load_sem.at[0])
    own_hidden.start()
    own_out = pltpu.make_async_copy(out_w, wout.at[chip, core], load_sem.at[1])

    def columns(side, p):
        return pl.ds(pl.multiple_of(side * half_cols + p * lanes, lanes), lanes)

    projections = (key_w, value_w, query_w)
    own_tiles, swap_tiles = [], []
    for p in range(pairs):
        for m in range(3):
            number = 3 * p + m
            own_tiles.append(
                pltpu.make_async_copy(
                    projections[m].at[:, columns(core, p)],
                    weights.at[p, m, chip, core],
                    tile_sem.at[number],
                )
            )
            own_tiles[-1].start()
            swap_tiles.append(
                remote(
                    src_ref=projections[m].at[:, columns(other, p)],
                    dst_ref=weights.at[p, m, chip, core],
                    send_sem=ws_send.at[number], recv_sem=ws_recv.at[number], device_id=sibling,
                )
            )

    pl.semaphore_wait(barrier, 5)

    def copy(block, sends, recvs, index, device, target=None):
        return remote(
            src_ref=block, dst_ref=block if target is None else target,
            send_sem=sends.at[index], recv_sem=recvs.at[index], device_id=device,
        )

    def half_of(s):
        return (core + s) % 2

    def block_of(r):
        return pl.ds(r * block_rows, block_rows)

    def hidden_right(r, step):
        target = hid.at[mdl - step, block_of(r)]
        return copy(
            target if step else hidden.at[block_of(r)],
            hr_send, hr_recv, r * (n_mdl - 1) + step, {"tok": tok, "mdl": mdl + 1}, target,
        )

    def hidden_left(r, step):
        target = hid.at[mdl + step, block_of(r)]
        return copy(
            target if step else hidden.at[block_of(r)],
            hl_send, hl_recv, r * (n_mdl - 1) + step, {"tok": tok, "mdl": mdl - 1}, target,
        )

    def swap_normed(r):
        return copy(nrm.at[core, block_of(r)], ns_send, ns_recv, r, sibling)

    swap_turns = copy(cs.at[core], swap_send, swap_recv, 0, sibling)

    def weight_x(s):
        return copy(weights.at[s // 2, :, chip, half_of(s)], wx_send, wx_recv, s, x_dev)

    def weight_y(s):
        return copy(weights.at[s // 2, :, chip, half_of(s)], wy_send, wy_recv, s, y_dev)

    upper, lower = pl.ds(0, tile_rows // 2), pl.ds(tile_rows // 2, tile_rows // 2)

    def weight_relay_y(s):
        return copy(
            weights.at[s // 2, :, x_chip, half_of(s), upper], wr_send, wr_recv, s, y_dev
        )

    def weight_relay_x(s):
        return copy(
            weights.at[s // 2, :, y_chip, half_of(s), lower], wl_send, wl_recv, s, x_dev
        )

    near, away = pl.ds(0, rows // 2), pl.ds(rows // 2, rows // 2)

    def direct_x(s, k):
        return copy(kv.at[s, chip, half_of(k)], dx_send, dx_recv, 2 * s + k, x_dev)

    def direct_y(s, k):
        return copy(kv.at[s, chip, half_of(k)], dy_send, dy_recv, 2 * s + k, y_dev)

    def relay_y(s, k):
        return copy(kv.at[s, x_chip, half_of(k), near], rk_send, rk_recv, 2 * s + k, y_dev)

    def relay_x(s, k):
        return copy(kv.at[s, y_chip, half_of(k), away], rv_send, rv_recv, 2 * s + k, x_dev)

    def direct_start(s, k):
        direct_x(s, k).start()
        direct_y(s, k).start()

    def direct_event(s, k):
        direct_x(s, k).wait_recv()
        direct_y(s, k).wait_recv()
        relay_y(s, k).start()
        relay_x(s, k).start()

    def swap_att(s):
        return copy(att_send.at[s], as_send, as_recv, s, sibling, att_in.at[s])

    def z_index(s, step):
        return s * (n_mdl - 1) + step

    def z_right(s, step):
        return copy(
            att.at[mdl - step, s], zr_send, zr_recv, z_index(s, step), {"tok": tok, "mdl": mdl + 1}
        )

    def z_left(s, step):
        return copy(
            att.at[mdl + step, s], zl_send, zl_recv, z_index(s, step), {"tok": tok, "mdl": mdl - 1}
        )

    def last_rows(i):
        return pl.ds(i * (rows // 2), rows // 2)

    def last_right(i, step):
        return copy(
            att.at[mdl - step, subs - 1, last_rows(i)],
            zr_send, zr_recv, z_index(subs - 1 + i, step), {"tok": tok, "mdl": mdl + 1},
        )

    def last_left(i, step):
        return copy(
            att.at[mdl + step, subs - 1, last_rows(i)],
            zl_send, zl_recv, z_index(subs - 1 + i, step), {"tok": tok, "mdl": mdl - 1},
        )

    def line_start(right, left, index, step):
        @pl.when((mdl >= step) & (mdl < n_mdl - 1))
        def _():
            right(index, step).start()

        @pl.when((mdl + step < n_mdl) & (mdl > 0))
        def _():
            left(index, step).start()

    def line_arrive(right, left, index, step):
        @pl.when(mdl >= step + 1)
        def _():
            right(index, step).wait_recv()

        @pl.when(mdl + step + 1 < n_mdl)
        def _():
            left(index, step).wait_recv()

    def line_sent(right, left, index, step):
        @pl.when((mdl >= step) & (mdl < n_mdl - 1))
        def _():
            right(index, step).wait_send()

        @pl.when((mdl + step < n_mdl) & (mdl > 0))
        def _():
            left(index, step).wait_send()

    z_start = functools.partial(line_start, z_right, z_left)
    z_arrive = functools.partial(line_arrive, z_right, z_left)
    z_sent = functools.partial(line_sent, z_right, z_left)
    last_start = functools.partial(line_start, last_right, last_left)
    last_arrive = functools.partial(line_arrive, last_right, last_left)
    last_sent = functools.partial(line_sent, last_right, last_left)
    hidden_start = functools.partial(line_start, hidden_right, hidden_left)
    hidden_arrive = functools.partial(line_arrive, hidden_right, hidden_left)
    hidden_sent = functools.partial(line_sent, hidden_right, hidden_left)

    pieces = 4
    piece_rows = tile_rows // pieces

    def piece(i):
        return pl.ds(i * piece_rows, piece_rows)

    out_x = [
        copy(out_w.at[piece(i)], ox_send, ox_recv, i, x_dev, wout.at[chip, core, piece(i)])
        for i in range(pieces)
    ]
    out_y = [
        copy(out_w.at[piece(i)], oy_send, oy_recv, i, y_dev, wout.at[chip, core, piece(i)])
        for i in range(pieces)
    ]
    out_relay = [
        copy(
            wout.at[x_chip if i < pieces // 2 else y_chip, core, piece(i)],
            ou_send, ou_recv, i, y_dev if i < pieces // 2 else x_dev,
        )
        for i in range(pieces)
    ]
    out_pass = [
        copy(out_w, op_send, op_recv, 0, sibling, wout.at[chip, core]),
        copy(wout.at[x_chip, core], op_send, op_recv, 1, sibling),
        copy(wout.at[y_chip, core], op_send, op_recv, 2, sibling),
        copy(wout.at[far_chip, core], op_send, op_recv, 3, sibling),
    ]

    for r in range(blocks):
        hidden_start(r, 0)

    def send_weights(s):
        if s % 2 == 0:
            for one in own_tiles[3 * (s // 2) : 3 * (s // 2) + 3]:
                one.wait()
        else:
            for one in swap_tiles[3 * (s // 2) : 3 * (s // 2) + 3]:
                one.wait_recv()
        weight_x(s).start()
        weight_y(s).start()

    for one in swap_tiles[:3]:
        one.start()
    send_weights(0)
    for one in swap_tiles[3:]:
        one.start()
    own_out.start()
    send_weights(1)

    def weight_event(s):
        weight_x(s).wait_recv()
        weight_y(s).wait_recv()
        weight_relay_y(s).start()
        weight_relay_x(s).start()
        if s + 2 < subs:
            send_weights(s + 2)

    lane = lax.broadcasted_iota(jnp.int32, (1, lanes), 1)
    first = lane < head_width
    early = lane % head_width < head_width // 2
    spot = lane % head_width
    bound = TEXT + lengths[0]

    def request_terms(start, count, same, differs):
        ids = start + lax.broadcasted_iota(jnp.int32, (count, lanes), 0)
        later = ids >= bound
        zero_side = jnp.where(later, differs, same)
        one_side = jnp.where(later, same, differs)
        return jnp.where(spot == 0, zero_side, jnp.where(spot == 1, one_side, 0.0))

    def bias_step(index, carry):
        kbias[index] = request_terms(index * rows, rows, 0.0, -16384.0).astype(jnp.bfloat16)
        return carry

    lax.fori_loop(0, total_rows // rows, bias_step, 0)

    def clear(s, carry):
        acc[s] = jnp.zeros(acc.shape[1:], jnp.float32)
        return carry

    lax.fori_loop(0, subs, clear, 0)

    def wide_gain(gain):
        return jnp.concatenate([gain[...], gain[...]], axis=1)

    same_head = (
        lax.broadcasted_iota(jnp.int32, average.shape, 0) // head_width
        == lax.broadcasted_iota(jnp.int32, average.shape, 1) // head_width
    )
    average[...] = jnp.where(same_head, 1.0 / head_width, 0.0).astype(jnp.bfloat16)

    def head_mean(terms):
        high = terms.astype(jnp.bfloat16)
        low = (terms - high.astype(jnp.float32)).astype(jnp.bfloat16)
        return jnp.dot(high, average[...], preferred_element_type=jnp.float32) + jnp.dot(
            low, average[...], preferred_element_type=jnp.float32
        )

    def turned(normal, turns):
        partner = jnp.where(
            early,
            pltpu.roll(normal, lanes - head_width // 2, axis=1),
            pltpu.roll(normal, head_width // 2, axis=1),
        )
        return normal * turns[0] + partner * turns[1]

    quarter = head_width // 2
    pair = lane % quarter
    one_count = quarter // 4
    two_count = (quarter - one_count) // 2
    three_count = quarter - one_count - two_count
    is_one, is_two = pair < one_count, pair < one_count + two_count
    local = pair - jnp.where(is_one, 0, jnp.where(is_two, one_count, one_count + two_count))
    count = jnp.where(is_one, one_count, jnp.where(is_two, two_count, three_count))
    power = local.astype(jnp.float32) / count.astype(jnp.float32)
    rates = jnp.exp(power * -9.210340371976184)
    places = jnp.transpose(
        jnp.concatenate(
            [positions[...].astype(jnp.float32), jnp.zeros((5, rows), jnp.float32)], axis=0
        )
    )
    angles = rates * jnp.where(
        is_one, places[:, 0:1], jnp.where(is_two, places[:, 1:2], places[:, 2:3])
    )

    def textual(start, count):
        ids = tok * rows + start + lax.broadcasted_iota(jnp.int32, (count, 1), 0)
        place = jnp.where(ids >= bound, ids - bound, ids)
        return place < TEXT

    is_text = textual(0, rows)
    cs[core, 0] = jnp.where(is_text, 1.0, jnp.cos(angles))
    sine = jnp.sin(angles)
    cs[core, 1] = jnp.where(is_text, 0.0, jnp.where(early, -sine, sine))
    swap_turns.start()

    def normalize(r):
        wide = jnp.concatenate([hid[z, block_of(r), :] for z in range(n_mdl)], axis=1)
        values_in = wide.astype(jnp.float32)
        center = values_in - jnp.mean(values_in, axis=1, keepdims=True)
        spread = jnp.mean(center * center, axis=1, keepdims=True)
        normal = center * lax.rsqrt(spread + 1e-05)
        text_rows = textual(r * block_rows, block_rows)
        shift = jnp.where(text_rows, modulation[3:4, :], modulation[0:1, :])
        scale = jnp.where(text_rows, modulation[4:5, :], modulation[1:2, :])
        nrm[core, block_of(r), :] = (normal * (1.0 + scale) + shift).astype(jnp.bfloat16)
        swap_normed(r).start()

    def hidden_hop(r, step):
        hidden_arrive(r, step - 1)
        if step < n_mdl - 1:
            hidden_start(r, step)
        else:
            if r == 0:
                own_hidden.wait()
            normalize(r)

    def weight_arrive(s):
        weight_relay_y(s).wait_recv()
        weight_relay_x(s).wait_recv()

    def project(p, half, start, size):
        where = pl.ds(start, size)
        here = pl.ds(pl.multiple_of(half * rows + start, block_rows), size)
        tall = [weights[p, m].reshape(depth, lanes) for m in range(3)]
        summed = jnp.dot(
            nrm[half, where, :], jnp.concatenate(tall, axis=1), preferred_element_type=jnp.float32
        )
        turns = cs[half, 0, where, :], cs[half, 1, where, :]
        both = jnp.concatenate([summed[:, :lanes], summed[:, 2 * lanes :]], axis=1)
        center = both - head_mean(both)
        scaled = wide_gain(query_gain) * (head_width ** (-0.5) * 1.4426950408889634)
        gain = jnp.concatenate([wide_gain(key_gain), scaled], axis=1)
        normal = center * lax.rsqrt(head_mean(center * center) + 1e-06) * gain
        keys = turned(normal[:, :lanes], turns)
        values = pltpu.roll(summed[:, lanes : 2 * lanes], head_width, axis=1)
        kv[2 * p, chip, half, where, :] = jnp.where(first, keys, values).astype(jnp.bfloat16)
        kv[2 * p + 1, chip, half, where, :] = jnp.where(first, values, keys).astype(jnp.bfloat16)
        query = turned(normal[:, lanes:], turns)
        terms = request_terms((chip * 2 + half) * rows + start, size, 0.0, 1.0)
        terms = jnp.where(spot < 2, 1.0 - terms, 0.0)
        qx[2 * p, here, :] = jnp.where(first, query, terms).astype(jnp.bfloat16)
        qx[2 * p + 1, here, :] = jnp.where(first, terms, query).astype(jnp.bfloat16)

    def project_own(p, r, count):
        project(p, core, r * block_rows, count * block_rows)

    def project_other(p, r, count):
        project(p, other, r * block_rows, count * block_rows)

    hidden_hop(0, 1)
    weight_event(0)
    hidden_hop(1, 1)
    hidden_hop(2, 1)
    weight_event(1)
    hidden_hop(3, 1)
    hidden_hop(0, 2)
    weight_event(2)
    hidden_hop(1, 2)
    hidden_hop(2, 2)
    hidden_hop(3, 2)
    weight_event(3)
    for s in range(4):
        weight_arrive(s)
    swap_turns.wait_recv()
    hidden_hop(0, 3)
    project_own(0, 0, 1)
    project_own(1, 0, 1)
    hidden_hop(1, 3)
    weight_event(4)
    swap_normed(0).wait_recv()
    project_own(0, 1, 1)
    project_other(0, 0, 1)
    project_own(1, 1, 1)
    project_other(1, 0, 1)
    hidden_hop(2, 3)
    swap_normed(1).wait_recv()
    project_own(0, 2, 1)
    project_other(0, 1, 1)
    swap_normed(2).wait_recv()
    project_other(0, 2, 1)
    hidden_hop(3, 3)
    project_own(0, 3, 1)
    direct_start(0, 0)
    weight_event(5)
    swap_normed(3).wait_recv()
    project_other(0, 3, 1)
    direct_start(0, 1)
    project_own(1, 2, 2)
    project_other(1, 1, 3)

    most = TEXT + (total_rows - 2 * TEXT) * 5 // 8
    last_first = -(-most // rows)
    first_last = (total_rows - most) // rows

    def needed(row_block, key_block):
        return (
            ((row_block < first_last) & (key_block < last_first))
            | ((row_block >= last_first) & (key_block >= first_last))
            | ((row_block >= first_last) & (row_block < last_first))
        )

    def attend_rows(where, s, source, halves):
        mine = (lane + (s % 2) * head_width) % lanes < head_width
        added = None
        for half in halves:
            block = kv[s, source, half]
            score = lax.dot_general(
                qx[s, where, :],
                jnp.where(mine, block, kbias[source * 2 + half]),
                (((1,), (1,)), ((), ())),
                preferred_element_type=jnp.float32,
            )
            part = jnp.dot(
                jnp.exp2(score).astype(jnp.bfloat16),
                jnp.where(mine, jnp.ones_like(block), block),
                preferred_element_type=jnp.float32,
            )
            added = part if added is None else added + part
        acc[s, where, :] += added

    def attend_block(s, source, r):
        where = pl.ds(pl.multiple_of(r * rows, rows), rows)
        low = needed(chip * 2 + r, source * 2)
        high = needed(chip * 2 + r, source * 2 + 1)

        @pl.when(low & high)
        def _():
            attend_rows(where, s, source, (0, 1))

        @pl.when(low != high)
        def _():
            attend_rows(where, s, source, (jnp.where(low, 0, 1),))

    def attend_unit(s, source):
        row_block, key_block = chip * 2, source * 2
        whole = (
            needed(row_block, key_block)
            & needed(row_block, key_block + 1)
            & needed(row_block + 1, key_block)
            & needed(row_block + 1, key_block + 1)
        )

        @pl.when(whole)
        def _():
            attend_rows(pl.ds(0, 2 * rows), s, source, (0, 1))

        @pl.when(jnp.logical_not(whole))
        def _():
            def one_block(r, inner):
                attend_block(s, source, r)
                return inner

            lax.fori_loop(0, 2, one_block, 0)

    def finish_head(s):
        moved = (s + 1) % 2 != core

        def one_side(turn, inner):
            r = jnp.where(turn == 0, other, core)
            attend_block(s, far_chip, r)
            both = acc[s, pl.ds(pl.multiple_of(r * rows, rows), rows), :]
            ratio = both / pltpu.roll(both, head_width, axis=1)
            ratio = jnp.where(moved, pltpu.roll(ratio, head_width, axis=1), ratio)
            ratio = ratio.astype(jnp.bfloat16)

            @pl.when(turn == 0)
            def _():
                att_send[s] = ratio
                swap_att(s).start()

            @pl.when(turn == 1)
            def _():
                swap_att(s).wait_recv()
                att[mdl, s] = jnp.where(lane // head_width == core, ratio, att_in[s])

            return inner

        lax.fori_loop(0, 2, one_side, 0)

    def pass_on(s, step):
        z_arrive(s, step - 1)
        z_start(s, step)

    final = subs - 1

    def turn(s, carry):
        direct_event(s, 0)

        def visit(j, inner):
            source = jnp.where(j == 0, chip, jnp.where(j == 1, x_chip, y_chip))

            @pl.when(j == 1)
            def _():
                direct_event(s, 1)

                @pl.when(s < final)
                def _():
                    direct_start(s + 1, 0)
                    direct_start(s + 1, 1)

                @pl.when(s == final)
                def _():
                    for i in range(pieces):
                        out_x[i].start()
                        out_y[i].start()
                    out_pass[0].start()

            @pl.when((j == 2) & (s >= 1))
            def _():
                pass_on(s - 1, 1)

            attend_unit(s, source)
            return inner

        lax.fori_loop(0, 3, visit, 0)
        for k in range(2):
            relay_y(s, k).wait_recv()
            relay_x(s, k).wait_recv()
        finish_head(s)

        @pl.when(s < final)
        def _():
            z_start(s, 0)

        @pl.when(s == final)
        def _():
            last_start(0, 0)
            last_start(1, 0)

        @pl.when(s >= 1)
        def _():
            pass_on(s - 1, 2)

        @pl.when(s < 2)
        def _():
            @pl.when(s == 0)
            def _():
                weight_arrive(4)
                weight_arrive(5)

            project(pairs - 1, half_of(s), 0, rows)

        return carry

    lax.fori_loop(0, subs, turn, 0)

    def out_event(i):
        out_x[i].wait_recv()
        out_y[i].wait_recv()
        out_relay[i].start()

    def last_on(i, step):
        last_arrive(i, step - 1)
        last_start(i, step)

    out_event(0)
    out_event(1)
    last_on(0, 1)
    last_on(1, 1)
    out_event(2)
    last_on(0, 2)
    out_event(3)
    last_on(1, 2)
    out_pass[1].start()
    out_pass[2].start()
    own_out.wait()

    def combine(block):
        tall = [
            wout[block, side, s * head_width : (s + 1) * head_width, :]
            for s in range(subs)
            for side in range(2)
        ]
        return jnp.dot(
            jnp.concatenate([att[block, s] for s in range(subs)], axis=1),
            jnp.concatenate(tall, axis=0),
            preferred_element_type=jnp.float32,
        )

    for s in range(final):
        z_arrive(s, n_mdl - 2)
    for i in range(2):
        last_arrive(i, n_mdl - 2)
    out_pass[0].wait_recv()
    out_acc[...] = combine(chip)
    out_pass[1].wait_recv()
    out_acc[...] += combine(x_chip)
    out_pass[2].wait_recv()
    out_acc[...] += combine(y_chip)
    for one in out_relay:
        one.wait_recv()
    out_pass[3].start()
    out_pass[3].wait_recv()
    projected = out_acc[...] + combine(far_chip)
    own_columns = pl.ds(pl.multiple_of(mdl * width, lanes), width)
    gate = jnp.where(is_text, modulation[5:6, own_columns], modulation[2:3, own_columns])
    result[...] = (hid[mdl].astype(jnp.float32) + gate * projected).astype(jnp.bfloat16)

    swap_turns.wait_send()
    for r in range(blocks):
        swap_normed(r).wait_send()
        for step in range(n_mdl - 1):
            hidden_sent(r, step)
    for one in swap_tiles:
        one.wait_send()
    for s in range(subs):
        weight_x(s).wait_send()
        weight_y(s).wait_send()
        weight_relay_y(s).wait_send()
        weight_relay_x(s).wait_send()
        for k in range(2):
            direct_x(s, k).wait_send()
            direct_y(s, k).wait_send()
            relay_y(s, k).wait_send()
            relay_x(s, k).wait_send()
        swap_att(s).wait_send()
    for step in range(n_mdl - 1):
        for s in range(final):
            z_sent(s, step)
        for i in range(2):
            last_sent(i, step)
    for one in out_x + out_y + out_relay + out_pass:
        one.wait_send()


def fused(
    mesh, lengths, hidden, positions, modulation, weights, out_weight, gains, collective_id
):
    n_tok, n_mdl = mesh.shape["tok"], mesh.shape["mdl"]
    rows, width = hidden.shape
    depth = width * n_mdl
    lanes = 2 * gains[0].shape[1]
    pairs = width // (2 * lanes)
    total_rows = rows * n_tok
    chips = n_tok // 2
    subs = 2 * pairs
    blocks = 4
    bf, f32 = jnp.bfloat16, jnp.float32
    anywhere = pl.BlockSpec(memory_space=pl.ANY)
    inside = pl.BlockSpec(memory_space=pltpu.VMEM)

    def sems(count):
        return [pltpu.SemaphoreType.DMA((count,))]

    return pl.pallas_call(
        functools.partial(fused_kernel, n_mdl, total_rows),
        out_shape=jax.ShapeDtypeStruct((rows, width), bf),
        in_specs=[pl.BlockSpec(memory_space=pltpu.SMEM), anywhere]
        + [inside] * 2
        + [anywhere] * 4
        + [inside] * 2,
        out_specs=inside,
        scratch_shapes=[
            pltpu.VMEM((n_mdl, rows, width), bf),
            pltpu.VMEM((2, rows, depth), bf),
            pltpu.VMEM((2, 2, rows, lanes), f32),
            pltpu.VMEM((pairs, 3, chips, 2, out_weight.shape[0], lanes), bf),
            pltpu.VMEM((2 * pairs, 2 * rows, lanes), bf),
            pltpu.VMEM((subs, chips, 2, rows, lanes), bf),
            pltpu.VMEM((n_tok, rows, lanes), bf),
            pltpu.VMEM((subs, 2 * rows, lanes), f32),
            pltpu.VMEM((n_mdl, subs, rows, lanes), bf),
            pltpu.VMEM((subs, rows, lanes), bf),
            pltpu.VMEM((subs, rows, lanes), bf),
            pltpu.VMEM((chips, 2) + out_weight.shape, bf),
            pltpu.VMEM((rows, width), f32),
            pltpu.VMEM((2 * lanes, 2 * lanes), bf),
        ]
        + sems(2)
        + sems(3 * pairs)
        + sems(1) * 2
        + sems(blocks * (n_mdl - 1)) * 4
        + sems(blocks) * 2
        + sems(3 * pairs) * 2
        + sems(subs) * 8
        + sems(2 * subs) * 8
        + sems(subs) * 2
        + sems((subs + 1) * (n_mdl - 1)) * 4
        + sems(4) * 8,
        compiler_params=pltpu.CompilerParams(
            collective_id=collective_id, has_side_effects=True, vmem_limit_bytes=60 * 2**20
        ),
        name="fused",
    )(lengths, hidden, positions, modulation, *weights, out_weight, *gains)


def shards(
    mesh,
    hidden_states,
    lengths,
    positions,
    modulation,
    query_weight,
    key_weight,
    value_weight,
    out_weight,
    query_gain,
    key_gain,
):
    own_rows = hidden_states.shape[0]
    head_width = query_gain.shape[0]
    if mesh.shape["tok"] == 8 and mesh.shape["mdl"] == 4:
        return fused(
            mesh,
            lengths,
            hidden_states,
            positions,
            modulation,
            (key_weight, value_weight, query_weight),
            out_weight,
            [gain[None, :] for gain in (key_gain, query_gain)],
            0,
        )
    full_rows = lax.all_gather(hidden_states, "mdl", axis=1, tiled=True)
    key_full, value_full, query_full = gather_all(
        mesh, [key_weight, value_weight, query_weight], [], 0
    )
    row_index = lax.axis_index("tok") * own_rows + jnp.arange(own_rows, dtype=jnp.int32)
    request, is_text, bound = token_labels(row_index, lengths)
    normed = modulate(full_rows, modulation, is_text)
    angles = pair_angles(positions, head_width // 2)
    textual = is_text[:, None]
    cosine = jnp.tile(jnp.where(textual, 1.0, jnp.cos(angles)), (1, 4))
    sine = jnp.where(textual, 0.0, jnp.sin(angles))
    sine = jnp.tile(jnp.concatenate([-sine, sine], axis=1), (1, 2))
    keys, values, query_flat = project_and_gather(
        mesh,
        normed,
        (key_full, value_full, query_full),
        [jnp.tile(gain, 2)[None, :] for gain in (key_gain, query_gain)],
        cosine,
        sine,
        head_width,
        1,
    )
    first_row = lax.axis_index("tok") * own_rows
    first, second = (
        attend(query_flat, keys, values, bound, first_row, head_width, part, 2)
        for part in range(2)
    )
    first_heads = lax.all_gather(first, "mdl", axis=1, tiled=True)
    out_full, second_heads = gather_all(mesh, [out_weight], [second], 2)
    out_width = out_weight.shape[1]
    projected = jnp.concatenate(
        [
            jnp.dot(heads, out_full, preferred_element_type=jnp.float32)
            for heads in (first_heads, second_heads)
        ],
        axis=0,
    )
    gate_rows = lax.dynamic_slice_in_dim(
        modulation, lax.axis_index("mdl") * out_width, out_width, 1
    )
    gate = jnp.where(is_text[:, None], gate_rows[5][None, :], gate_rows[2][None, :])
    return (hidden_states.astype(jnp.float32) + gate * projected).astype(jnp.bfloat16)


def solution(mesh):
    return jax.shard_map(
        functools.partial(shards, mesh),
        mesh=mesh,
        in_specs=(
            P("tok", "mdl"),
            P(),
            P(None, "tok"),
            P(),
            P("tok", "mdl"),
            P("tok", "mdl"),
            P("tok", "mdl"),
            P("tok", "mdl"),
            P(),
            P(),
        ),
        out_specs=P("tok", "mdl"),
        check_vma=False,
    )
```

```python
import functools
import jax
import jax.numpy as jnp
from jax import lax
from jax.experimental import pallas as pl
from jax.experimental.pallas import tpu as pltpu
from jax.sharding import PartitionSpec as P

TEXT = 226


def token_labels(row_index, lengths):
    bound = TEXT + lengths[0]
    request = (row_index >= bound).astype(jnp.int32)
    place = row_index - request * bound
    return (request, place < TEXT, bound)


def modulate(rows_bf, modulation, is_text):
    values = rows_bf.astype(jnp.float32)
    center = values - jnp.mean(values, axis=1, keepdims=True)
    spread = jnp.mean(center * center, axis=1, keepdims=True)
    normal = center * lax.rsqrt(spread + 1e-05)
    textual = is_text[:, None]
    shift = jnp.where(textual, modulation[3][None, :], modulation[0][None, :])
    scale = jnp.where(textual, modulation[4][None, :], modulation[1][None, :])
    return (normal * (1.0 + scale) + shift).astype(jnp.bfloat16)


def pair_angles(positions, pairs):
    index = jnp.arange(pairs, dtype=jnp.int32)
    first = pairs // 4
    second = (pairs - first) // 2
    third = pairs - first - second
    component = jnp.where(index < first, 0, jnp.where(index < first + second, 1, 2))
    local = index - jnp.where(component == 0, 0, jnp.where(component == 1, first, first + second))
    count = jnp.where(component == 0, first, jnp.where(component == 1, second, third))
    rates = jnp.power(jnp.float32(10000.0), -local.astype(jnp.float32) / count.astype(jnp.float32))
    places = positions.astype(jnp.float32)
    chosen = jnp.where(
        component[:, None] == 0,
        places[0][None, :],
        jnp.where(component[:, None] == 1, places[1][None, :], places[2][None, :]),
    )
    return jnp.transpose(chosen * rates[:, None])


def gather_kernel(n_tok, n_mdl, n_row, n_col, *refs):
    count = n_row + n_col
    ins, outs = refs[:count], refs[count : 2 * count]
    exchange(
        n_tok, n_mdl, ins[:n_row], ins[n_row:], outs[:n_row], outs[n_row:], refs[2 * count :]
    )


def exchange(
    n_tok, n_mdl, rows_in, cols_in, rows_out, cols_out, semaphores, prepare=None, between=None
):
    n_row, n_col = len(rows_in), len(cols_in)
    (
        local_sem,
        send1,
        recv1,
        send2,
        recv2,
        send3,
        recv3,
        to_right,
        from_left,
        to_left,
        from_right,
    ) = semaphores
    square = n_tok == 8
    chips = n_tok // 2
    tok, mdl = lax.axis_index("tok"), lax.axis_index("mdl")
    chip, core = tok // 2, tok % 2
    sibling = chip * 2 + 1 - core

    def chip_at(step):
        if square:
            return (chip, chip + 1 - 2 * (chip % 2), (chip + 2) % 4, 3 - chip)[step]
        return (chip + step) % chips

    def source_at(step):
        return chip_at(step) if square else chip_at(chips - step)

    barrier = pltpu.get_barrier_semaphore()
    greeted = 0
    if n_row:
        for step in (1, 2) if square else range(1, chips):
            pl.semaphore_signal(
                barrier, inc=1, device_id={"tok": chip_at(step) * 2 + core, "mdl": mdl}
            )
            greeted += 1
        pl.semaphore_signal(barrier, inc=1, device_id={"tok": sibling, "mdl": mdl})
        greeted += 1
    if n_col:
        for side in (1, n_mdl - 1):
            pl.semaphore_signal(
                barrier, inc=1, device_id={"tok": tok, "mdl": (mdl + side) % n_mdl}
            )
            greeted += 1
    pl.semaphore_wait(barrier, greeted)

    def row_block(number, owner):
        size = rows_in[number].shape[0]
        return rows_out[number].at[pl.ds(pl.multiple_of(owner * size, size), size), :]

    def col_block(number, owner):
        size = cols_in[number].shape[1]
        return cols_out[number].at[:, pl.ds(pl.multiple_of(owner * size, size), size)]

    def direct(number, step):
        target = chip_at(step) * 2 + core if step else sibling
        return pltpu.make_async_remote_copy(
            src_ref=rows_in[number],
            dst_ref=row_block(number, tok),
            send_sem=send1.at[number, step],
            recv_sem=recv1.at[number, step],
            device_id={"tok": target, "mdl": mdl},
        )

    def passed(number, step):
        block = row_block(number, source_at(step) * 2 + core)
        return pltpu.make_async_remote_copy(
            src_ref=block,
            dst_ref=block,
            send_sem=send2.at[number, step],
            recv_sem=recv2.at[number, step],
            device_id={"tok": sibling, "mdl": mdl},
        )

    def relayed(number, step):
        half = rows_in[number].shape[0] // 2
        first = (source_at(step) * 2 + core) * 2 * half + (step - 1) * half
        block = rows_out[number].at[pl.ds(pl.multiple_of(first, half), half), :]
        return pltpu.make_async_remote_copy(
            src_ref=block,
            dst_ref=block,
            send_sem=send3.at[number, step],
            recv_sem=recv3.at[number, step],
            device_id={"tok": chip_at(3 - step) * 2 + core, "mdl": mdl},
        )

    directs = (1, 2) if square else range(1, chips)

    def rightward(number, step):
        block = col_block(number, mdl - step)
        return pltpu.make_async_remote_copy(
            src_ref=block if step else cols_in[number],
            dst_ref=block,
            send_sem=to_right.at[number, step],
            recv_sem=from_left.at[number, step],
            device_id={"tok": tok, "mdl": mdl + 1},
        )

    def leftward(number, step):
        block = col_block(number, mdl + step)
        return pltpu.make_async_remote_copy(
            src_ref=block if step else cols_in[number],
            dst_ref=block,
            send_sem=to_left.at[number, step],
            recv_sem=from_right.at[number, step],
            device_id={"tok": tok, "mdl": mdl - 1},
        )

    def right_if(step):
        return (mdl >= step) & (mdl < n_mdl - 1)

    def left_if(step):
        return (mdl + step < n_mdl) & (mdl > 0)

    for number in range(n_col):
        @pl.when(right_if(0))
        def _():
            rightward(number, 0).start()

        @pl.when(left_if(0))
        def _():
            leftward(number, 0).start()

    locals_ = []
    for number in range(n_col):
        locals_.append(
            pltpu.make_async_copy(
                cols_in[number], col_block(number, mdl), local_sem.at[n_row + number]
            )
        )
        locals_[-1].start()
    for number in range(n_row):
        if prepare is not None:
            prepare(number)
        for step in directs:
            direct(number, step).start()
        direct(number, 0).start()
        locals_.append(
            pltpu.make_async_copy(rows_in[number], row_block(number, tok), local_sem.at[number])
        )
        locals_[-1].start()

    def finish_diagonal(number):
        for step in (1, 2):
            relayed(number, step).wait_recv()
        passed(number, 3).start()

    for turn in range(max(n_row, n_mdl - 2 if n_col else 0)):
        hop = turn + 1
        if hop < n_mdl - 1:
            for number in range(n_col):
                @pl.when(mdl >= hop)
                def _():
                    rightward(number, hop - 1).wait_recv()

                @pl.when(right_if(hop))
                def _():
                    rightward(number, hop).start()

                @pl.when(mdl + hop < n_mdl)
                def _():
                    leftward(number, hop - 1).wait_recv()

                @pl.when(left_if(hop))
                def _():
                    leftward(number, hop).start()

        if turn < n_row:
            for step in directs:
                direct(turn, step).wait_recv()
                if square:
                    relayed(turn, step).start()
                passed(turn, step).start()
            if square and turn > 0:
                finish_diagonal(turn - 1)
        if between is not None:
            between(turn)

    if square and n_row:
        finish_diagonal(n_row - 1)
    for copy in locals_:
        copy.wait()
    for number in range(n_col):
        @pl.when(mdl >= n_mdl - 1)
        def _():
            rightward(number, n_mdl - 2).wait_recv()

        @pl.when(mdl + n_mdl - 1 < n_mdl)
        def _():
            leftward(number, n_mdl - 2).wait_recv()

    for number in range(n_row):
        direct(number, 0).wait()
        for step in directs:
            direct(number, step).wait_send()
            if square:
                relayed(number, step).wait_send()
        for step in range(1, chips):
            passed(number, step).wait()
    for number in range(n_col):
        for step in range(n_mdl - 1):
            @pl.when(right_if(step))
            def _():
                rightward(number, step).wait_send()

            @pl.when(left_if(step))
            def _():
                leftward(number, step).wait_send()


def exchange_semaphores(n_tok, n_mdl, n_row, n_col):
    row_sem = pltpu.SemaphoreType.DMA((max(n_row, 1), n_tok // 2))
    col_sem = pltpu.SemaphoreType.DMA((max(n_col, 1), n_mdl))
    return [pltpu.SemaphoreType.DMA((n_row + n_col,))] + [row_sem] * 6 + [col_sem] * 4


def project_kernel(n_tok, n_mdl, head_width, *refs):
    normed, key_w, value_w, query_w, key_gain, query_gain, cosine, sine = refs[:8]
    keys_out, values_out, query_out = refs[8:11]
    keys, values, query, key_held, value_held, query_held, load_sem = refs[11:18]
    width = keys.shape[1]
    lanes = 2 * head_width
    block = 256 if width % 256 == 0 else lanes
    loads = [
        pltpu.make_async_copy(source, held, load_sem.at[number])
        for number, (source, held) in enumerate(
            ((key_w, key_held), (value_w, value_held), (query_w, query_held))
        )
    ]
    for load in loads:
        load.start()
    lane = lax.broadcasted_iota(jnp.int32, (1, lanes), 1)
    first = lane < head_width
    early = lane % head_width < head_width // 2

    def head_mean(terms):
        one = jnp.sum(jnp.where(first, terms, 0.0), axis=1, keepdims=True)
        other = jnp.sum(jnp.where(first, 0.0, terms), axis=1, keepdims=True)
        return jnp.where(first, one, other) * (1.0 / head_width)

    def finished(summed, gain):
        center = summed - head_mean(summed)
        normal = center * lax.rsqrt(head_mean(center * center) + 1e-06) * gain[...]
        partner = jnp.where(
            early,
            pltpu.roll(normal, lanes - head_width // 2, axis=1),
            pltpu.roll(normal, head_width // 2, axis=1),
        )
        return normal * cosine[...] + partner * sine[...]

    def project(held, gain, target):
        def step(number, carry):
            columns = pl.ds(pl.multiple_of(number * block, block), block)
            summed = jnp.dot(
                normed[...], held[:, columns], preferred_element_type=jnp.float32
            )
            if gain is not None:
                summed = jnp.concatenate(
                    [
                        finished(summed[:, start : start + lanes], gain)
                        for start in range(0, block, lanes)
                    ],
                    axis=1,
                )
            target[:, columns] = summed.astype(jnp.bfloat16)
            return carry

        lax.fori_loop(0, width // block, step, 0)

    def prepare(number):
        loads[number].wait()
        if number == 0:
            project(key_held, key_gain, keys)
        else:
            project(value_held, None, values)

    query_copy = pltpu.make_async_copy(query, query_out, load_sem.at[3])

    def between(turn):
        if turn == 0:
            loads[2].wait()
            project(query_held, query_gain, query)
            query_copy.start()

    exchange(
        n_tok,
        n_mdl,
        (keys, values),
        (),
        (keys_out, values_out),
        (),
        refs[18:],
        prepare,
        between,
    )
    query_copy.wait()


def project_and_gather(mesh, normed, weights, gains, cosine, sine, head_width, collective_id):
    n_tok, n_mdl = mesh.shape["tok"], mesh.shape["mdl"]
    own_rows, depth = normed.shape
    width = weights[0].shape[1]
    full = jax.ShapeDtypeStruct((own_rows * n_tok, width), jnp.bfloat16)
    own = jax.ShapeDtypeStruct((own_rows, width), jnp.bfloat16)
    anywhere = pl.BlockSpec(memory_space=pl.ANY)
    inside = pl.BlockSpec(memory_space=pltpu.VMEM)
    return pl.pallas_call(
        functools.partial(project_kernel, n_tok, n_mdl, head_width),
        out_shape=[full, full, own],
        in_specs=[inside] + [anywhere] * 3 + [inside] * 4,
        out_specs=[anywhere] * 3,
        scratch_shapes=[pltpu.VMEM((own_rows, width), jnp.bfloat16)] * 3
        + [pltpu.VMEM((depth, width), jnp.bfloat16)] * 3
        + [pltpu.SemaphoreType.DMA((4,))]
        + exchange_semaphores(n_tok, n_mdl, 2, 0),
        compiler_params=pltpu.CompilerParams(
            collective_id=collective_id, has_side_effects=True, vmem_limit_bytes=48 * 2**20
        ),
        name="project_and_gather",
    )(normed, *weights, *gains, cosine, sine)


def gather_all(mesh, over_tok, over_mdl, collective_id):
    n_tok, n_mdl = mesh.shape["tok"], mesh.shape["mdl"]
    n_row, n_col = len(over_tok), len(over_mdl)
    shapes = [
        jax.ShapeDtypeStruct((one.shape[0] * n_tok, one.shape[1]), one.dtype) for one in over_tok
    ] + [jax.ShapeDtypeStruct((one.shape[0], one.shape[1] * n_mdl), one.dtype) for one in over_mdl]
    return pl.pallas_call(
        functools.partial(gather_kernel, n_tok, n_mdl, n_row, n_col),
        out_shape=shapes,
        in_specs=[pl.BlockSpec(memory_space=pl.ANY)] * (n_row + n_col),
        out_specs=[pl.BlockSpec(memory_space=pl.ANY)] * (n_row + n_col),
        scratch_shapes=exchange_semaphores(n_tok, n_mdl, n_row, n_col),
        compiler_params=pltpu.CompilerParams(collective_id=collective_id, has_side_effects=True),
        name=f"gather_{collective_id}",
    )(*over_tok, *over_mdl)


def attend_kernel(rows_at_once, keys_at_once, head_width, meta_ref, q_ref, k_ref, v_ref, o_ref):
    bound, first_row = meta_ref[0], meta_ref[1]
    own_rows, lanes = q_ref.shape
    count = k_ref.shape[0]
    chunks = count // keys_at_once
    per = lanes // head_width
    lane = lax.broadcasted_iota(jnp.int32, (1, lanes), 1) // head_width
    masks = [(lane == head).astype(jnp.float32) for head in range(per)]
    edge = bound // keys_at_once
    edge_start = pl.multiple_of(edge * keys_at_once, keys_at_once)
    edge_keys = edge_start + lax.broadcasted_iota(jnp.int32, (keys_at_once, 1), 0)

    for block in range(own_rows // rows_at_once):
        rows = pl.ds(block * rows_at_once, rows_at_once)
        start = first_row + block * rows_at_once
        row_ids = start + lax.broadcasted_iota(jnp.int32, (rows_at_once, 1), 0)

        def add_chunk(carry, keys, values):
            queries = q_ref[rows, :]
            result = []
            for head in range(per):
                mine = queries * (masks[head] * head_width ** (-0.5)).astype(jnp.bfloat16)
                score = lax.dot_general(
                    mine, keys, (((1,), (1,)), ((), ())), preferred_element_type=jnp.float32
                )
                expo = jnp.exp(score).astype(jnp.bfloat16)
                result.append(
                    carry[head]
                    + jnp.dot(expo, values[head], preferred_element_type=jnp.float32)
                )
            return tuple(result)

        def inner(chunk, carry):
            here = pl.ds(pl.multiple_of(chunk * keys_at_once, keys_at_once), keys_at_once)
            values = v_ref[here, :]
            with_ones = [
                values * mask.astype(jnp.bfloat16) + (1.0 - mask).astype(jnp.bfloat16)
                for mask in masks
            ]
            return add_chunk(carry, k_ref[here, :], with_ones)

        for request in range(2):
            active = start < bound if request == 0 else start + rows_at_once > bound

            @pl.when(active)
            def _():
                here = pl.ds(edge_start, keys_at_once)
                inside = edge_keys < bound if request == 0 else edge_keys >= bound
                wide = v_ref[here, :].astype(jnp.float32)
                with_ones = [
                    jnp.where(inside, wide * mask + (1.0 - mask), 0.0).astype(jnp.bfloat16)
                    for mask in masks
                ]
                zero = jnp.zeros((rows_at_once, lanes), jnp.float32)
                carry = add_chunk((zero,) * per, k_ref[here, :], with_ones)
                if request == 0:
                    low, high = 0, edge
                else:
                    low, high = edge + 1, chunks
                carry = lax.fori_loop(low, high, inner, carry)
                output = zero
                for head in range(per):
                    total = pltpu.roll(carry[head], head_width, axis=1)
                    output = jnp.where(lane == head, carry[head] / total, output)
                if request == 0:
                    o_ref[rows, :] = output.astype(o_ref.dtype)
                else:
                    old = o_ref[rows, :].astype(jnp.float32)
                    o_ref[rows, :] = jnp.where(row_ids >= bound, output, old).astype(o_ref.dtype)


def attend(query, keys, values, bound, first_row, head_width, part, parts):
    width = query.shape[1]
    own_rows = query.shape[0] // parts
    count = keys.shape[0]
    lanes = 2 * head_width
    meta = jnp.stack([bound, first_row + part * own_rows]).astype(jnp.int32)
    block = pl.BlockSpec((own_rows, lanes), lambda pair, meta: (part, pair))
    out_block = pl.BlockSpec((own_rows, lanes), lambda pair, meta: (0, pair))
    full = pl.BlockSpec((count, lanes), lambda pair, meta: (0, pair))
    return pl.pallas_call(
        functools.partial(attend_kernel, 256, 512, head_width),
        out_shape=jax.ShapeDtypeStruct((own_rows, width), jnp.bfloat16),
        grid_spec=pltpu.PrefetchScalarGridSpec(
            num_scalar_prefetch=1,
            grid=(width // lanes,),
            in_specs=[block, full, full],
            out_specs=out_block,
        ),
        compiler_params=pltpu.CompilerParams(vmem_limit_bytes=58 * 2**20),
        cost_estimate=pl.CostEstimate(
            flops=4 * own_rows * count * width,
            bytes_accessed=4 * count * width,
            transcendentals=own_rows * count * width // head_width,
        ),
        name=f"attend_{part}",
    )(meta, query, keys, values)

def fused_kernel(n_mdl, total_rows, *refs):
    (
        lengths, hidden, positions, modulation, key_w, value_w, query_w, out_w, key_gain, query_gain,
        result,
        hid, nrm, cs, weights, qx, kv, kbias, acc, att, att_send, att_in, wout, out_acc, average,
        load_sem, tile_sem, swap_send, swap_recv,
        hr_send, hr_recv, hl_send, hl_recv, ns_send, ns_recv, ws_send, ws_recv,
        wx_send, wx_recv, wy_send, wy_recv, wr_send, wr_recv, wl_send, wl_recv,
        dx_send, dx_recv, dy_send, dy_recv, rk_send, rk_recv, rv_send, rv_recv,
        as_send, as_recv, zr_send, zr_recv, zl_send, zl_recv,
        ox_send, ox_recv, oy_send, oy_recv, ou_send, ou_recv, op_send, op_recv,
    ) = refs
    rows, width = hidden.shape
    pairs = weights.shape[0]
    depth = nrm.shape[2]
    lanes = weights.shape[-1]
    tile_rows = key_w.shape[0]
    blocks = 4
    block_rows = rows // blocks
    head_width = lanes // 2
    half_cols = pairs * lanes
    subs = 2 * pairs
    tok, mdl = lax.axis_index("tok"), lax.axis_index("mdl")
    chip, core = tok // 2, tok % 2
    other = 1 - core
    x_chip, y_chip, far_chip = chip + 1 - 2 * (chip % 2), (chip + 2) % 4, 3 - chip
    sibling = {"tok": chip * 2 + other, "mdl": mdl}
    x_dev = {"tok": x_chip * 2 + core, "mdl": mdl}
    y_dev = {"tok": y_chip * 2 + core, "mdl": mdl}
    remote = pltpu.make_async_remote_copy

    barrier = pltpu.get_barrier_semaphore()
    for device in (sibling, x_dev, y_dev):
        pl.semaphore_signal(barrier, inc=1, device_id=device)
    for side in (1, n_mdl - 1):
        pl.semaphore_signal(barrier, inc=1, device_id={"tok": tok, "mdl": (mdl + side) % n_mdl})

    own_hidden = pltpu.make_async_copy(hidden, hid.at[mdl], load_sem.at[0])
    own_hidden.start()
    own_out = pltpu.make_async_copy(out_w, wout.at[chip, core], load_sem.at[1])

    def columns(side, p):
        return pl.ds(pl.multiple_of(side * half_cols + p * lanes, lanes), lanes)

    projections = (key_w, value_w, query_w)
    own_tiles, swap_tiles = [], []
    for p in range(pairs):
        for m in range(3):
            number = 3 * p + m
            own_tiles.append(
                pltpu.make_async_copy(
                    projections[m].at[:, columns(core, p)],
                    weights.at[p, m, chip, core],
                    tile_sem.at[number],
                )
            )
            own_tiles[-1].start()
            swap_tiles.append(
                remote(
                    src_ref=projections[m].at[:, columns(other, p)],
                    dst_ref=weights.at[p, m, chip, core],
                    send_sem=ws_send.at[number], recv_sem=ws_recv.at[number], device_id=sibling,
                )
            )

    pl.semaphore_wait(barrier, 5)

    def copy(block, sends, recvs, index, device, target=None):
        return remote(
            src_ref=block, dst_ref=block if target is None else target,
            send_sem=sends.at[index], recv_sem=recvs.at[index], device_id=device,
        )

    def half_of(s):
        return (core + s) % 2

    def block_of(r):
        return pl.ds(r * block_rows, block_rows)

    def hidden_right(r, step):
        target = hid.at[mdl - step, block_of(r)]
        return copy(
            target if step else hidden.at[block_of(r)],
            hr_send, hr_recv, r * (n_mdl - 1) + step, {"tok": tok, "mdl": mdl + 1}, target,
        )

    def hidden_left(r, step):
        target = hid.at[mdl + step, block_of(r)]
        return copy(
            target if step else hidden.at[block_of(r)],
            hl_send, hl_recv, r * (n_mdl - 1) + step, {"tok": tok, "mdl": mdl - 1}, target,
        )

    def swap_normed(r):
        return copy(nrm.at[core, block_of(r)], ns_send, ns_recv, r, sibling)

    swap_turns = copy(cs.at[core], swap_send, swap_recv, 0, sibling)

    def weight_x(s):
        return copy(weights.at[s // 2, :, chip, half_of(s)], wx_send, wx_recv, s, x_dev)

    def weight_y(s):
        return copy(weights.at[s // 2, :, chip, half_of(s)], wy_send, wy_recv, s, y_dev)

    upper, lower = pl.ds(0, tile_rows // 2), pl.ds(tile_rows // 2, tile_rows // 2)

    def weight_relay_y(s):
        return copy(
            weights.at[s // 2, :, x_chip, half_of(s), upper], wr_send, wr_recv, s, y_dev
        )

    def weight_relay_x(s):
        return copy(
            weights.at[s // 2, :, y_chip, half_of(s), lower], wl_send, wl_recv, s, x_dev
        )

    near, away = pl.ds(0, rows // 2), pl.ds(rows // 2, rows // 2)

    def direct_x(s, k):
        return copy(kv.at[s, chip, half_of(k)], dx_send, dx_recv, 2 * s + k, x_dev)

    def direct_y(s, k):
        return copy(kv.at[s, chip, half_of(k)], dy_send, dy_recv, 2 * s + k, y_dev)

    def relay_y(s, k):
        return copy(kv.at[s, x_chip, half_of(k), near], rk_send, rk_recv, 2 * s + k, y_dev)

    def relay_x(s, k):
        return copy(kv.at[s, y_chip, half_of(k), away], rv_send, rv_recv, 2 * s + k, x_dev)

    def direct_start(s, k):
        direct_x(s, k).start()
        direct_y(s, k).start()

    def direct_event(s, k):
        direct_x(s, k).wait_recv()
        direct_y(s, k).wait_recv()
        relay_y(s, k).start()
        relay_x(s, k).start()

    def swap_att(s):
        return copy(att_send.at[s], as_send, as_recv, s, sibling, att_in.at[s])

    def z_index(s, step):
        return s * (n_mdl - 1) + step

    def z_right(s, step):
        return copy(
            att.at[mdl - step, s], zr_send, zr_recv, z_index(s, step), {"tok": tok, "mdl": mdl + 1}
        )

    def z_left(s, step):
        return copy(
            att.at[mdl + step, s], zl_send, zl_recv, z_index(s, step), {"tok": tok, "mdl": mdl - 1}
        )

    def last_rows(i):
        return pl.ds(i * (rows // 2), rows // 2)

    def last_right(i, step):
        return copy(
            att.at[mdl - step, subs - 1, last_rows(i)],
            zr_send, zr_recv, z_index(subs - 1 + i, step), {"tok": tok, "mdl": mdl + 1},
        )

    def last_left(i, step):
        return copy(
            att.at[mdl + step, subs - 1, last_rows(i)],
            zl_send, zl_recv, z_index(subs - 1 + i, step), {"tok": tok, "mdl": mdl - 1},
        )

    def line_start(right, left, index, step):
        @pl.when((mdl >= step) & (mdl < n_mdl - 1))
        def _():
            right(index, step).start()

        @pl.when((mdl + step < n_mdl) & (mdl > 0))
        def _():
            left(index, step).start()

    def line_arrive(right, left, index, step):
        @pl.when(mdl >= step + 1)
        def _():
            right(index, step).wait_recv()

        @pl.when(mdl + step + 1 < n_mdl)
        def _():
            left(index, step).wait_recv()

    def line_sent(right, left, index, step):
        @pl.when((mdl >= step) & (mdl < n_mdl - 1))
        def _():
            right(index, step).wait_send()

        @pl.when((mdl + step < n_mdl) & (mdl > 0))
        def _():
            left(index, step).wait_send()

    z_start = functools.partial(line_start, z_right, z_left)
    z_arrive = functools.partial(line_arrive, z_right, z_left)
    z_sent = functools.partial(line_sent, z_right, z_left)
    last_start = functools.partial(line_start, last_right, last_left)
    last_arrive = functools.partial(line_arrive, last_right, last_left)
    last_sent = functools.partial(line_sent, last_right, last_left)
    hidden_start = functools.partial(line_start, hidden_right, hidden_left)
    hidden_arrive = functools.partial(line_arrive, hidden_right, hidden_left)
    hidden_sent = functools.partial(line_sent, hidden_right, hidden_left)

    pieces = 4
    piece_rows = tile_rows // pieces

    def piece(i):
        return pl.ds(i * piece_rows, piece_rows)

    out_x = [
        copy(out_w.at[piece(i)], ox_send, ox_recv, i, x_dev, wout.at[chip, core, piece(i)])
        for i in range(pieces)
    ]
    out_y = [
        copy(out_w.at[piece(i)], oy_send, oy_recv, i, y_dev, wout.at[chip, core, piece(i)])
        for i in range(pieces)
    ]
    out_relay = [
        copy(
            wout.at[x_chip if i < pieces // 2 else y_chip, core, piece(i)],
            ou_send, ou_recv, i, y_dev if i < pieces // 2 else x_dev,
        )
        for i in range(pieces)
    ]
    out_pass = [
        copy(out_w, op_send, op_recv, 0, sibling, wout.at[chip, core]),
        copy(wout.at[x_chip, core], op_send, op_recv, 1, sibling),
        copy(wout.at[y_chip, core], op_send, op_recv, 2, sibling),
        copy(wout.at[far_chip, core], op_send, op_recv, 3, sibling),
    ]

    for r in range(2):
        hidden_start(r, 0)

    def send_weights(s):
        if s % 2 == 0:
            for one in own_tiles[3 * (s // 2) : 3 * (s // 2) + 3]:
                one.wait()
        else:
            for one in swap_tiles[3 * (s // 2) : 3 * (s // 2) + 3]:
                one.wait_recv()
        weight_x(s).start()
        weight_y(s).start()

    for one in swap_tiles[:3]:
        one.start()
    send_weights(0)
    for one in swap_tiles[3:]:
        one.start()
    own_out.start()
    send_weights(1)

    def weight_event(s):
        weight_x(s).wait_recv()
        weight_y(s).wait_recv()
        weight_relay_y(s).start()
        weight_relay_x(s).start()
        if s + 2 < subs:
            send_weights(s + 2)

    lane = lax.broadcasted_iota(jnp.int32, (1, lanes), 1)
    first = lane < head_width
    early = lane % head_width < head_width // 2
    spot = lane % head_width
    bound = TEXT + lengths[0]

    def request_terms(start, count, same, differs):
        ids = start + lax.broadcasted_iota(jnp.int32, (count, lanes), 0)
        later = ids >= bound
        zero_side = jnp.where(later, differs, same)
        one_side = jnp.where(later, same, differs)
        return jnp.where(spot == 0, zero_side, jnp.where(spot == 1, one_side, 0.0))

    def bias_step(index, carry):
        kbias[index] = request_terms(index * rows, rows, 0.0, -16384.0).astype(jnp.bfloat16)
        return carry

    lax.fori_loop(0, total_rows // rows, bias_step, 0)

    def clear(s, carry):
        acc[s] = jnp.zeros(acc.shape[1:], jnp.float32)
        return carry

    lax.fori_loop(0, subs, clear, 0)

    def wide_gain(gain):
        return jnp.concatenate([gain[...], gain[...]], axis=1)

    same_head = (
        lax.broadcasted_iota(jnp.int32, average.shape, 0) // head_width
        == lax.broadcasted_iota(jnp.int32, average.shape, 1) // head_width
    )
    average[...] = jnp.where(same_head, 1.0 / head_width, 0.0).astype(jnp.bfloat16)

    def head_mean(terms):
        high = terms.astype(jnp.bfloat16)
        low = (terms - high.astype(jnp.float32)).astype(jnp.bfloat16)
        return jnp.dot(high, average[...], preferred_element_type=jnp.float32) + jnp.dot(
            low, average[...], preferred_element_type=jnp.float32
        )

    def turned(normal, turns):
        partner = jnp.where(
            early,
            pltpu.roll(normal, lanes - head_width // 2, axis=1),
            pltpu.roll(normal, head_width // 2, axis=1),
        )
        return normal * turns[0] + partner * turns[1]

    quarter = head_width // 2
    pair = lane % quarter
    one_count = quarter // 4
    two_count = (quarter - one_count) // 2
    three_count = quarter - one_count - two_count
    is_one, is_two = pair < one_count, pair < one_count + two_count
    local = pair - jnp.where(is_one, 0, jnp.where(is_two, one_count, one_count + two_count))
    count = jnp.where(is_one, one_count, jnp.where(is_two, two_count, three_count))
    power = local.astype(jnp.float32) / count.astype(jnp.float32)
    rates = jnp.exp(power * -9.210340371976184)
    places = jnp.transpose(
        jnp.concatenate(
            [positions[...].astype(jnp.float32), jnp.zeros((5, rows), jnp.float32)], axis=0
        )
    )
    angles = rates * jnp.where(
        is_one, places[:, 0:1], jnp.where(is_two, places[:, 1:2], places[:, 2:3])
    )

    def textual(start, count):
        ids = tok * rows + start + lax.broadcasted_iota(jnp.int32, (count, 1), 0)
        place = jnp.where(ids >= bound, ids - bound, ids)
        return place < TEXT

    is_text = textual(0, rows)
    cs[core, 0] = jnp.where(is_text, 1.0, jnp.cos(angles))
    sine = jnp.sin(angles)
    cs[core, 1] = jnp.where(is_text, 0.0, jnp.where(early, -sine, sine))
    swap_turns.start()

    def normalize(r):
        wide = jnp.concatenate([hid[z, block_of(r), :] for z in range(n_mdl)], axis=1)
        values_in = wide.astype(jnp.float32)
        center = values_in - jnp.mean(values_in, axis=1, keepdims=True)
        spread = jnp.mean(center * center, axis=1, keepdims=True)
        normal = center * lax.rsqrt(spread + 1e-05)
        text_rows = textual(r * block_rows, block_rows)
        shift = jnp.where(text_rows, modulation[3:4, :], modulation[0:1, :])
        scale = jnp.where(text_rows, modulation[4:5, :], modulation[1:2, :])
        nrm[core, block_of(r), :] = (normal * (1.0 + scale) + shift).astype(jnp.bfloat16)
        swap_normed(r).start()

    def hidden_hop(r, step):
        hidden_arrive(r, step - 1)
        if step < n_mdl - 1:
            hidden_start(r, step)
            if step == 1 and r + 2 < blocks:
                hidden_start(r + 2, 0)
        else:
            if r == 0:
                own_hidden.wait()
            normalize(r)

    def weight_arrive(s):
        weight_relay_y(s).wait_recv()
        weight_relay_x(s).wait_recv()

    def project(p, half, start, size):
        where = pl.ds(start, size)
        here = pl.ds(pl.multiple_of(half * rows + start, block_rows), size)
        tall = [weights[p, m].reshape(depth, lanes) for m in range(3)]
        summed = jnp.dot(
            nrm[half, where, :], jnp.concatenate(tall, axis=1), preferred_element_type=jnp.float32
        )
        turns = cs[half, 0, where, :], cs[half, 1, where, :]
        both = jnp.concatenate([summed[:, :lanes], summed[:, 2 * lanes :]], axis=1)
        center = both - head_mean(both)
        scaled = wide_gain(query_gain) * (head_width ** (-0.5) * 1.4426950408889634)
        gain = jnp.concatenate([wide_gain(key_gain), scaled], axis=1)
        normal = center * lax.rsqrt(head_mean(center * center) + 1e-06) * gain
        keys = turned(normal[:, :lanes], turns)
        values = pltpu.roll(summed[:, lanes : 2 * lanes], head_width, axis=1)
        kv[2 * p, chip, half, where, :] = jnp.where(first, keys, values).astype(jnp.bfloat16)
        kv[2 * p + 1, chip, half, where, :] = jnp.where(first, values, keys).astype(jnp.bfloat16)
        query = turned(normal[:, lanes:], turns)
        terms = request_terms((chip * 2 + half) * rows + start, size, 0.0, 1.0)
        terms = jnp.where(spot < 2, 1.0 - terms, 0.0)
        qx[2 * p, here, :] = jnp.where(first, query, terms).astype(jnp.bfloat16)
        qx[2 * p + 1, here, :] = jnp.where(first, terms, query).astype(jnp.bfloat16)

    def project_own(p, r, count):
        project(p, core, r * block_rows, count * block_rows)

    def project_other(p, r, count):
        project(p, other, r * block_rows, count * block_rows)

    hidden_hop(0, 1)
    weight_event(0)
    hidden_hop(1, 1)
    weight_event(1)
    hidden_hop(0, 2)
    hidden_hop(2, 1)
    hidden_hop(1, 2)
    weight_event(2)
    hidden_hop(3, 1)
    weight_arrive(0)
    weight_arrive(1)
    swap_turns.wait_recv()
    hidden_hop(0, 3)
    weight_event(3)
    project_own(0, 0, 1)
    swap_normed(0).wait_recv()
    project_other(0, 0, 1)
    hidden_hop(2, 2)
    hidden_hop(1, 3)
    project_own(0, 1, 1)
    weight_event(4)
    swap_normed(1).wait_recv()
    project_other(0, 1, 1)
    hidden_hop(3, 2)
    weight_arrive(2)
    weight_arrive(3)
    project_own(1, 0, 2)
    project_other(1, 0, 2)
    hidden_hop(2, 3)
    project_own(0, 2, 1)
    swap_normed(2).wait_recv()
    project_other(0, 2, 1)
    weight_event(5)
    hidden_hop(3, 3)
    project_own(0, 3, 1)
    direct_start(0, 0)
    swap_normed(3).wait_recv()
    project_other(0, 3, 1)
    direct_start(0, 1)
    project_own(1, 2, 2)
    project_other(1, 2, 2)
    weight_arrive(4)
    weight_arrive(5)
    project_own(2, 0, 4)

    most = TEXT + (total_rows - 2 * TEXT) * 5 // 8
    last_first = -(-most // rows)
    first_last = (total_rows - most) // rows

    def needed(row_block, key_block):
        return (
            ((row_block < first_last) & (key_block < last_first))
            | ((row_block >= last_first) & (key_block >= first_last))
            | ((row_block >= first_last) & (row_block < last_first))
        )

    def attend_rows(where, s, source, halves):
        mine = (lane + (s % 2) * head_width) % lanes < head_width
        added = None
        for half in halves:
            block = kv[s, source, half]
            score = lax.dot_general(
                qx[s, where, :],
                jnp.where(mine, block, kbias[source * 2 + half]),
                (((1,), (1,)), ((), ())),
                preferred_element_type=jnp.float32,
            )
            part = jnp.dot(
                jnp.exp2(score).astype(jnp.bfloat16),
                jnp.where(mine, jnp.ones_like(block), block),
                preferred_element_type=jnp.float32,
            )
            added = part if added is None else added + part
        acc[s, where, :] += added

    def attend_block(s, source, r):
        where = pl.ds(pl.multiple_of(r * rows, rows), rows)
        low = needed(chip * 2 + r, source * 2)
        high = needed(chip * 2 + r, source * 2 + 1)

        @pl.when(low & high)
        def _():
            attend_rows(where, s, source, (0, 1))

        @pl.when(low != high)
        def _():
            attend_rows(where, s, source, (jnp.where(low, 0, 1),))

    def attend_unit(s, source):
        row_block, key_block = chip * 2, source * 2
        whole = (
            needed(row_block, key_block)
            & needed(row_block, key_block + 1)
            & needed(row_block + 1, key_block)
            & needed(row_block + 1, key_block + 1)
        )

        @pl.when(whole)
        def _():
            attend_rows(pl.ds(0, 2 * rows), s, source, (0, 1))

        @pl.when(jnp.logical_not(whole))
        def _():
            def one_block(r, inner):
                attend_block(s, source, r)
                return inner

            lax.fori_loop(0, 2, one_block, 0)

    def finish_head(s):
        moved = (s + 1) % 2 != core

        def one_side(turn, inner):
            r = jnp.where(turn == 0, other, core)
            attend_block(s, far_chip, r)
            both = acc[s, pl.ds(pl.multiple_of(r * rows, rows), rows), :]
            ratio = both / pltpu.roll(both, head_width, axis=1)
            ratio = jnp.where(moved, pltpu.roll(ratio, head_width, axis=1), ratio)
            ratio = ratio.astype(jnp.bfloat16)

            @pl.when(turn == 0)
            def _():
                att_send[s] = ratio
                swap_att(s).start()

            @pl.when(turn == 1)
            def _():
                swap_att(s).wait_recv()
                att[mdl, s] = jnp.where(lane // head_width == core, ratio, att_in[s])

            return inner

        lax.fori_loop(0, 2, one_side, 0)

    def pass_on(s, step):
        z_arrive(s, step - 1)
        z_start(s, step)

    final = subs - 1

    def turn(s, carry):
        direct_event(s, 0)

        def visit(j, inner):
            source = jnp.where(j == 0, chip, jnp.where(j == 1, x_chip, y_chip))

            @pl.when(j == 1)
            def _():
                direct_event(s, 1)

                @pl.when(s < final)
                def _():
                    direct_start(s + 1, 0)
                    direct_start(s + 1, 1)

                @pl.when(s == final)
                def _():
                    for i in range(pieces):
                        out_x[i].start()
                        out_y[i].start()
                    out_pass[0].start()

            @pl.when((j == 2) & (s >= 1))
            def _():
                pass_on(s - 1, 1)

            attend_unit(s, source)
            return inner

        lax.fori_loop(0, 3, visit, 0)
        for k in range(2):
            relay_y(s, k).wait_recv()
            relay_x(s, k).wait_recv()
        finish_head(s)

        @pl.when(s < final)
        def _():
            z_start(s, 0)

        @pl.when(s == final)
        def _():
            last_start(0, 0)
            last_start(1, 0)

        @pl.when(s >= 1)
        def _():
            pass_on(s - 1, 2)

        @pl.when(s == 0)
        def _():
            project_other(2, 0, 2)

        @pl.when(s == 1)
        def _():
            project_other(2, 2, 2)

        return carry

    lax.fori_loop(0, subs, turn, 0)

    def out_event(i):
        out_x[i].wait_recv()
        out_y[i].wait_recv()
        out_relay[i].start()

    def last_on(i, step):
        last_arrive(i, step - 1)
        last_start(i, step)

    out_event(0)
    out_event(1)
    last_on(0, 1)
    last_on(1, 1)
    out_event(2)
    last_on(0, 2)
    out_event(3)
    last_on(1, 2)
    out_pass[1].start()
    out_pass[2].start()
    own_out.wait()

    def combine(block):
        tall = [
            wout[block, side, s * head_width : (s + 1) * head_width, :]
            for s in range(subs)
            for side in range(2)
        ]
        return jnp.dot(
            jnp.concatenate([att[block, s] for s in range(subs)], axis=1),
            jnp.concatenate(tall, axis=0),
            preferred_element_type=jnp.float32,
        )

    for s in range(final):
        z_arrive(s, n_mdl - 2)
    for i in range(2):
        last_arrive(i, n_mdl - 2)
    out_pass[0].wait_recv()
    out_acc[...] = combine(chip)
    out_pass[1].wait_recv()
    out_acc[...] += combine(x_chip)
    out_pass[2].wait_recv()
    out_acc[...] += combine(y_chip)
    for one in out_relay:
        one.wait_recv()
    out_pass[3].start()
    out_pass[3].wait_recv()
    projected = out_acc[...] + combine(far_chip)
    own_columns = pl.ds(pl.multiple_of(mdl * width, lanes), width)
    gate = jnp.where(is_text, modulation[5:6, own_columns], modulation[2:3, own_columns])
    result[...] = (hid[mdl].astype(jnp.float32) + gate * projected).astype(jnp.bfloat16)

    swap_turns.wait_send()
    for r in range(blocks):
        swap_normed(r).wait_send()
        for step in range(n_mdl - 1):
            hidden_sent(r, step)
    for one in swap_tiles:
        one.wait_send()
    for s in range(subs):
        weight_x(s).wait_send()
        weight_y(s).wait_send()
        weight_relay_y(s).wait_send()
        weight_relay_x(s).wait_send()
        for k in range(2):
            direct_x(s, k).wait_send()
            direct_y(s, k).wait_send()
            relay_y(s, k).wait_send()
            relay_x(s, k).wait_send()
        swap_att(s).wait_send()
    for step in range(n_mdl - 1):
        for s in range(final):
            z_sent(s, step)
        for i in range(2):
            last_sent(i, step)
    for one in out_x + out_y + out_relay + out_pass:
        one.wait_send()


def fused(
    mesh, lengths, hidden, positions, modulation, weights, out_weight, gains, collective_id
):
    n_tok, n_mdl = mesh.shape["tok"], mesh.shape["mdl"]
    rows, width = hidden.shape
    depth = width * n_mdl
    lanes = 2 * gains[0].shape[1]
    pairs = width // (2 * lanes)
    total_rows = rows * n_tok
    chips = n_tok // 2
    subs = 2 * pairs
    blocks = 4
    bf, f32 = jnp.bfloat16, jnp.float32
    anywhere = pl.BlockSpec(memory_space=pl.ANY)
    inside = pl.BlockSpec(memory_space=pltpu.VMEM)

    def sems(count):
        return [pltpu.SemaphoreType.DMA((count,))]

    return pl.pallas_call(
        functools.partial(fused_kernel, n_mdl, total_rows),
        out_shape=jax.ShapeDtypeStruct((rows, width), bf),
        in_specs=[pl.BlockSpec(memory_space=pltpu.SMEM), anywhere]
        + [inside] * 2
        + [anywhere] * 4
        + [inside] * 2,
        out_specs=inside,
        scratch_shapes=[
            pltpu.VMEM((n_mdl, rows, width), bf),
            pltpu.VMEM((2, rows, depth), bf),
            pltpu.VMEM((2, 2, rows, lanes), f32),
            pltpu.VMEM((pairs, 3, chips, 2, out_weight.shape[0], lanes), bf),
            pltpu.VMEM((2 * pairs, 2 * rows, lanes), bf),
            pltpu.VMEM((subs, chips, 2, rows, lanes), bf),
            pltpu.VMEM((n_tok, rows, lanes), bf),
            pltpu.VMEM((subs, 2 * rows, lanes), f32),
            pltpu.VMEM((n_mdl, subs, rows, lanes), bf),
            pltpu.VMEM((subs, rows, lanes), bf),
            pltpu.VMEM((subs, rows, lanes), bf),
            pltpu.VMEM((chips, 2) + out_weight.shape, bf),
            pltpu.VMEM((rows, width), f32),
            pltpu.VMEM((2 * lanes, 2 * lanes), bf),
        ]
        + sems(2)
        + sems(3 * pairs)
        + sems(1) * 2
        + sems(blocks * (n_mdl - 1)) * 4
        + sems(blocks) * 2
        + sems(3 * pairs) * 2
        + sems(subs) * 8
        + sems(2 * subs) * 8
        + sems(subs) * 2
        + sems((subs + 1) * (n_mdl - 1)) * 4
        + sems(4) * 8,
        compiler_params=pltpu.CompilerParams(
            collective_id=collective_id, has_side_effects=True, vmem_limit_bytes=60 * 2**20
        ),
        name="fused",
    )(lengths, hidden, positions, modulation, *weights, out_weight, *gains)


def shards(
    mesh,
    hidden_states,
    lengths,
    positions,
    modulation,
    query_weight,
    key_weight,
    value_weight,
    out_weight,
    query_gain,
    key_gain,
):
    own_rows = hidden_states.shape[0]
    head_width = query_gain.shape[0]
    if mesh.shape["tok"] == 8 and mesh.shape["mdl"] == 4:
        return fused(
            mesh,
            lengths,
            hidden_states,
            positions,
            modulation,
            (key_weight, value_weight, query_weight),
            out_weight,
            [gain[None, :] for gain in (key_gain, query_gain)],
            0,
        )
    full_rows = lax.all_gather(hidden_states, "mdl", axis=1, tiled=True)
    key_full, value_full, query_full = gather_all(
        mesh, [key_weight, value_weight, query_weight], [], 0
    )
    row_index = lax.axis_index("tok") * own_rows + jnp.arange(own_rows, dtype=jnp.int32)
    request, is_text, bound = token_labels(row_index, lengths)
    normed = modulate(full_rows, modulation, is_text)
    angles = pair_angles(positions, head_width // 2)
    textual = is_text[:, None]
    cosine = jnp.tile(jnp.where(textual, 1.0, jnp.cos(angles)), (1, 4))
    sine = jnp.where(textual, 0.0, jnp.sin(angles))
    sine = jnp.tile(jnp.concatenate([-sine, sine], axis=1), (1, 2))
    keys, values, query_flat = project_and_gather(
        mesh,
        normed,
        (key_full, value_full, query_full),
        [jnp.tile(gain, 2)[None, :] for gain in (key_gain, query_gain)],
        cosine,
        sine,
        head_width,
        1,
    )
    first_row = lax.axis_index("tok") * own_rows
    first, second = (
        attend(query_flat, keys, values, bound, first_row, head_width, part, 2)
        for part in range(2)
    )
    first_heads = lax.all_gather(first, "mdl", axis=1, tiled=True)
    out_full, second_heads = gather_all(mesh, [out_weight], [second], 2)
    out_width = out_weight.shape[1]
    projected = jnp.concatenate(
        [
            jnp.dot(heads, out_full, preferred_element_type=jnp.float32)
            for heads in (first_heads, second_heads)
        ],
        axis=0,
    )
    gate_rows = lax.dynamic_slice_in_dim(
        modulation, lax.axis_index("mdl") * out_width, out_width, 1
    )
    gate = jnp.where(is_text[:, None], gate_rows[5][None, :], gate_rows[2][None, :])
    return (hidden_states.astype(jnp.float32) + gate * projected).astype(jnp.bfloat16)


def solution(mesh):
    return jax.shard_map(
        functools.partial(shards, mesh),
        mesh=mesh,
        in_specs=(
            P("tok", "mdl"),
            P(),
            P(None, "tok"),
            P(),
            P("tok", "mdl"),
            P("tok", "mdl"),
            P("tok", "mdl"),
            P("tok", "mdl"),
            P(),
            P(),
        ),
        out_specs=P("tok", "mdl"),
        check_vma=False,
    )
```
